32 devices in a mesh: runs: 2 (over x), fibre: 16 (over z, y, core).
Axes of the slice: x: 2, y: 2, z: 4, core: 2. Of those that a mesh axis runs over, the one named last changes fastest.
Arguments:
- records: bfloat16 [2048, 1600], P(('runs', 'fibre')), parts along dimension 0, may hold values from -6 to 6
- filter_taps: bfloat16 [9, 63], replicated, may hold values from -0.25 to 0.25
- segment_ids: int32 [2048], P('runs'), parts along dimension 0, may hold values from 0 to 7, never falling along the last dimension, each value on 1 to 256 neighbouring positions
Outputs:
- correlations: bfloat16 [2048, 5, 2048], P(('runs', 'fibre')), parts along dimension 0
- source_gathers: bfloat16 [2048, 512], P(('runs', 'fibre')), parts along dimension 0
The draws below stay inside these ranges and needn't reach their ends.
There are 2 independent parts, one for each index of `runs`. The reference program is written for one: setup_inputs(seed, part) draws one part's arguments, and reference() takes and returns one part's arrays. A program takes and returns all parts, laid end to end along the dimension named above; an argument that names none is the same for every part. Nothing has to cross between parts.
Inputs may be any that keep to these rules, and one draw needn't show every extreme that they name: `segment_ids`: segment numbers never fall along the fibre; each segment has 1 to 256 channels and one has exactly 256.
All inputs are finite; a program needn't handle non-finite values.
Results may differ from the reference program's by a relative error of at most 0.0073.
Values may be sent and summed in bfloat16 or wider, within the bound.
No kernel may reach another device: no remote copies, remote signals or barrier semaphores. Data moves between devices by JAX's collectives and lax.ppermute only.
A program may use at most 128 MiB of HBM per device.

```python
import math
import jax
import jax.numpy as jnp
import numpy as np
from jax import lax

CB = 64
W = 4
F = 200
L = 400
TAPS = 63
SPAN = 9
LAGS = 32
BAND = 4
CHANNELS = 1024
SAMPLES = 1600
SEGCOUNT = 8
SEGMAX = 256
N_FIBRE = 16


def shard_levels(stream_key, shape, cuts, low, high):
    def one(axis_at, shards_of):
        steps = jax.random.uniform(jax.random.fold_in(jax.random.fold_in(stream_key, 6), axis_at), (shards_of,), jnp.float32, low / len(cuts), high / len(cuts))
        return jnp.repeat(jnp.exp(steps), shape[axis_at] // shards_of).reshape((-1,) + (1,) * (len(shape) - axis_at - 1))

    gain = one(*cuts[0])
    for cut in cuts[1:]:
        gain = gain * one(*cut)
    return gain


def length_profile(count, total, limit, skew):
    weights = [(1 << 20) // math.isqrt(standing ** skew) + 1 for standing in range(2, count + 1)]
    surplus, given = total - limit - (count - 1), [1] * (count - 1)
    while surplus > 0:
        free = [i for i in range(count - 1) if given[i] < limit]
        mass, remaining = sum([weights[i] for i in free]), surplus
        for i in free:
            extra = min(limit - given[i], max(1, remaining * weights[i] // mass), surplus)
            given[i] = given[i] + extra
            surplus = surplus - extra
    return np.array([limit] + given)


def uneven(stream_key, number_of, total, limit, slope):
    if number_of == 2:
        one = jax.random.randint(stream_key, (), max(1, total - limit), min(limit, total - 1) + 1)
        return jnp.stack([one, total - one])
    lengths = jnp.asarray(length_profile(number_of, total, limit, slope), jnp.int32)
    pairs = (number_of - 1) // 2
    giver, sink = lengths[1:1 + 2 * pairs:2], lengths[2:2 + 2 * pairs:2]
    room = jnp.minimum(giver - 1, limit - sink)
    shifted = jax.random.randint(jax.random.fold_in(stream_key, 1), (pairs,), 0, 1 << 20) % (room + 1)
    lengths = lengths.at[1:1 + 2 * pairs:2].set(giver - shifted).at[2:2 + 2 * pairs:2].set(sink + shifted)
    return lengths[jax.random.permutation(jax.random.fold_in(stream_key, 2), number_of)]


def noise(own_key, dims, width, most, split=(), held_as=jnp.bfloat16):
    drawn = jax.random.normal(own_key, dims, jnp.float32) * width
    if len(split) > 0:
        drawn = shard_levels(own_key, dims, split, -0.22, 0.18) * drawn
    return jnp.clip(drawn, min=-most, max=most).astype(held_as)


def setup_inputs(seed: int = 0, part: int = 0) -> dict:
    seeds = jax.random.split(jax.random.key(seed), 4)
    part_splits = jax.random.split(jax.random.fold_in(seeds[3], part), 4)
    records = noise(part_splits[0], (CHANNELS, SAMPLES), 1.0, 6.0, ((0, 16),))
    filter_taps = noise(seeds[1], (SPAN, TAPS), (SPAN * TAPS) ** -0.5, 0.25)
    segment_ids = jnp.searchsorted(jnp.cumsum(uneven(part_splits[2], SEGCOUNT, CHANNELS, SEGMAX, 2)), jnp.arange(CHANNELS), side="right").astype(jnp.int32)
    return dict(records=records, filter_taps=filter_taps, segment_ids=segment_ids)


def make_tables(filter_taps):
    extent = L + TAPS - 1
    out_time = jnp.arange(L).astype(jnp.int32)
    in_time = jnp.arange(extent).astype(jnp.int32)
    tap_index = out_time[None, :] - in_time[:, None] + (TAPS - 1)
    inside = (tap_index >= 0) & (tap_index < TAPS)
    safe_index = jnp.clip(tap_index, 0, TAPS - 1)
    toeplitz = jnp.where(inside[None], filter_taps[:, safe_index], jnp.zeros((), filter_taps.dtype))
    bin_index = jnp.arange(F).astype(jnp.int32)
    phase = (out_time[:, None] * bin_index[None, :] % L).astype(jnp.float32) * (2.0 * jnp.pi / L)
    window_taper = 0.5 - 0.5 * jnp.cos((out_time.astype(jnp.float32) + 0.5) * (2.0 * jnp.pi / L))
    dft_table = jnp.concatenate([window_taper[:, None] * jnp.cos(phase), -window_taper[:, None] * jnp.sin(phase)], axis=1).astype(jnp.bfloat16)
    lag_index = jnp.arange(LAGS).astype(jnp.int32) - LAGS // 2
    lag_phase = (bin_index[:, None] * lag_index[None, :] % L).astype(jnp.float32) * (2.0 * jnp.pi / L)
    scale = 1.0 / jnp.sqrt(jnp.float32(W * F))
    lag_table = (jnp.concatenate([jnp.cos(lag_phase), -jnp.sin(lag_phase)], axis=0) * scale).astype(jnp.bfloat16)
    return (toeplitz, dft_table, lag_table)

def spectra_of(padded, seg_local, toeplitz, dft_table):
    half_span = (SPAN - 1) // 2
    total = padded.shape[0]
    windows = padded.reshape(total, W, L)
    history = jnp.concatenate([jnp.zeros((total, 1, TAPS - 1), padded.dtype), windows[:, :-1, L - (TAPS - 1):]], axis=1)
    extended = jnp.concatenate([history, windows], axis=2)
    extent = L + TAPS - 1
    accum = jnp.zeros((CB * W, L), jnp.float32)
    for offset in range(SPAN):
        rows_in = extended[offset:offset + CB].reshape(CB * W, extent)
        product = jnp.dot(rows_in, toeplitz[offset], preferred_element_type=jnp.float32)
        keeping = (seg_local[offset:offset + CB] == seg_local[half_span:half_span + CB]).astype(jnp.float32)
        accum = accum + product * jnp.repeat(keeping, W)[:, None]
    filtered = accum.astype(jnp.bfloat16)
    spectrum = jnp.dot(filtered, dft_table, preferred_element_type=jnp.float32)
    power = lax.optimization_barrier(jnp.mean(spectrum * spectrum, axis=-1, keepdims=True))
    return (spectrum * lax.rsqrt(power + 1e-06)).astype(jnp.bfloat16).reshape(CB, W, 2 * F)

def correlate(own, partner, lag_table):
    count = partner.shape[0]
    own_four = own.reshape(CB, W, 2, F).astype(jnp.float32)
    other_four = partner.reshape(count, W, 2, F)
    rotated = jnp.stack([-other_four[:, :, 1], other_four[:, :, 0]], axis=2)
    stacked = jnp.concatenate([other_four, rotated], axis=0).astype(jnp.float32)
    cross = jnp.einsum('cwrf,dwrf->fcd', own_four, stacked).astype(jnp.bfloat16)
    parts = jnp.concatenate([cross[:, :, :count], cross[:, :, count:]], axis=0).astype(jnp.float32)
    return jnp.einsum('gcd,gl->cld', parts, lag_table.astype(jnp.float32))

def pair_block(own, partner, lag_table, keeping):
    total = correlate(own, partner, lag_table)
    return (total * keeping[:, None, :]).astype(jnp.bfloat16)

def reference(records, filter_taps, segment_ids):
    toeplitz, dft_table, lag_table = make_tables(filter_taps)
    half_span = (SPAN - 1) // 2
    padded_all = jnp.pad(records, ((half_span, half_span), (0, 0)))
    seg_padded = jnp.concatenate([jnp.full((half_span,), -1, jnp.int32), segment_ids.astype(jnp.int32), jnp.full((half_span + BAND * CB,), -1, jnp.int32)])

    def one_block(block):
        start = (block * CB).astype(jnp.int32)
        padded = lax.dynamic_slice_in_dim(padded_all, start, CB + 2 * half_span, 0)
        seg_local = lax.dynamic_slice_in_dim(seg_padded, start, CB + 2 * half_span, 0)
        return spectra_of(padded, seg_local, toeplitz, dft_table)
    blocks = jnp.arange(N_FIBRE).astype(jnp.int32)
    all_spectra = lax.map(one_block, blocks)
    sources = all_spectra[:, 0]
    extended = jnp.concatenate([all_spectra, jnp.zeros((BAND,) + all_spectra.shape[1:], all_spectra.dtype)], axis=0)

    def pairs(block):
        start = (block * CB).astype(jnp.int32)
        own_seg = lax.dynamic_slice_in_dim(seg_padded, start + half_span, CB, 0)
        own = lax.dynamic_index_in_dim(extended, block, 0, keepdims=False)
        results = []
        for offset in range(BAND + 1):
            partner = lax.dynamic_index_in_dim(extended, block + offset, 0, keepdims=False)
            partner_seg = lax.dynamic_slice_in_dim(seg_padded, start + offset * CB + half_span, CB, 0)
            keeping = (own_seg[:, None] == partner_seg[None, :]).astype(jnp.float32)
            results.append(pair_block(own, partner, lag_table, keeping))
        return jnp.stack(results, axis=1)

    def gathers(block):
        own = lax.dynamic_index_in_dim(extended, block, 0, keepdims=False)
        return correlate(own, sources, lag_table).astype(jnp.bfloat16)
    outcome = lax.map(pairs, blocks)
    source_out = lax.map(gathers, blocks)
    return (outcome.reshape(CHANNELS, BAND + 1, LAGS * CB), source_out.reshape(CHANNELS, LAGS * N_FIBRE))
```

```python
import functools

import jax
import jax.numpy as jnp
import numpy as np
from jax import lax
from jax.experimental import pallas as pl
from jax.experimental.pallas import tpu as pltpu
from jax.sharding import PartitionSpec as P

CB = 64
W = 4
F = 200
L = 400
TAPS = 63
SPAN = 9
LAGS = 32
BAND = 4
HALF = (SPAN - 1) // 2
HALO = 8
CHUNK = 128
NCHUNK = -(-W * L // CHUNK)
FP = 256
KP = W * 2 * FP
ROWS = (BAND + 1) * CB
SHIFT = L % CHUNK
COVER = 4 * CHUNK

f32 = jnp.float32
bf16 = jnp.bfloat16


def dft_table():
    t = np.arange(L)
    taper = 0.5 - 0.5 * np.cos((t + 0.5) * (2.0 * np.pi / L))
    phase = (t[:, None] * np.arange(F)[None, :] % L) * (2.0 * np.pi / L)
    lead = (W - 1) * SHIFT
    table = np.zeros((lead + COVER, 2 * FP))
    table[lead : lead + L, :F] = taper[:, None] * np.cos(phase)
    table[lead : lead + L, FP : FP + F] = -taper[:, None] * np.sin(phase)
    return jnp.asarray(table.astype(np.float32), bf16)


def lag_tables():
    m = np.arange(LAGS) - LAGS // 2
    phase = (m[:, None] * np.arange(F)[None, :] % L) * (2.0 * np.pi / L)
    scale = 1.0 / np.sqrt(2.0 * L)
    tables = np.zeros((2, LAGS, FP))
    tables[0, :, :F] = np.cos(phase) * scale
    tables[1, :, :F] = -np.sin(phase) * scale
    return jnp.asarray(tables.astype(np.float32), bf16).astype(f32)


def band_kernel(taps_ref, band_ref):
    for e in range(SPAN):
        row = jnp.broadcast_to(taps_ref[e : e + 1, :], (2 * CHUNK, 2 * CHUNK))
        rolled = pltpu.roll(row, CHUNK, 1, stride=1, stride_axis=0)
        band_ref[e * 2 * CHUNK : (e + 1) * 2 * CHUNK, :] = rolled[:, :CHUNK].astype(bf16)


def spectra_kernel(parity_ref, own_ref, two_ref, four_ref, swap_ref, halo_ref, seg_ref, band_ref, dft_ref,
                   spec_ref, rec, masked, filt):
    even = parity_ref[0] == 0

    def put(start, rows):
        count = rows.shape[0]
        rows = jnp.concatenate(
            [rows.astype(f32), jnp.zeros((count, NCHUNK * CHUNK - W * L), f32)], axis=1
        )
        for j in range(NCHUNK):
            rec[j, start : start + count, :] = rows[:, j * CHUNK : (j + 1) * CHUNK]

    put(HALO, own_ref[...])
    put(HALO + CB, swap_ref[:CB])
    put(HALO + 2 * CB, two_ref[...])
    put(HALO + 3 * CB, swap_ref[CB : 2 * CB])
    put(HALO + 4 * CB, four_ref[...])
    halo, other = halo_ref[...].astype(f32), swap_ref[2 * CB :].astype(f32)
    put(0, jnp.where(even, halo, other))
    put(HALO + 5 * CB, jnp.where(even, other, halo))
    masked[:, :CB, :] = jnp.zeros((SPAN, CB, CHUNK), bf16)

    @pl.loop(0, BAND + 1)
    def _(k):
        base = pl.multiple_of(k * CB, CB)
        centre = seg_ref[pl.ds(base + HALO, CB), :]
        for e in range(SPAN):
            first = base + (HALO - HALF + e)
            keep = seg_ref[pl.ds(first, CB), :] == centre
            for j in range(NCHUNK):
                rows = rec[j, pl.ds(first, CB), :]
                masked[e, (j + 1) * CB : (j + 2) * CB, :] = jnp.where(keep, rows, 0.0).astype(bf16)
        pieces = []
        for e in range(SPAN):
            pieces.append(masked[e, : NCHUNK * CB, :])
            pieces.append(masked[e, CB : (NCHUNK + 1) * CB, :])
        lhs = jnp.concatenate(pieces, axis=1)
        filt[...] = jnp.dot(lhs, band_ref[...], preferred_element_type=f32).astype(bf16)
        for w in range(W):
            first = w * (L // CHUNK)
            lhs = jnp.concatenate(
                [filt[(first + q) * CB : (first + q + 1) * CB, :] for q in range(COVER // CHUNK)], axis=1
            )
            lead = (W - 1 - w) * SHIFT
            raw = jnp.dot(lhs, dft_ref[lead : lead + COVER, :], preferred_element_type=f32)
            power = jnp.sum(raw * raw, axis=-1, keepdims=True) * (1.0 / L)
            spec_ref[pl.ds(base, CB), w * 2 * FP : (w + 1) * 2 * FP] = (
                raw * lax.rsqrt(power + 1e-06)
            ).astype(bf16)


def correlate_kernel(seg_ref, pseg_ref, spec_ref, lag_ref, out_ref, turned):
    group = turned.shape[0] // CB
    own_seg = seg_ref[HALO : HALO + CB, :]
    keeps = [own_seg == pseg_ref[k : k + 1, :] for k in range(BAND + 1)]

    @pl.loop(0, LAGS // group)
    def _(step):
        start = pl.multiple_of(step * group, group)
        cosines = lag_ref[0, pl.ds(start, group), :]
        sines = lag_ref[1, pl.ds(start, group), :]
        for w in range(W):
            re_at, im_at = w * 2 * FP, w * 2 * FP + FP
            re = spec_ref[:CB, re_at : re_at + FP].astype(f32)
            im = spec_ref[:CB, im_at : im_at + FP].astype(f32)
            for g in range(group):
                c, s = cosines[g : g + 1, :], sines[g : g + 1, :]
                turned[g * CB : (g + 1) * CB, re_at : re_at + FP] = (re * c + im * s).astype(bf16)
                turned[g * CB : (g + 1) * CB, im_at : im_at + FP] = (im * c - re * s).astype(bf16)
        total = lax.dot_general(
            turned[...], spec_ref[...], (((1,), (1,)), ((), ())), preferred_element_type=f32
        )
        for pair in range(group // 2):
            low = total[2 * pair * CB : (2 * pair + 1) * CB]
            high = total[(2 * pair + 1) * CB : (2 * pair + 2) * CB]
            lanes = pl.ds(pl.multiple_of(start * CB + pair * 2 * CB, 2 * CB), 2 * CB)
            for k in range(BAND + 1):
                both = jnp.concatenate(
                    [low[:, k * CB : (k + 1) * CB], high[:, k * CB : (k + 1) * CB]], axis=1
                )
                out_ref[k, :, lanes] = jnp.where(keeps[k], both, 0.0).astype(bf16)


def source_kernel(index_ref, spec_ref, src_ref, lag_ref, out_ref, turned):
    count = src_ref.shape[0]
    row = lax.broadcasted_iota(jnp.int32, (count, count), 0)
    column = lax.broadcasted_iota(jnp.int32, (count, count), 1)
    ahead = row - index_ref[0]
    ahead = jnp.where(ahead < 0, ahead + count, ahead)
    order = jnp.where(ahead == column, 1.0, 0.0).astype(bf16)
    sources = jnp.dot(order, src_ref[...], preferred_element_type=f32)
    for w in range(W):
        re_at, im_at = w * 2 * FP, w * 2 * FP + FP
        re = sources[:, re_at : re_at + FP]
        im = sources[:, im_at : im_at + FP]
        for l in range(LAGS):
            c, s = lag_ref[0, l : l + 1, :], lag_ref[1, l : l + 1, :]
            turned[l * count : (l + 1) * count, re_at : re_at + FP] = (re * c - im * s).astype(bf16)
            turned[l * count : (l + 1) * count, im_at : im_at + FP] = (im * c + re * s).astype(bf16)
    out_ref[...] = lax.dot_general(
        spec_ref[:CB, :], turned[...], (((1,), (1,)), ((), ())), preferred_element_type=f32
    ).astype(bf16)


VMEM = pl.BlockSpec(memory_space=pltpu.VMEM)
SMEM = pl.BlockSpec(memory_space=pltpu.SMEM)


def call(kernel, shapes, scratch, specs, **kwargs):
    return pl.pallas_call(
        kernel, out_shape=shapes, in_specs=specs, out_specs=VMEM, scratch_shapes=scratch, **kwargs
    )


def per_device(records, filter_taps, segment_ids):
    count = lax.axis_size("fibre")
    device = lax.axis_index("fibre")
    parity = device % 2

    def ahead(value, distance):
        return lax.ppermute(value, "fibre", [(i, (i - distance) % count) for i in range(count)])

    halo_route = [(i, (i + 1) % count if i % 2 else (i - 5) % count) for i in range(count)]
    edge = jnp.where(parity == 1, records[CB - HALO :], records[:HALO])
    halo = lax.ppermute(edge, "fibre", halo_route)
    two = ahead(records, 2)
    four = ahead(records, 4)
    give = jnp.where(
        parity == 0,
        jnp.concatenate([two, four, records[CB - HALO :]], axis=0),
        jnp.concatenate([records, two, four[:HALO]], axis=0),
    )
    swap = lax.ppermute(give, "fibre", [(i, i ^ 1) for i in range(count)])

    taps = jnp.pad(filter_taps.astype(f32), ((0, 16 - SPAN), (0, 2 * CHUNK - TAPS)))
    band = call(band_kernel, jax.ShapeDtypeStruct((SPAN * 2 * CHUNK, CHUNK), bf16), (), [VMEM])(taps)

    seg_ring = jnp.concatenate([segment_ids[-HALO:], segment_ids, segment_ids[: ROWS - CB + HALO]])
    seg_local = lax.dynamic_slice_in_dim(seg_ring, device * CB, ROWS + 2 * HALO, 0)
    seg_rows = jnp.broadcast_to(seg_local[:, None], (ROWS + 2 * HALO, CHUNK))
    block = device + jnp.arange(BAND + 1)
    partner = jnp.where(
        block[:, None] < count, seg_local[HALO : HALO + ROWS].reshape(BAND + 1, CB), -1
    )
    partner = jnp.pad(jnp.concatenate([partner, partner], axis=1), ((0, 8 - BAND - 1), (0, 0)))

    spec = call(
        spectra_kernel,
        jax.ShapeDtypeStruct((ROWS, KP), bf16),
        [
            pltpu.VMEM((NCHUNK, ROWS + 2 * HALO, CHUNK), f32),
            pltpu.VMEM((SPAN, (NCHUNK + 1) * CB, CHUNK), bf16),
            pltpu.VMEM((NCHUNK * CB, CHUNK), bf16),
        ],
        [SMEM] + [VMEM] * 8,
    )(parity.reshape(1), records, two, four, swap, halo, seg_rows, band, dft_table())
    lags = lag_tables()

    known = spec[::CB]
    while known.shape[0] < count:
        have = known.shape[0]
        more = min(have, count - have)
        known = jnp.concatenate([known, ahead(known[:more], have)], axis=0)
    known = known[:count]

    group = 8
    stacked = call(
        correlate_kernel,
        jax.ShapeDtypeStruct((BAND + 1, CB, LAGS * CB), bf16),
        [pltpu.VMEM((group * CB, KP), bf16)],
        [VMEM] * 4,
    )(seg_rows, partner, spec, lags)
    source_out = call(
        source_kernel,
        jax.ShapeDtypeStruct((CB, LAGS * count), bf16),
        [pltpu.VMEM((LAGS * count, KP), bf16)],
        [SMEM] + [VMEM] * 3,
    )(device.reshape(1), spec, known, lags)
    return (jnp.swapaxes(stacked, 0, 1), source_out)


def solution(mesh):
    return jax.shard_map(
        per_device,
        mesh=mesh,
        in_specs=(P(("runs", "fibre"), None), P(), P("runs")),
        out_specs=(P(("runs", "fibre"), None, None), P(("runs", "fibre"), None)),
        check_vma=False,
    )
```

```python
import functools

import jax
import jax.numpy as jnp
import numpy as np
from jax import lax
from jax.experimental import pallas as pl
from jax.experimental.pallas import tpu as pltpu
from jax.sharding import PartitionSpec as P

CB = 64
W = 4
F = 200
L = 400
TAPS = 63
SPAN = 9
LAGS = 32
BAND = 4
HALF = (SPAN - 1) // 2
HALO = 8
CHUNK = 128
NCHUNK = -(-W * L // CHUNK)
FP = 256
KP = W * 2 * FP
ROWS = (BAND + 1) * CB
SHIFT = L % CHUNK
COVER = 4 * CHUNK

f32 = jnp.float32
bf16 = jnp.bfloat16


def dft_table():
    t = np.arange(L)
    taper = 0.5 - 0.5 * np.cos((t + 0.5) * (2.0 * np.pi / L))
    phase = (t[:, None] * np.arange(F)[None, :] % L) * (2.0 * np.pi / L)
    lead = (W - 1) * SHIFT
    table = np.zeros((lead + COVER, 2 * FP))
    table[lead : lead + L, :F] = taper[:, None] * np.cos(phase)
    table[lead : lead + L, FP : FP + F] = -taper[:, None] * np.sin(phase)
    return jnp.asarray(table.astype(np.float32), bf16)


def lag_tables():
    m = np.arange(LAGS) - LAGS // 2
    phase = (m[:, None] * np.arange(F)[None, :] % L) * (2.0 * np.pi / L)
    scale = 1.0 / np.sqrt(2.0 * L)
    tables = np.zeros((2, LAGS, FP))
    tables[0, :, :F] = np.cos(phase) * scale
    tables[1, :, :F] = -np.sin(phase) * scale
    return jnp.asarray(tables.astype(np.float32), bf16).astype(f32)


def band_kernel(taps_ref, band_ref):
    for e in range(SPAN):
        row = jnp.broadcast_to(taps_ref[e : e + 1, :], (2 * CHUNK, 2 * CHUNK))
        rolled = pltpu.roll(row, CHUNK, 1, stride=1, stride_axis=0)
        band_ref[e * 2 * CHUNK : (e + 1) * 2 * CHUNK, :] = rolled[:, :CHUNK].astype(bf16)


def main_kernel(index_ref, own_ref, two_ref, four_ref, sown_ref, stwo_ref, sfour_ref, edge_ref, sedge_ref, pick_ref,
                seg_ref, pseg_ref, band_ref, dft_ref, lag_ref, out_ref, src_ref, rec, masked, smasked, filt, spec,
                turned):
    even = index_ref[0] % 2 == 0
    count = smasked.shape[1] // (NCHUNK + 1)
    lanes_in = [slice(j * CHUNK, min((j + 1) * CHUNK, W * L)) for j in range(NCHUNK)]

    def chunk(rows, j):
        piece = rows[:, lanes_in[j]]
        if piece.shape[1] < CHUNK:
            piece = jnp.concatenate(
                [piece, jnp.zeros((piece.shape[0], CHUNK - piece.shape[1]), piece.dtype)], axis=1
            )
        return piece

    def put(start, rows):
        for j in range(NCHUNK):
            rec[j, start : start + rows.shape[0], :] = chunk(rows, j)

    stwo = stwo_ref[...].astype(f32)
    put(HALO, own_ref[...].astype(f32))
    put(HALO + CB, jnp.where(even, sown_ref[...].astype(f32), stwo))
    put(HALO + 2 * CB, two_ref[...].astype(f32))
    put(HALO + 3 * CB, jnp.where(even, stwo, sfour_ref[...].astype(f32)))
    put(HALO + 4 * CB, four_ref[...].astype(f32))

    edges = jnp.concatenate([edge_ref[...], sedge_ref[...]], axis=0)
    picked = jnp.dot(pick_ref[...], edges, preferred_element_type=f32)
    put(0, picked[SPAN * count : SPAN * count + HALO])
    put(HALO + ROWS, picked[SPAN * count + HALO :])
    masked[:, :CB, :] = jnp.zeros((SPAN, CB, CHUNK), bf16)
    smasked[:, :count, :] = jnp.zeros((SPAN, count, CHUNK), bf16)
    for e in range(SPAN):
        for j in range(NCHUNK):
            smasked[e, (j + 1) * count : (j + 2) * count, :] = chunk(
                picked[e * count : (e + 1) * count], j
            ).astype(bf16)

    def filtered(inputs, rows):
        pieces = []
        for e in range(SPAN):
            pieces.append(inputs[e, : NCHUNK * rows, :])
            pieces.append(inputs[e, rows : (NCHUNK + 1) * rows, :])
        return jnp.dot(
            jnp.concatenate(pieces, axis=1), band_ref[...], preferred_element_type=f32
        ).astype(bf16)

    result = filtered(smasked, count)
    for j in range(NCHUNK):
        filt[j, ROWS : ROWS + count, :] = result[j * count : (j + 1) * count]

    @pl.loop(0, BAND + 1)
    def _(k):
        base = pl.multiple_of(k * CB, CB)
        centre = seg_ref[pl.ds(base + HALO, CB), :]
        for e in range(SPAN):
            first = base + (HALO - HALF + e)
            keep = seg_ref[pl.ds(first, CB), :] == centre
            for j in range(NCHUNK):
                rows = rec[j, pl.ds(first, CB), :]
                masked[e, (j + 1) * CB : (j + 2) * CB, :] = jnp.where(keep, rows, 0.0).astype(bf16)
        result = filtered(masked, CB)
        for j in range(NCHUNK):
            filt[j, pl.ds(base, CB), :] = result[j * CB : (j + 1) * CB]

    for w in range(W):
        first = w * (L // CHUNK)
        lhs = jnp.concatenate([filt[first + q] for q in range(COVER // CHUNK)], axis=1)
        lead = (W - 1 - w) * SHIFT
        raw = jnp.dot(lhs, dft_ref[lead : lead + COVER, :], preferred_element_type=f32)
        power = jnp.sum(raw * raw, axis=-1, keepdims=True) * (1.0 / L)
        spec[:, w * 2 * FP : (w + 1) * 2 * FP] = (raw * lax.rsqrt(power + 1e-06)).astype(bf16)

    row = lax.broadcasted_iota(jnp.int32, (count, count), 0)
    column = lax.broadcasted_iota(jnp.int32, (count, count), 1)
    ahead = row - index_ref[0]
    ahead = jnp.where(ahead < 0, ahead + count, ahead)
    order = jnp.where(ahead == column, 1.0, 0.0).astype(bf16)
    spec[ROWS:, :] = jnp.dot(order, spec[ROWS:, :], preferred_element_type=f32).astype(bf16)

    group = turned.shape[0] // CB
    own_seg = seg_ref[HALO : HALO + CB, :]

    @pl.loop(0, LAGS // group)
    def _(step):
        start = pl.multiple_of(step * group, group)
        cosines = lag_ref[0, pl.ds(start, group), :]
        sines = lag_ref[1, pl.ds(start, group), :]
        for w in range(W):
            re_at, im_at = w * 2 * FP, w * 2 * FP + FP
            re = spec[:CB, re_at : re_at + FP].astype(f32)
            im = spec[:CB, im_at : im_at + FP].astype(f32)
            for g in range(group):
                c, s = cosines[g : g + 1, :], sines[g : g + 1, :]
                turned[g * CB : (g + 1) * CB, re_at : re_at + FP] = (re * c + im * s).astype(bf16)
                turned[g * CB : (g + 1) * CB, im_at : im_at + FP] = (im * c - re * s).astype(bf16)
        total = lax.dot_general(
            turned[...], spec[...], (((1,), (1,)), ((), ())), preferred_element_type=f32
        )
        for pair in range(group // 2):
            low = total[2 * pair * CB : (2 * pair + 1) * CB]
            high = total[(2 * pair + 1) * CB : (2 * pair + 2) * CB]
            lanes = pl.ds(pl.multiple_of(start * CB + pair * 2 * CB, 2 * CB), 2 * CB)
            for k in range(BAND + 1):
                both = jnp.concatenate(
                    [low[:, k * CB : (k + 1) * CB], high[:, k * CB : (k + 1) * CB]], axis=1
                )
                keep = own_seg == pseg_ref[k : k + 1, :]
                out_ref[k, :, lanes] = jnp.where(keep, both, 0.0).astype(bf16)
        sources = jnp.concatenate(
            [total[g * CB : (g + 1) * CB, ROWS : ROWS + count] for g in range(group)], axis=1
        )
        src_ref[:, pl.ds(pl.multiple_of(start * count, group * count), group * count)] = sources.astype(bf16)


VMEM = pl.BlockSpec(memory_space=pltpu.VMEM)
SMEM = pl.BlockSpec(memory_space=pltpu.SMEM)


def call(kernel, shapes, scratch, specs, **kwargs):
    return pl.pallas_call(
        kernel, out_shape=shapes, in_specs=specs, out_specs=jax.tree.map(lambda _: VMEM, shapes), scratch_shapes=scratch, **kwargs
    )


def per_device(records, filter_taps, segment_ids):
    count = lax.axis_size("fibre")
    device = lax.axis_index("fibre")

    def ahead(value, distance):
        return lax.ppermute(value, "fibre", [(i, (i - distance) % count) for i in range(count)])

    def swap(value):
        return lax.ppermute(value, "fibre", [(i, i ^ 1) for i in range(count)])

    four, two = ahead(records, 4), ahead(records, 2)

    def edges_of(rows):
        return jnp.concatenate([rows[CB - HALF :], rows[: HALF + 1]], axis=0)

    edge = edges_of(records)
    near = [edge] + [ahead(edge, 2 * s) for s in reversed(range(3, min(8, count // 2)))][::-1]
    near[1:1] = [edges_of(two), edges_of(four)]
    known = jnp.concatenate(near, axis=0)
    while known.shape[0] < SPAN * count // 2:
        have = known.shape[0] // SPAN
        parts = [known]
        for s in range(1, 8):
            left = count // 2 - s * have
            if left > 0:
                parts.append(ahead(known[: SPAN * left], 2 * s * have))
        known = jnp.concatenate(parts, axis=0)
    sown, sfour, stwo, sknown = swap(records), swap(four), swap(two), swap(known)

    taps = jnp.pad(filter_taps.astype(f32), ((0, 16 - SPAN), (0, 2 * CHUNK - TAPS)))
    band = call(band_kernel, jax.ShapeDtypeStruct((SPAN * 2 * CHUNK, CHUNK), bf16), (), [VMEM])(taps)

    ring = jnp.concatenate([segment_ids[-HALO:], segment_ids, segment_ids[: CB * (count - 1) + HALO]])
    ring = lax.dynamic_slice_in_dim(ring, device * CB, CB * count + HALO, 0)
    seg_rows = jnp.broadcast_to(ring[: ROWS + 2 * HALO, None], (ROWS + 2 * HALO, CHUNK))
    block = device + jnp.arange(BAND + 1)
    partner = jnp.where(
        block[:, None] < count, ring[HALO : HALO + ROWS].reshape(BAND + 1, CB), -1
    )
    partner = jnp.pad(jnp.concatenate([partner, partner], axis=1), ((0, 8 - BAND - 1), (0, 0)))

    near_rows = jnp.stack([ring[HALO - HALF + e :: CB][:count] for e in range(SPAN)])
    agree = (near_rows == near_rows[HALF]).reshape(-1)
    e, r = jnp.arange(SPAN)[:, None], jnp.arange(count)[None, :]
    want_block = jnp.where(e < HALF, r - 1, r).reshape(-1)
    want_row = jnp.broadcast_to(e, (SPAN, count)).reshape(-1)
    side = jnp.arange(HALO)
    want_block = jnp.concatenate([want_block, jnp.full((HALO,), -1), jnp.full((HALO,), BAND + 1)])
    want_row = jnp.concatenate([want_row, jnp.clip(side - HALF, 0), jnp.minimum(side + HALF, SPAN - 1)])
    agree = jnp.concatenate([agree, side >= HALO - HALF, side < HALF])
    want_block = want_block % count
    place = jnp.where(
        want_block % 2 == 0, want_block // 2, count // 2 + (want_block // 2 + device % 2) % (count // 2)
    )
    pick = jnp.where(
        (place * SPAN + want_row)[:, None] == jnp.arange(SPAN * count)[None, :], agree[:, None], False
    ).astype(bf16)

    group = 8
    stacked, source_out = call(
        main_kernel,
        (
            jax.ShapeDtypeStruct((BAND + 1, CB, LAGS * CB), bf16),
            jax.ShapeDtypeStruct((CB, LAGS * count), bf16),
        ),
        [
            pltpu.VMEM((NCHUNK, ROWS + 2 * HALO, CHUNK), f32),
            pltpu.VMEM((SPAN, (NCHUNK + 1) * CB, CHUNK), bf16),
            pltpu.VMEM((SPAN, (NCHUNK + 1) * count, CHUNK), bf16),
            pltpu.VMEM((NCHUNK, ROWS + count, CHUNK), bf16),
            pltpu.VMEM((ROWS + count, KP), bf16),
            pltpu.VMEM((group * CB, KP), bf16),
        ],
        [SMEM] + [VMEM] * 14,
    )(
        device.reshape(1), records, two, four, sown, stwo, sfour, known, sknown, pick, seg_rows, partner, band,
        dft_table(), lag_tables(),
    )
    return (jnp.swapaxes(stacked, 0, 1), source_out)


def solution(mesh):
    return jax.shard_map(
        per_device,
        mesh=mesh,
        in_specs=(P(("runs", "fibre"), None), P(), P("runs")),
        out_specs=(P(("runs", "fibre"), None, None), P(("runs", "fibre"), None)),
        check_vma=False,
    )
```

```python
import functools

import jax
import jax.numpy as jnp
import numpy as np
from jax import lax
from jax.experimental import pallas as pl
from jax.experimental.pallas import tpu as pltpu
from jax.sharding import PartitionSpec as P


CB = 64
W = 4
F = 200
L = 400
TAPS = 63
SPAN = 9
LAGS = 32
BAND = 4
HALF = (SPAN - 1) // 2
SLOT = 16
HALO = 8
CHUNK = 128
NCHUNK = -(-W * L // CHUNK)
FP = 256
KP = W * 2 * FP
ROWS = (BAND + 1) * CB
SHIFT = L % CHUNK
COVER = 4 * CHUNK

f32 = jnp.float32
bf16 = jnp.bfloat16


def dft_table():
    t = np.arange(L)
    taper = 0.5 - 0.5 * np.cos((t + 0.5) * (2.0 * np.pi / L))
    phase = (t[:, None] * np.arange(F)[None, :] % L) * (2.0 * np.pi / L)
    lead = (W - 1) * SHIFT
    table = np.zeros((lead + COVER, 2 * FP))
    table[lead : lead + L, :F] = taper[:, None] * np.cos(phase)
    table[lead : lead + L, FP : FP + F] = -taper[:, None] * np.sin(phase)
    return jnp.asarray(table.astype(np.float32), bf16)


def lag_tables():
    m = np.arange(LAGS) - LAGS // 2
    phase = (m[:, None] * np.arange(F)[None, :] % L) * (2.0 * np.pi / L)
    scale = 1.0 / np.sqrt(2.0 * L)
    tables = np.zeros((2, LAGS, FP))
    tables[0, :, :F] = np.cos(phase) * scale
    tables[1, :, :F] = -np.sin(phase) * scale
    return jnp.asarray(tables.astype(np.float32), bf16).astype(f32)


def prep_kernel(index_ref, taps_ref, ids_ref, band_ref, seg_ref, pseg_ref, pick_ref):
    device = index_ref[0]
    total = ids_ref.shape[1]
    count = total // CB
    wide = jnp.concatenate([taps_ref[...].astype(f32), jnp.zeros((SPAN, 2 * CHUNK - TAPS), f32)], axis=1)
    for e in range(SPAN):
        row = jnp.broadcast_to(wide[e : e + 1, :], (CHUNK, 2 * CHUNK))
        band_ref[e * CHUNK : (e + 1) * CHUNK, :] = pltpu.roll(row, 0, 1, stride=1, stride_axis=0).astype(bf16)

    ids = jnp.broadcast_to(ids_ref[...].astype(bf16), (CHUNK, total))

    def segments_at(channels):
        rows = channels.shape[0]
        channels = jnp.where(channels < 0, channels + total, channels)
        channels = jnp.where(channels >= total, channels - total, channels)
        hit = lax.broadcasted_iota(jnp.int32, (rows, total), 1) == channels
        return lax.dot_general(
            jnp.where(hit, 1.0, 0.0).astype(bf16), ids, (((1,), (1,)), ((), ())), preferred_element_type=f32
        )

    def rows_of(rows):
        return lax.broadcasted_iota(jnp.int32, (rows, 1), 0)

    start = device * CB
    near = segments_at(start - HALO + rows_of(ROWS + 2 * HALO))
    seg_ref[...] = near
    for k in range(BAND + 1):
        block = near[HALO + k * CB : HALO + (k + 1) * CB]
        turned = jnp.transpose(jnp.concatenate([block, block], axis=0))
        pseg_ref[k : k + 1, :] = jnp.where(device + k < count, turned[:1], -1.0)
    pseg_ref[BAND + 1 :, :] = jnp.full((8 - BAND - 1, CHUNK), -1.0, f32)

    row = rows_of(SPAN * count)
    e, r = row // count, row % count
    agree = segments_at(start + r * CB + e - HALF) == segments_at(start + r * CB)
    want_block = jnp.where(e < HALF, r - 1, r)
    want_block = jnp.where(want_block < 0, count - 1, want_block)
    side = rows_of(HALO)

    def column_of(block, edge_row):
        other = block // 2 + device % 2
        other = jnp.where(other >= count // 2, other - count // 2, other)
        place = jnp.where(block % 2 == 0, block // 2, count // 2 + other)
        return place * SLOT + edge_row

    columns = SLOT * count

    def one_hot(column, valid):
        hit = lax.broadcasted_iota(jnp.int32, (column.shape[0], columns), 1) == column
        return jnp.where(hit & valid, 1.0, 0.0).astype(bf16)

    agree = jnp.broadcast_to(agree[:, :1], (SPAN * count, columns))
    pick_ref[: SPAN * count, :] = one_hot(column_of(want_block, e), agree)
    low = column_of(jnp.full((HALO, 1), count - 1, jnp.int32), side - HALF)
    pick_ref[SPAN * count : SPAN * count + HALO, :] = one_hot(low, side >= HALF)
    high = column_of(jnp.full((HALO, 1), BAND + 1, jnp.int32), side + HALF)
    pick_ref[SPAN * count + HALO :, :] = one_hot(high, side < HALF)


def main_kernel(pieces, *refs):
    index_ref, own_ref, two_ref, four_ref, sown_ref, stwo_ref, sfour_ref = refs[:7]
    edge_refs, swapped_refs, refs = refs[7 : 7 + pieces], refs[7 + pieces : 7 + 2 * pieces], refs[7 + 2 * pieces :]
    pick_ref, seg_ref, pseg_ref, band_ref, dft_ref, lag_ref, out_ref, src_ref = refs[:8]
    rec, masked, smasked, edges, filt, spec, turned = refs[8:]
    even = index_ref[0] % 2 == 0
    count = edges.shape[0] // SLOT

    def chunk(rows, j):
        piece = rows[:, j * CHUNK : min((j + 1) * CHUNK, W * L)]
        if piece.shape[1] < CHUNK:
            piece = jnp.concatenate(
                [piece, jnp.zeros((piece.shape[0], CHUNK - piece.shape[1]), piece.dtype)], axis=1
            )
        return piece

    def put(start, rows):
        for j in range(NCHUNK):
            rec[j, start : start + rows.shape[0], :] = chunk(rows, j)

    stwo = stwo_ref[...].astype(f32)
    put(HALO, own_ref[...].astype(f32))
    put(HALO + CB, jnp.where(even, sown_ref[...].astype(f32), stwo))
    put(HALO + 2 * CB, two_ref[...].astype(f32))
    put(HALO + 3 * CB, jnp.where(even, stwo, sfour_ref[...].astype(f32)))
    put(HALO + 4 * CB, four_ref[...].astype(f32))

    empty = jnp.zeros((SLOT - SPAN, W * L), f32)
    for half, blocks, rest in ((0, (own_ref, two_ref, four_ref), edge_refs), (1, (sown_ref, stwo_ref, sfour_ref), swapped_refs)):
        slot = half * count // 2
        for ref in blocks:
            rows = [ref[CB - HALO :].astype(f32)[HALO - HALF :], ref[:HALO].astype(f32)[: HALF + 1]]
            edges[slot * SLOT : (slot + 1) * SLOT, :] = jnp.concatenate(rows + [empty], axis=0).astype(bf16)
            slot += 1
        for ref in rest:
            rows = ref[...].astype(f32)
            for first in range(0, rows.shape[0], SPAN):
                edges[slot * SLOT : (slot + 1) * SLOT, :] = jnp.concatenate(
                    [rows[first : first + SPAN], empty], axis=0
                ).astype(bf16)
                slot += 1
    picked = jnp.dot(pick_ref[...], edges[...], preferred_element_type=f32)
    put(0, picked[SPAN * count : SPAN * count + HALO])
    put(HALO + ROWS, picked[SPAN * count + HALO :])
    for e in range(SPAN):
        for j in range(NCHUNK):
            smasked[j * count : (j + 1) * count, e * CHUNK : (e + 1) * CHUNK] = chunk(
                picked[e * count : (e + 1) * count], j
            ).astype(bf16)

    def filtered(inputs, rows, start):
        share = jnp.dot(inputs[...], band_ref[...], preferred_element_type=f32)
        for j in range(NCHUNK):
            result = share[j * rows : (j + 1) * rows, :CHUNK]
            if j:
                result = result + share[(j - 1) * rows : j * rows, CHUNK:]
            filt[j, pl.ds(start, rows), :] = result.astype(bf16)

    filtered(smasked, count, ROWS)

    @pl.loop(0, BAND + 1)
    def _(k):
        base = pl.multiple_of(k * CB, CB)
        centre = seg_ref[pl.ds(base + HALO, CB), :]
        for e in range(SPAN):
            first = base + (HALO - HALF + e)
            keep = seg_ref[pl.ds(first, CB), :] == centre
            for j in range(NCHUNK):
                rows = rec[j, pl.ds(first, CB), :]
                masked[j * CB : (j + 1) * CB, e * CHUNK : (e + 1) * CHUNK] = jnp.where(keep, rows, 0.0).astype(bf16)
        filtered(masked, CB, base)

    for w in range(W):
        first = w * (L // CHUNK)
        lhs = jnp.concatenate([filt[first + q] for q in range(COVER // CHUNK)], axis=1)
        lead = (W - 1 - w) * SHIFT
        raw = jnp.dot(lhs, dft_ref[lead : lead + COVER, :], preferred_element_type=f32)
        power = jnp.sum(raw * raw, axis=-1, keepdims=True) * (1.0 / L)
        spec[:, w * 2 * FP : (w + 1) * 2 * FP] = (raw * lax.rsqrt(power + 1e-06)).astype(bf16)

    row = lax.broadcasted_iota(jnp.int32, (count, count), 0)
    column = lax.broadcasted_iota(jnp.int32, (count, count), 1)
    ahead = row - index_ref[0]
    ahead = jnp.where(ahead < 0, ahead + count, ahead)
    order = jnp.where(ahead == column, 1.0, 0.0).astype(bf16)
    spec[ROWS:, :] = jnp.dot(order, spec[ROWS:, :], preferred_element_type=f32).astype(bf16)

    group = turned.shape[0] // CB
    own_seg = seg_ref[HALO : HALO + CB, :]

    @pl.loop(0, LAGS // group)
    def _(step):
        start = pl.multiple_of(step * group, group)
        cosines = lag_ref[0, pl.ds(start, group), :]
        sines = lag_ref[1, pl.ds(start, group), :]
        for w in range(W):
            re_at, im_at = w * 2 * FP, w * 2 * FP + FP
            re = spec[:CB, re_at : re_at + FP].astype(f32)
            im = spec[:CB, im_at : im_at + FP].astype(f32)
            for g in range(group):
                c, s = cosines[g : g + 1, :], sines[g : g + 1, :]
                turned[g * CB : (g + 1) * CB, re_at : re_at + FP] = (re * c + im * s).astype(bf16)
                turned[g * CB : (g + 1) * CB, im_at : im_at + FP] = (im * c - re * s).astype(bf16)
        total = lax.dot_general(
            turned[...], spec[...], (((1,), (1,)), ((), ())), preferred_element_type=f32
        )
        for pair in range(group // 2):
            low = total[2 * pair * CB : (2 * pair + 1) * CB]
            high = total[(2 * pair + 1) * CB : (2 * pair + 2) * CB]
            lanes = pl.ds(pl.multiple_of(start * CB + pair * 2 * CB, 2 * CB), 2 * CB)
            for k in range(BAND + 1):
                both = jnp.concatenate(
                    [low[:, k * CB : (k + 1) * CB], high[:, k * CB : (k + 1) * CB]], axis=1
                )
                keep = own_seg == pseg_ref[k : k + 1, :]
                out_ref[k, :, lanes] = jnp.where(keep, both, 0.0).astype(bf16)
        sources = jnp.concatenate(
            [total[g * CB : (g + 1) * CB, ROWS : ROWS + count] for g in range(group)], axis=1
        )
        src_ref[:, pl.ds(pl.multiple_of(start * count, group * count), group * count)] = sources.astype(bf16)


VMEM = pl.BlockSpec(memory_space=pltpu.VMEM)
SMEM = pl.BlockSpec(memory_space=pltpu.SMEM)


def call(kernel, shapes, scratch, specs, **kwargs):
    return pl.pallas_call(
        kernel, out_shape=shapes, in_specs=specs, out_specs=jax.tree.map(lambda _: VMEM, shapes), scratch_shapes=scratch, **kwargs
    )


def per_device(records, filter_taps, segment_ids):
    count = lax.axis_size("fibre")
    device = lax.axis_index("fibre")

    def ahead(value, distance):
        return lax.ppermute(value, "fibre", [(i, (i - distance) % count) for i in range(count)])

    def swap(value):
        return lax.ppermute(value, "fibre", [(i, i ^ 1) for i in range(count)])

    four = ahead(records, 4)
    two = ahead(records, 2)
    sown = swap(records)

    def edges_of(rows):
        return jnp.concatenate([rows[CB - HALF :], rows[: HALF + 1]], axis=0)

    edge = edges_of(records)
    pieces = []
    for s in range(3, min(8, count // 2)):
        pieces.append(ahead(edge, 2 * s))
    have = 8
    if have < count // 2:
        known = jnp.concatenate([edge, edges_of(two), edges_of(four)] + pieces, axis=0)
    while have < count // 2:
        parts = []
        for s in range(1, 8):
            left = count // 2 - s * have
            if left > 0:
                parts.append(ahead(known[: SPAN * left], 2 * s * have))
        pieces += parts
        known = jnp.concatenate([known] + parts, axis=0)
        have = known.shape[0] // SPAN
    swapped = [swap(piece) for piece in pieces]
    sfour, stwo = swap(four), swap(two)

    index = device.reshape(1)
    band, segs, pseg, pick = call(
        prep_kernel,
        (
            jax.ShapeDtypeStruct((SPAN * CHUNK, 2 * CHUNK), bf16),
            jax.ShapeDtypeStruct((ROWS + 2 * HALO, CHUNK), f32),
            jax.ShapeDtypeStruct((8, CHUNK), f32),
            jax.ShapeDtypeStruct((SPAN * count + 2 * HALO, SLOT * count), bf16),
        ),
        (),
        [SMEM, VMEM, VMEM],
    )(index, filter_taps, segment_ids.reshape(1, -1))

    group = 8
    stacked, source_out = call(
        functools.partial(main_kernel, len(pieces)),
        (
            jax.ShapeDtypeStruct((BAND + 1, CB, LAGS * CB), bf16),
            jax.ShapeDtypeStruct((CB, LAGS * count), bf16),
        ),
        [
            pltpu.VMEM((NCHUNK, ROWS + 2 * HALO, CHUNK), f32),
            pltpu.VMEM((NCHUNK * CB, SPAN * CHUNK), bf16),
            pltpu.VMEM((NCHUNK * count, SPAN * CHUNK), bf16),
            pltpu.VMEM((SLOT * count, W * L), bf16),
            pltpu.VMEM((NCHUNK, ROWS + count, CHUNK), bf16),
            pltpu.VMEM((ROWS + count, KP), bf16),
            pltpu.VMEM((group * CB, KP), bf16),
        ],
        [SMEM] + [VMEM] * (12 + 2 * len(pieces)),
    )(
        index, records, two, four, sown, stwo, sfour, *pieces, *swapped, pick, segs, pseg, band,
        dft_table(), lag_tables(),
    )
    return (jnp.swapaxes(stacked, 0, 1), source_out)


def solution(mesh):
    return jax.shard_map(
        per_device,
        mesh=mesh,
        in_specs=(P(("runs", "fibre"), None), P(), P("runs")),
        out_specs=(P(("runs", "fibre"), None, None), P(("runs", "fibre"), None)),
        check_vma=False,
    )
```

```python
import functools

import jax
import jax.numpy as jnp
import numpy as np
from jax import lax
from jax.experimental import pallas as pl
from jax.experimental.pallas import tpu as pltpu
from jax.sharding import PartitionSpec as P


CB = 64
W = 4
F = 200
L = 400
TAPS = 63
SPAN = 9
LAGS = 32
BAND = 4
HALF = (SPAN - 1) // 2
SLOT = 16
HALO = 8
CHUNK = 128
NCHUNK = -(-W * L // CHUNK)
FP = 256
KP = W * 2 * FP
ROWS = (BAND + 1) * CB
SHIFT = L % CHUNK
COVER = 4 * CHUNK

VMEM_LIMIT = 28 << 20
PREP_LIMIT = 12 << 20
TABLE_LIMIT = 4 << 20

f32 = jnp.float32
bf16 = jnp.bfloat16


def dft_table():
    t = np.arange(L)
    taper = 0.5 - 0.5 * np.cos((t + 0.5) * (2.0 * np.pi / L))
    phase = (t[:, None] * np.arange(F)[None, :] % L) * (2.0 * np.pi / L)
    lead = (W - 1) * SHIFT
    table = np.zeros((lead + COVER, 2 * FP))
    table[lead : lead + L, :F] = taper[:, None] * np.cos(phase)
    table[lead : lead + L, FP : FP + F] = -taper[:, None] * np.sin(phase)
    return jnp.asarray(table.astype(np.float32), bf16)


def lag_tables():
    m = np.arange(LAGS) - LAGS // 2
    phase = (m[:, None] * np.arange(F)[None, :] % L) * (2.0 * np.pi / L)
    scale = 1.0 / np.sqrt(2.0 * L)
    tables = np.zeros((2, LAGS, FP))
    tables[0, :, :F] = np.cos(phase) * scale
    tables[1, :, :F] = -np.sin(phase) * scale
    return jnp.asarray(tables.astype(np.float32), bf16).astype(f32)


def edge_rows(ref):
    return jnp.concatenate(
        [ref[CB - HALO :].astype(f32)[HALO - HALF :], ref[:HALO].astype(f32)[: HALF + 1]], axis=0
    )


def prep_kernel(index_ref, taps_ref, ids_ref, own_ref, edge_ref, band_ref, seg_ref, pseg_ref, pick_ref):
    device = index_ref[0]
    total = ids_ref.shape[1]
    edge_ref[...] = edge_rows(own_ref).astype(bf16)
    count = total // CB
    wide = jnp.concatenate([taps_ref[...].astype(f32), jnp.zeros((SPAN, 2 * CHUNK - TAPS), f32)], axis=1)
    for e in range(SPAN):
        row = jnp.broadcast_to(wide[e : e + 1, :], (CHUNK, 2 * CHUNK))
        band_ref[e * CHUNK : (e + 1) * CHUNK, :] = pltpu.roll(row, 0, 1, stride=1, stride_axis=0).astype(bf16)

    ids = jnp.broadcast_to(ids_ref[...].astype(bf16), (CHUNK, total))

    def segments_at(channels):
        rows = channels.shape[0]
        channels = jnp.where(channels < 0, channels + total, channels)
        channels = jnp.where(channels >= total, channels - total, channels)
        hit = lax.broadcasted_iota(jnp.int32, (rows, total), 1) == channels
        return lax.dot_general(
            jnp.where(hit, 1.0, 0.0).astype(bf16), ids, (((1,), (1,)), ((), ())), preferred_element_type=f32
        )

    def rows_of(rows):
        return lax.broadcasted_iota(jnp.int32, (rows, 1), 0)

    start = device * CB
    near = segments_at(start - HALO + rows_of(ROWS + 2 * HALO))
    seg_ref[...] = near
    for k in range(BAND + 1):
        block = near[HALO + k * CB : HALO + (k + 1) * CB]
        turned = jnp.transpose(jnp.concatenate([block, block], axis=0))
        pseg_ref[k : k + 1, :] = jnp.where(device + k < count, turned[:1], -1.0)
    pseg_ref[BAND + 1 :, :] = jnp.full((8 - BAND - 1, CHUNK), -1.0, f32)

    row = rows_of(SPAN * count)
    e, r = row // count, row % count
    agree = segments_at(start + r * CB + e - HALF) == segments_at(start + r * CB)
    want_block = jnp.where(e < HALF, r - 1, r)
    want_block = jnp.where(want_block < 0, count - 1, want_block)
    side = rows_of(HALO)

    def column_of(block, edge_row):
        other = block // 2 + device % 2
        other = jnp.where(other >= count // 2, other - count // 2, other)
        place = jnp.where(block % 2 == 0, block // 2, count // 2 + other)
        return place * SLOT + edge_row

    columns = SLOT * count

    def one_hot(column, valid):
        hit = lax.broadcasted_iota(jnp.int32, (column.shape[0], columns), 1) == column
        return jnp.where(hit & valid, 1.0, 0.0).astype(bf16)

    agree = jnp.broadcast_to(agree[:, :1], (SPAN * count, columns))
    pick_ref[: SPAN * count, :] = one_hot(column_of(want_block, e), agree)
    low = column_of(jnp.full((HALO, 1), count - 1, jnp.int32), side - HALF)
    pick_ref[SPAN * count : SPAN * count + HALO, :] = one_hot(low, side >= HALF)
    high = column_of(jnp.full((HALO, 1), BAND + 1, jnp.int32), side + HALF)
    pick_ref[SPAN * count + HALO :, :] = one_hot(high, side < HALF)


def copy_kernel(*refs):
    half = len(refs) // 2
    for source, target in zip(refs[:half], refs[half:]):
        target[...] = source[...]


def main_kernel(pieces, *refs):
    index_ref, own_ref, two_ref, four_ref, sown_ref, stwo_ref, sfour_ref = refs[:7]
    edge_refs, swapped_refs, refs = refs[7 : 7 + pieces], refs[7 + pieces : 7 + 2 * pieces], refs[7 + 2 * pieces :]
    pick_ref, seg_ref, pseg_ref, band_ref, dft_ref, lag_ref, out_ref, src_ref = refs[:8]
    rec, masked, smasked, edges, filt, spec, turned, totals = refs[8:]
    even = index_ref[0] % 2 == 0
    count = edges.shape[0] // SLOT

    def chunk(rows, j):
        piece = rows[:, j * CHUNK : min((j + 1) * CHUNK, W * L)]
        if piece.shape[1] < CHUNK:
            piece = jnp.concatenate(
                [piece, jnp.zeros((piece.shape[0], CHUNK - piece.shape[1]), piece.dtype)], axis=1
            )
        return piece

    def put(start, rows):
        for j in range(NCHUNK):
            rec[j, start : start + rows.shape[0], :] = chunk(rows, j)

    stwo = stwo_ref[...].astype(f32)
    put(HALO + CB, jnp.where(even, sown_ref[...].astype(f32), stwo))
    put(HALO + 2 * CB, two_ref[...].astype(f32))
    put(HALO + 3 * CB, jnp.where(even, stwo, sfour_ref[...].astype(f32)))
    put(HALO + 4 * CB, four_ref[...].astype(f32))
    put(HALO, own_ref[...].astype(f32))

    empty = jnp.zeros((SLOT - SPAN, W * L), f32)
    for half, blocks, rest in ((0, (own_ref, two_ref, four_ref), edge_refs), (1, (sown_ref, stwo_ref, sfour_ref), swapped_refs)):
        slot = half * count // 2
        for ref in blocks:
            rows = edge_rows(ref)
            edges[slot * SLOT : (slot + 1) * SLOT, :] = jnp.concatenate([rows, empty], axis=0).astype(bf16)
            slot += 1
        for ref in rest:
            rows = ref[...].astype(f32)
            for first in range(0, rows.shape[0], SPAN):
                edges[slot * SLOT : (slot + 1) * SLOT, :] = jnp.concatenate(
                    [rows[first : first + SPAN], empty], axis=0
                ).astype(bf16)
                slot += 1
    picked = jnp.dot(pick_ref[...], edges[...], preferred_element_type=f32)
    put(0, picked[SPAN * count : SPAN * count + HALO])
    put(HALO + ROWS, picked[SPAN * count + HALO :])
    for e in range(SPAN):
        for j in range(NCHUNK):
            smasked[j * count : (j + 1) * count, e * CHUNK : (e + 1) * CHUNK] = chunk(
                picked[e * count : (e + 1) * count], j
            ).astype(bf16)

    def filtered(inputs, rows, start):
        share = jnp.dot(inputs[...], band_ref[...], preferred_element_type=f32)
        for j in range(NCHUNK):
            result = share[j * rows : (j + 1) * rows, :CHUNK]
            if j:
                result = result + share[(j - 1) * rows : j * rows, CHUNK:]
            filt[j, pl.ds(start, rows), :] = result.astype(bf16)

    filtered(smasked, count, ROWS)

    for k in range(BAND + 1):
        base = k * CB
        held = masked.at[k % 2]
        centre = seg_ref[pl.ds(base + HALO, CB), :]
        for e in range(SPAN):
            first = base + (HALO - HALF + e)
            keep = seg_ref[pl.ds(first, CB), :] == centre
            for j in range(NCHUNK):
                rows = rec[j, pl.ds(first, CB), :]
                held[j * CB : (j + 1) * CB, e * CHUNK : (e + 1) * CHUNK] = jnp.where(keep, rows, 0.0).astype(bf16)
        filtered(held, CB, base)

    for w in range(W):
        first = w * (L // CHUNK)
        lhs = jnp.concatenate([filt[first + q] for q in range(COVER // CHUNK)], axis=1)
        lead = (W - 1 - w) * SHIFT
        raw = jnp.dot(lhs, dft_ref[lead : lead + COVER, :], preferred_element_type=f32)
        power = jnp.sum(raw * raw, axis=-1, keepdims=True) * (1.0 / L)
        spec[:, w * 2 * FP : (w + 1) * 2 * FP] = (raw * lax.rsqrt(power + 1e-06)).astype(bf16)

    row = lax.broadcasted_iota(jnp.int32, (count, count), 0)
    column = lax.broadcasted_iota(jnp.int32, (count, count), 1)
    ahead = row - index_ref[0]
    ahead = jnp.where(ahead < 0, ahead + count, ahead)
    order = jnp.where(ahead == column, 1.0, 0.0).astype(bf16)
    spec[ROWS:, :] = jnp.dot(order, spec[ROWS:, :], preferred_element_type=f32).astype(bf16)

    group = turned.shape[0] // CB
    steps = LAGS // group
    own_seg = seg_ref[HALO : HALO + CB, :]

    def multiply(step, slot):
        start = pl.multiple_of(step * group, group)
        cosines = lag_ref[0, pl.ds(start, group), :]
        sines = lag_ref[1, pl.ds(start, group), :]
        for w in range(W):
            re_at, im_at = w * 2 * FP, w * 2 * FP + FP
            re = spec[:CB, re_at : re_at + FP].astype(f32)
            im = spec[:CB, im_at : im_at + FP].astype(f32)
            for g in range(group):
                c, s = cosines[g : g + 1, :], sines[g : g + 1, :]
                turned[g * CB : (g + 1) * CB, re_at : re_at + FP] = (re * c + im * s).astype(bf16)
                turned[g * CB : (g + 1) * CB, im_at : im_at + FP] = (im * c - re * s).astype(bf16)
        totals[slot] = lax.dot_general(
            turned[...], spec[...], (((1,), (1,)), ((), ())), preferred_element_type=f32
        )

    def write(step, slot):
        start = pl.multiple_of(step * group, group)
        for pair in range(group // 2):
            low, high = 2 * pair * CB, (2 * pair + 1) * CB
            lanes = pl.ds(pl.multiple_of(start * CB + pair * 2 * CB, 2 * CB), 2 * CB)
            for k in range(BAND + 1):
                both = jnp.concatenate(
                    [totals[slot, at : at + CB, k * CB : (k + 1) * CB] for at in (low, high)], axis=1
                )
                keep = own_seg == pseg_ref[k : k + 1, :]
                out_ref[k, :, lanes] = jnp.where(keep, both, 0.0).astype(bf16)
        sources = jnp.concatenate(
            [totals[slot, g * CB : (g + 1) * CB, ROWS : ROWS + count] for g in range(group)], axis=1
        )
        src_ref[:, pl.ds(pl.multiple_of(start * count, group * count), group * count)] = sources.astype(bf16)

    multiply(0, 0)

    @pl.loop(1, steps)
    def _(step):
        write(step - 1, (step - 1) % 2)
        multiply(step, step % 2)

    write(steps - 1, (steps - 1) % 2)


VMEM = pl.BlockSpec(memory_space=pltpu.VMEM)
SMEM = pl.BlockSpec(memory_space=pltpu.SMEM)


def call(kernel, shapes, scratch, specs, **kwargs):
    return pl.pallas_call(
        kernel, out_shape=shapes, in_specs=specs, out_specs=jax.tree.map(lambda _: VMEM, shapes), scratch_shapes=scratch, **kwargs
    )


def per_device(records, filter_taps, segment_ids):
    count = lax.axis_size("fibre")
    device = lax.axis_index("fibre")

    def ahead(value, distance):
        return lax.ppermute(value, "fibre", [(i, (i - distance) % count) for i in range(count)])

    def swap(value):
        return lax.ppermute(value, "fibre", [(i, i ^ 1) for i in range(count)])

    four = ahead(records, 4)
    two = ahead(records, 2)
    sown = swap(records)

    index = device.reshape(1)
    few = count <= 16
    edge, band, segs, pseg, pick = call(
        prep_kernel,
        (
            jax.ShapeDtypeStruct((SPAN, W * L), bf16),
            jax.ShapeDtypeStruct((SPAN * CHUNK, 2 * CHUNK), bf16),
            jax.ShapeDtypeStruct((ROWS + 2 * HALO, CHUNK), f32),
            jax.ShapeDtypeStruct((8, CHUNK), f32),
            jax.ShapeDtypeStruct((SPAN * count + 2 * HALO, SLOT * count), bf16),
        ),
        (),
        [SMEM, VMEM, VMEM, VMEM],
        compiler_params=pltpu.CompilerParams(vmem_limit_bytes=PREP_LIMIT if few else None),
    )(index, filter_taps, segment_ids.reshape(1, -1), records)

    def edges_of(rows):
        return jnp.concatenate([rows[CB - HALF :], rows[: HALF + 1]], axis=0)

    pieces = []
    for s in range(3, min(8, count // 2)):
        pieces.append(ahead(edge, 2 * s))
    have = 8
    if have < count // 2:
        known = jnp.concatenate([edge, edges_of(two), edges_of(four)] + pieces, axis=0)
    while have < count // 2:
        parts = []
        for s in range(1, 8):
            left = count // 2 - s * have
            if left > 0:
                parts.append(ahead(known[: SPAN * left], 2 * s * have))
        pieces += parts
        known = jnp.concatenate([known] + parts, axis=0)
        have = known.shape[0] // SPAN
    swapped = [swap(piece) for piece in pieces]
    sfour, stwo = swap(four), swap(two)

    group = 8
    tables = (records, dft_table(), lag_tables())
    own, dft, lags = call(
        copy_kernel,
        tuple(jax.ShapeDtypeStruct(table.shape, table.dtype) for table in tables),
        (),
        [VMEM] * 3,
        compiler_params=pltpu.CompilerParams(vmem_limit_bytes=TABLE_LIMIT),
    )(*tables)
    stacked, source_out = call(
        functools.partial(main_kernel, len(pieces)),
        (
            jax.ShapeDtypeStruct((BAND + 1, CB, LAGS * CB), bf16),
            jax.ShapeDtypeStruct((CB, LAGS * count), bf16),
        ),
        [
            pltpu.VMEM((NCHUNK, ROWS + 2 * HALO, CHUNK), f32),
            pltpu.VMEM((2, NCHUNK * CB, SPAN * CHUNK), bf16),
            pltpu.VMEM((NCHUNK * count, SPAN * CHUNK), bf16),
            pltpu.VMEM((SLOT * count, W * L), bf16),
            pltpu.VMEM((NCHUNK, ROWS + count, CHUNK), bf16),
            pltpu.VMEM((ROWS + count, KP), bf16),
            pltpu.VMEM((group * CB, KP), bf16),
            pltpu.VMEM((2, group * CB, ROWS + count), f32),
        ],
        [SMEM] + [VMEM] * (12 + 2 * len(pieces)),
        compiler_params=pltpu.CompilerParams(vmem_limit_bytes=VMEM_LIMIT if few else None),
    )(
        index, own, two, four, sown, stwo, sfour, *pieces, *swapped, pick, segs, pseg, band,
        dft, lags,
    )
    return (jnp.swapaxes(stacked, 0, 1), source_out)


def solution(mesh):
    return jax.shard_map(
        per_device,
        mesh=mesh,
        in_specs=(P(("runs", "fibre"), None), P(), P("runs")),
        out_specs=(P(("runs", "fibre"), None, None), P(("runs", "fibre"), None)),
        check_vma=False,
    )
```

```python
import functools

import jax
import jax.numpy as jnp
import numpy as np
from jax import lax
from jax.experimental import pallas as pl
from jax.experimental.pallas import tpu as pltpu
from jax.sharding import PartitionSpec as P


CB = 64
W = 4
F = 200
L = 400
TAPS = 63
SPAN = 9
LAGS = 32
BAND = 4
HALF = (SPAN - 1) // 2
SLOT = 16
HALO = 8
CHUNK = 128
NCHUNK = -(-W * L // CHUNK)
FP = 256
KP = W * 2 * FP
ROWS = (BAND + 1) * CB
SHIFT = L % CHUNK
COVER = 4 * CHUNK

VMEM_LIMIT = 28 << 20
PREP_LIMIT = 12 << 20

f32 = jnp.float32
bf16 = jnp.bfloat16


def dft_table():
    t = np.arange(L)
    taper = 0.5 - 0.5 * np.cos((t + 0.5) * (2.0 * np.pi / L))
    phase = (t[:, None] * np.arange(F)[None, :] % L) * (2.0 * np.pi / L)
    lead = (W - 1) * SHIFT
    table = np.zeros((lead + COVER, 2 * FP))
    table[lead : lead + L, :F] = taper[:, None] * np.cos(phase)
    table[lead : lead + L, FP : FP + F] = -taper[:, None] * np.sin(phase)
    return jnp.asarray(table.astype(np.float32), bf16)


def lag_tables():
    m = np.arange(LAGS) - LAGS // 2
    phase = (m[:, None] * np.arange(F)[None, :] % L) * (2.0 * np.pi / L)
    scale = 1.0 / np.sqrt(2.0 * L)
    tables = np.zeros((2, LAGS, FP))
    tables[0, :, :F] = np.cos(phase) * scale
    tables[1, :, :F] = -np.sin(phase) * scale
    return jnp.asarray(tables.astype(np.float32), bf16).astype(f32)


def start_loads(pairs, sems):
    loads = [pltpu.make_async_copy(source, target, sems.at[i]) for i, (source, target) in enumerate(pairs)]
    for load in loads:
        load.start()
    return loads


def edge_rows(ref):
    return jnp.concatenate(
        [ref[CB - HALO :].astype(f32)[HALO - HALF :], ref[:HALO].astype(f32)[: HALF + 1]], axis=0
    )


def prep_kernel(
    index_ref, taps_hbm, ids_hbm, own_hbm, edge_ref, band_ref, seg_ref, pseg_ref, pick_ref, taps_ref, ids_ref, own_ref, sems
):
    device = index_ref[0]
    total = ids_ref.shape[1]
    loads = start_loads(((own_hbm, own_ref), (taps_hbm, taps_ref), (ids_hbm, ids_ref)), sems)
    for load in loads:
        load.wait()
    edge_ref[...] = edge_rows(own_ref).astype(bf16)
    count = total // CB
    wide = jnp.concatenate([taps_ref[...].astype(f32), jnp.zeros((SPAN, 2 * CHUNK - TAPS), f32)], axis=1)
    for e in range(SPAN):
        row = jnp.broadcast_to(wide[e : e + 1, :], (CHUNK, 2 * CHUNK))
        band_ref[e * CHUNK : (e + 1) * CHUNK, :] = pltpu.roll(row, 0, 1, stride=1, stride_axis=0).astype(bf16)

    ids = jnp.broadcast_to(ids_ref[...].astype(bf16), (CHUNK, total))

    def segments_at(channels):
        rows = channels.shape[0]
        channels = jnp.where(channels < 0, channels + total, channels)
        channels = jnp.where(channels >= total, channels - total, channels)
        hit = lax.broadcasted_iota(jnp.int32, (rows, total), 1) == channels
        return lax.dot_general(
            jnp.where(hit, 1.0, 0.0).astype(bf16), ids, (((1,), (1,)), ((), ())), preferred_element_type=f32
        )

    def rows_of(rows):
        return lax.broadcasted_iota(jnp.int32, (rows, 1), 0)

    start = device * CB
    near = segments_at(start - HALO + rows_of(ROWS + 2 * HALO))
    seg_ref[...] = near
    for k in range(BAND + 1):
        block = near[HALO + k * CB : HALO + (k + 1) * CB]
        turned = jnp.transpose(jnp.concatenate([block, block], axis=0))
        pseg_ref[k : k + 1, :] = jnp.where(device + k < count, turned[:1], -1.0)
    pseg_ref[BAND + 1 :, :] = jnp.full((8 - BAND - 1, CHUNK), -1.0, f32)

    row = rows_of(SPAN * count)
    e, r = row // count, row % count
    agree = segments_at(start + r * CB + e - HALF) == segments_at(start + r * CB)
    want_block = jnp.where(e < HALF, r - 1, r)
    want_block = jnp.where(want_block < 0, count - 1, want_block)
    side = rows_of(HALO)

    def column_of(block, edge_row):
        other = block // 2 + device % 2
        other = jnp.where(other >= count // 2, other - count // 2, other)
        place = jnp.where(block % 2 == 0, block // 2, count // 2 + other)
        return place * SLOT + edge_row

    columns = SLOT * count

    def one_hot(column, valid):
        hit = lax.broadcasted_iota(jnp.int32, (column.shape[0], columns), 1) == column
        return jnp.where(hit & valid, 1.0, 0.0).astype(bf16)

    agree = jnp.broadcast_to(agree[:, :1], (SPAN * count, columns))
    pick_ref[: SPAN * count, :] = one_hot(column_of(want_block, e), agree)
    low = column_of(jnp.full((HALO, 1), count - 1, jnp.int32), side - HALF)
    pick_ref[SPAN * count : SPAN * count + HALO, :] = one_hot(low, side >= HALF)
    high = column_of(jnp.full((HALO, 1), BAND + 1, jnp.int32), side + HALF)
    pick_ref[SPAN * count + HALO :, :] = one_hot(high, side < HALF)


def main_kernel(pieces, *refs):
    index_ref, own_hbm, two_ref, four_ref, sown_ref, stwo_ref, sfour_ref = refs[:7]
    edge_refs, swapped_refs, refs = refs[7 : 7 + pieces], refs[7 + pieces : 7 + 2 * pieces], refs[7 + 2 * pieces :]
    pick_ref, seg_ref, pseg_ref, band_ref, dft_hbm, lag_hbm, out_ref, src_ref = refs[:8]
    rec, masked, smasked, edges, filt, spec, turned, totals, own_ref, dft_ref, lag_ref, sems = refs[8:]
    loads = start_loads(((own_hbm, own_ref), (dft_hbm, dft_ref), (lag_hbm, lag_ref)), sems)
    even = index_ref[0] % 2 == 0
    count = edges.shape[0] // SLOT

    def chunk(rows, j):
        piece = rows[:, j * CHUNK : min((j + 1) * CHUNK, W * L)]
        if piece.shape[1] < CHUNK:
            piece = jnp.concatenate(
                [piece, jnp.zeros((piece.shape[0], CHUNK - piece.shape[1]), piece.dtype)], axis=1
            )
        return piece

    def put(start, rows):
        for j in range(NCHUNK):
            rec[j, start : start + rows.shape[0], :] = chunk(rows, j)

    stwo = stwo_ref[...].astype(f32)
    put(HALO + CB, jnp.where(even, sown_ref[...].astype(f32), stwo))
    put(HALO + 2 * CB, two_ref[...].astype(f32))
    put(HALO + 3 * CB, jnp.where(even, stwo, sfour_ref[...].astype(f32)))
    put(HALO + 4 * CB, four_ref[...].astype(f32))
    loads[0].wait()
    put(HALO, own_ref[...].astype(f32))

    empty = jnp.zeros((SLOT - SPAN, W * L), f32)
    for half, blocks, rest in ((0, (own_ref, two_ref, four_ref), edge_refs), (1, (sown_ref, stwo_ref, sfour_ref), swapped_refs)):
        slot = half * count // 2
        for ref in blocks:
            rows = edge_rows(ref)
            edges[slot * SLOT : (slot + 1) * SLOT, :] = jnp.concatenate([rows, empty], axis=0).astype(bf16)
            slot += 1
        for ref in rest:
            rows = ref[...].astype(f32)
            for first in range(0, rows.shape[0], SPAN):
                edges[slot * SLOT : (slot + 1) * SLOT, :] = jnp.concatenate(
                    [rows[first : first + SPAN], empty], axis=0
                ).astype(bf16)
                slot += 1
    picked = jnp.dot(pick_ref[...], edges[...], preferred_element_type=f32)
    put(0, picked[SPAN * count : SPAN * count + HALO])
    put(HALO + ROWS, picked[SPAN * count + HALO :])
    for e in range(SPAN):
        for j in range(NCHUNK):
            smasked[j * count : (j + 1) * count, e * CHUNK : (e + 1) * CHUNK] = chunk(
                picked[e * count : (e + 1) * count], j
            ).astype(bf16)

    def filtered(inputs, rows, start):
        share = jnp.dot(inputs[...], band_ref[...], preferred_element_type=f32)
        for j in range(NCHUNK):
            result = share[j * rows : (j + 1) * rows, :CHUNK]
            if j:
                result = result + share[(j - 1) * rows : j * rows, CHUNK:]
            filt[j, pl.ds(start, rows), :] = result.astype(bf16)

    filtered(smasked, count, ROWS)

    for k in range(BAND + 1):
        base = k * CB
        held = masked.at[k % 2]
        centre = seg_ref[pl.ds(base + HALO, CB), :]
        for e in range(SPAN):
            first = base + (HALO - HALF + e)
            keep = seg_ref[pl.ds(first, CB), :] == centre
            for j in range(NCHUNK):
                rows = rec[j, pl.ds(first, CB), :]
                held[j * CB : (j + 1) * CB, e * CHUNK : (e + 1) * CHUNK] = jnp.where(keep, rows, 0.0).astype(bf16)
        filtered(held, CB, base)

    loads[1].wait()
    loads[2].wait()
    for w in range(W):
        first = w * (L // CHUNK)
        lhs = jnp.concatenate([filt[first + q] for q in range(COVER // CHUNK)], axis=1)
        lead = (W - 1 - w) * SHIFT
        raw = jnp.dot(lhs, dft_ref[lead : lead + COVER, :], preferred_element_type=f32)
        power = jnp.sum(raw * raw, axis=-1, keepdims=True) * (1.0 / L)
        spec[:, w * 2 * FP : (w + 1) * 2 * FP] = (raw * lax.rsqrt(power + 1e-06)).astype(bf16)

    row = lax.broadcasted_iota(jnp.int32, (count, count), 0)
    column = lax.broadcasted_iota(jnp.int32, (count, count), 1)
    ahead = row - index_ref[0]
    ahead = jnp.where(ahead < 0, ahead + count, ahead)
    order = jnp.where(ahead == column, 1.0, 0.0).astype(bf16)
    spec[ROWS:, :] = jnp.dot(order, spec[ROWS:, :], preferred_element_type=f32).astype(bf16)

    group = turned.shape[0] // CB
    steps = LAGS // group
    own_seg = seg_ref[HALO : HALO + CB, :]

    def multiply(step, slot):
        start = pl.multiple_of(step * group, group)
        cosines = lag_ref[0, pl.ds(start, group), :]
        sines = lag_ref[1, pl.ds(start, group), :]
        for w in range(W):
            re_at, im_at = w * 2 * FP, w * 2 * FP + FP
            re = spec[:CB, re_at : re_at + FP].astype(f32)
            im = spec[:CB, im_at : im_at + FP].astype(f32)
            for g in range(group):
                c, s = cosines[g : g + 1, :], sines[g : g + 1, :]
                turned[g * CB : (g + 1) * CB, re_at : re_at + FP] = (re * c + im * s).astype(bf16)
                turned[g * CB : (g + 1) * CB, im_at : im_at + FP] = (im * c - re * s).astype(bf16)
        totals[slot] = lax.dot_general(
            turned[...], spec[...], (((1,), (1,)), ((), ())), preferred_element_type=f32
        )

    def write(step, slot):
        start = pl.multiple_of(step * group, group)
        for pair in range(group // 2):
            low, high = 2 * pair * CB, (2 * pair + 1) * CB
            lanes = pl.ds(pl.multiple_of(start * CB + pair * 2 * CB, 2 * CB), 2 * CB)
            for k in range(BAND + 1):
                both = jnp.concatenate(
                    [totals[slot, at : at + CB, k * CB : (k + 1) * CB] for at in (low, high)], axis=1
                )
                keep = own_seg == pseg_ref[k : k + 1, :]
                out_ref[k, :, lanes] = jnp.where(keep, both, 0.0).astype(bf16)
        sources = jnp.concatenate(
            [totals[slot, g * CB : (g + 1) * CB, ROWS : ROWS + count] for g in range(group)], axis=1
        )
        src_ref[:, pl.ds(pl.multiple_of(start * count, group * count), group * count)] = sources.astype(bf16)

    multiply(0, 0)

    @pl.loop(1, steps)
    def _(step):
        write(step - 1, (step - 1) % 2)
        multiply(step, step % 2)

    write(steps - 1, (steps - 1) % 2)


VMEM = pl.BlockSpec(memory_space=pltpu.VMEM)
SMEM = pl.BlockSpec(memory_space=pltpu.SMEM)
HBM = pl.BlockSpec(memory_space=pltpu.HBM)


def call(kernel, shapes, scratch, specs, **kwargs):
    return pl.pallas_call(
        kernel, out_shape=shapes, in_specs=specs, out_specs=jax.tree.map(lambda _: VMEM, shapes), scratch_shapes=scratch, **kwargs
    )


def per_device(records, filter_taps, segment_ids):
    count = lax.axis_size("fibre")
    device = lax.axis_index("fibre")

    def ahead(value, distance):
        return lax.ppermute(value, "fibre", [(i, (i - distance) % count) for i in range(count)])

    def swap(value):
        return lax.ppermute(value, "fibre", [(i, i ^ 1) for i in range(count)])

    four = ahead(records, 4)
    two = ahead(records, 2)
    sown = swap(records)

    index = device.reshape(1)
    stay = functools.partial(pltpu.with_memory_space_constraint, memory_space=pltpu.HBM)
    few = count <= 16
    edge, band, segs, pseg, pick = call(
        prep_kernel,
        (
            jax.ShapeDtypeStruct((SPAN, W * L), bf16),
            jax.ShapeDtypeStruct((SPAN * CHUNK, 2 * CHUNK), bf16),
            jax.ShapeDtypeStruct((ROWS + 2 * HALO, CHUNK), f32),
            jax.ShapeDtypeStruct((8, CHUNK), f32),
            jax.ShapeDtypeStruct((SPAN * count + 2 * HALO, SLOT * count), bf16),
        ),
        [
            pltpu.VMEM(filter_taps.shape, bf16),
            pltpu.VMEM((1,) + segment_ids.shape, jnp.int32),
            pltpu.VMEM(records.shape, bf16),
            pltpu.SemaphoreType.DMA((3,)),
        ],
        [SMEM, HBM, HBM, HBM],
        compiler_params=pltpu.CompilerParams(vmem_limit_bytes=PREP_LIMIT if few else None),
    )(index, stay(filter_taps), stay(segment_ids.reshape(1, -1)), stay(records))

    def edges_of(rows):
        return jnp.concatenate([rows[CB - HALF :], rows[: HALF + 1]], axis=0)

    pieces = []
    for s in range(3, min(8, count // 2)):
        pieces.append(ahead(edge, 2 * s))
    have = 8
    if have < count // 2:
        known = jnp.concatenate([edge, edges_of(two), edges_of(four)] + pieces, axis=0)
    while have < count // 2:
        parts = []
        for s in range(1, 8):
            left = count // 2 - s * have
            if left > 0:
                parts.append(ahead(known[: SPAN * left], 2 * s * have))
        pieces += parts
        known = jnp.concatenate([known] + parts, axis=0)
        have = known.shape[0] // SPAN
    swapped = [swap(piece) for piece in pieces]
    sfour, stwo = swap(four), swap(two)

    group = 8
    dft, lags = dft_table(), lag_tables()
    stacked, source_out = call(
        functools.partial(main_kernel, len(pieces)),
        (
            jax.ShapeDtypeStruct((BAND + 1, CB, LAGS * CB), bf16),
            jax.ShapeDtypeStruct((CB, LAGS * count), bf16),
        ),
        [
            pltpu.VMEM((NCHUNK, ROWS + 2 * HALO, CHUNK), f32),
            pltpu.VMEM((2, NCHUNK * CB, SPAN * CHUNK), bf16),
            pltpu.VMEM((NCHUNK * count, SPAN * CHUNK), bf16),
            pltpu.VMEM((SLOT * count, W * L), bf16),
            pltpu.VMEM((NCHUNK, ROWS + count, CHUNK), bf16),
            pltpu.VMEM((ROWS + count, KP), bf16),
            pltpu.VMEM((group * CB, KP), bf16),
            pltpu.VMEM((2, group * CB, ROWS + count), f32),
            pltpu.VMEM((CB, W * L), bf16),
            pltpu.VMEM(dft.shape, bf16),
            pltpu.VMEM(lags.shape, f32),
            pltpu.SemaphoreType.DMA((3,)),
        ],
        [SMEM, HBM] + [VMEM] * (9 + 2 * len(pieces)) + [HBM] * 2,
        compiler_params=pltpu.CompilerParams(vmem_limit_bytes=VMEM_LIMIT if few else None),
    )(
        index, stay(records), two, four, sown, stwo, sfour, *pieces, *swapped, pick, segs, pseg, band,
        stay(dft), stay(lags),
    )
    return (jnp.swapaxes(stacked, 0, 1), source_out)


def solution(mesh):
    return jax.shard_map(
        per_device,
        mesh=mesh,
        in_specs=(P(("runs", "fibre"), None), P(), P("runs")),
        out_specs=(P(("runs", "fibre"), None, None), P(("runs", "fibre"), None)),
        check_vma=False,
    )
```

```python
import functools

import jax
import jax.numpy as jnp
import numpy as np
from jax import lax
from jax.experimental import pallas as pl
from jax.experimental.pallas import tpu as pltpu
from jax.sharding import PartitionSpec as P


CB = 64
W = 4
F = 200
L = 400
TAPS = 63
SPAN = 9
LAGS = 32
BAND = 4
HALF = (SPAN - 1) // 2
SLOT = 16
HALO = 8
CHUNK = 128
NCHUNK = -(-W * L // CHUNK)
FP = 256
KP = W * 2 * FP
ROWS = (BAND + 1) * CB
SHIFT = L % CHUNK
COVER = 4 * CHUNK

VMEM_LIMIT = 28 << 20
PREP_LIMIT = 12 << 20
EDGE_LIMIT = 1 << 20
TABLE_LIMIT = 2 << 20

f32 = jnp.float32
bf16 = jnp.bfloat16


def dft_table():
    t = np.arange(L)
    taper = 0.5 - 0.5 * np.cos((t + 0.5) * (2.0 * np.pi / L))
    phase = (t[:, None] * np.arange(F)[None, :] % L) * (2.0 * np.pi / L)
    lead = (W - 1) * SHIFT
    table = np.zeros((lead + COVER, 2 * FP))
    table[lead : lead + L, :F] = taper[:, None] * np.cos(phase)
    table[lead : lead + L, FP : FP + F] = -taper[:, None] * np.sin(phase)
    return jnp.asarray(table.astype(np.float32), bf16)


def lag_tables():
    m = np.arange(LAGS) - LAGS // 2
    phase = (m[:, None] * np.arange(F)[None, :] % L) * (2.0 * np.pi / L)
    scale = 1.0 / np.sqrt(2.0 * L)
    tables = np.zeros((2, LAGS, FP))
    tables[0, :, :F] = np.cos(phase) * scale
    tables[1, :, :F] = -np.sin(phase) * scale
    return jnp.asarray(tables.astype(np.float32), bf16).astype(f32)


def start_loads(pairs, sems):
    loads = [pltpu.make_async_copy(source, target, sems.at[i]) for i, (source, target) in enumerate(pairs)]
    for load in loads:
        load.start()
    return loads


def edge_kernel(own_hbm, edge_ref, sems):
    last = (own_hbm.at[pl.ds(CB - HALO, HALO)], edge_ref.at[pl.ds(0, HALO)])
    first = (own_hbm.at[pl.ds(0, HALO)], edge_ref.at[pl.ds(HALO, HALO)])
    for load in start_loads((last, first), sems):
        load.wait()


def chunk(rows, j):
    piece = rows[:, j * CHUNK : min((j + 1) * CHUNK, W * L)]
    if piece.shape[1] < CHUNK:
        piece = jnp.concatenate([piece, jnp.zeros((piece.shape[0], CHUNK - piece.shape[1]), piece.dtype)], axis=1)
    return piece


def filter_row(row_at, seg_ref, centre, line, band_ref):
    own = seg_ref[centre : centre + 1, :]
    line[...] = jnp.zeros_like(line)
    for e in range(SPAN):
        at = centre - HALF + e
        keep = seg_ref[at : at + 1, :] == own
        for j in range(NCHUNK):
            line[j : j + 1, e * CHUNK : (e + 1) * CHUNK] = jnp.where(keep, row_at(e, j), 0.0)
    share = jnp.dot(line[...].astype(bf16), band_ref[...], preferred_element_type=f32)
    before = jnp.concatenate([jnp.zeros((1, CHUNK), f32), share[:-1, CHUNK:]], axis=0)
    return share[:, :CHUNK] + before


def prep_kernel(
    index_ref, edge_ref, halo_ref, sown_ref, taps_hbm, ids_hbm, source_ref, band_ref, seg_ref, pseg_ref,
    taps_ref, ids_ref, line, sems,
):
    loads = start_loads(((taps_hbm, taps_ref), (ids_hbm, ids_ref)), sems)
    device = index_ref[0]
    total = ids_ref.shape[1]
    count = total // CB
    loads[0].wait()
    wide = jnp.concatenate([taps_ref[...].astype(f32), jnp.zeros((SPAN, 2 * CHUNK - TAPS), f32)], axis=1)
    for e in range(SPAN):
        row = jnp.broadcast_to(wide[e : e + 1, :], (CHUNK, 2 * CHUNK))
        band_ref[e * CHUNK : (e + 1) * CHUNK, :] = pltpu.roll(row, 0, 1, stride=1, stride_axis=0).astype(bf16)

    loads[1].wait()
    ids = jnp.broadcast_to(ids_ref[...].astype(bf16), (CHUNK, total))
    channels = device * CB - HALO + lax.broadcasted_iota(jnp.int32, (ROWS + 2 * HALO, 1), 0)
    channels = jnp.where(channels < 0, channels + total, channels)
    channels = jnp.where(channels >= total, channels - total, channels)
    hit = lax.broadcasted_iota(jnp.int32, (ROWS + 2 * HALO, total), 1) == channels
    seg_ref[...] = lax.dot_general(
        jnp.where(hit, 1.0, 0.0).astype(bf16), ids, (((1,), (1,)), ((), ())), preferred_element_type=f32
    )
    for k in range(BAND + 1):
        block = seg_ref[HALO + k * CB : HALO + (k + 1) * CB, :]
        turned = jnp.transpose(jnp.concatenate([block, block], axis=0))
        pseg_ref[k : k + 1, :] = jnp.where(device + k < count, turned[:1], -1.0)
    pseg_ref[BAND + 1 :, :] = jnp.full((8 - BAND - 1, CHUNK), -1.0, f32)

    even = device % 2 == 0
    behind = jnp.where(even, halo_ref[:HALO].astype(f32), sown_ref[CB - HALO :].astype(f32))
    first = edge_ref[HALO:].astype(f32)

    def row_at(e, j):
        rows, at = (behind, HALO - HALF + e) if e < HALF else (first, e - HALF)
        return chunk(rows, j)[at : at + 1]

    source_ref[...] = filter_row(row_at, seg_ref, HALO, line, band_ref).astype(bf16)


def table_kernel(*refs):
    half = (len(refs) - 1) // 2
    for load in start_loads(tuple(zip(refs[:half], refs[half:-1])), refs[-1]):
        load.wait()


def main_kernel(pieces, count, *refs):
    index_ref, own_ref, two_ref, four_ref, sown_ref, stwo_ref, sfour_ref, halo_ref = refs[:8]
    part_refs, swapped_refs, refs = refs[8 : 8 + pieces], refs[8 + pieces : 9 + 2 * pieces], refs[9 + 2 * pieces :]
    seg_ref, pseg_ref, band_ref, dft_ref, lag_ref, out_ref, src_ref = refs[:7]
    rec, masked, filt, spec, turned, totals, line = refs[7:]
    even = index_ref[0] % 2 == 0

    def put(start, rows):
        for j in range(NCHUNK):
            rec[j, start : start + rows.shape[0], :] = chunk(rows, j)

    stwo, sfour = stwo_ref[...].astype(f32), sfour_ref[...].astype(f32)
    sown, halo = sown_ref[...].astype(f32), halo_ref[...].astype(f32)
    put(0, jnp.where(even, halo[:HALO], sown[CB - HALO :]))
    put(HALO, own_ref[...].astype(f32))
    put(HALO + CB, jnp.where(even, sown, stwo))
    put(HALO + 2 * CB, two_ref[...].astype(f32))
    put(HALO + 3 * CB, jnp.where(even, stwo, sfour))
    put(HALO + 4 * CB, four_ref[...].astype(f32))
    put(HALO + ROWS, jnp.where(even, sfour[:HALO], halo[HALO:]))

    def filtered(inputs, rows, start):
        share = jnp.dot(inputs[...], band_ref[...], preferred_element_type=f32)
        for j in range(NCHUNK):
            result = share[j * rows : (j + 1) * rows, :CHUNK]
            if j:
                result = result + share[(j - 1) * rows : j * rows, CHUNK:]
            filt[j, pl.ds(start, rows), :] = result.astype(bf16)

    for k in range(BAND + 1):
        base = k * CB
        held = masked.at[k % 2]
        centre = seg_ref[pl.ds(base + HALO, CB), :]
        for e in range(SPAN):
            first = base + (HALO - HALF + e)
            keep = seg_ref[pl.ds(first, CB), :] == centre
            for j in range(NCHUNK):
                rows = rec[j, pl.ds(first, CB), :]
                held[j * CB : (j + 1) * CB, e * CHUNK : (e + 1) * CHUNK] = jnp.where(keep, rows, 0.0).astype(bf16)
        filtered(held, CB, base)

    mine, theirs = [], []
    for refs, rows in ((part_refs, mine), (swapped_refs, theirs)):
        for ref in refs:
            value = ref[...].astype(f32)
            rows += [value[at : at + SLOT] for at in range(0, value.shape[0], SLOT)]
    lists = count // 2
    skip = lists - len(mine)
    theirs = [theirs[0]] + [None] * (skip - 1) + theirs[1:]

    def next_row(e, j):
        at = HALO + ROWS - HALF + e
        return rec[j, at : at + 1, :]

    for r in range(count):
        if r <= BAND:
            rows = [filt[j, r * CB : r * CB + 1, :] for j in range(NCHUNK)]
        else:
            if r == BAND + 1:
                value = filter_row(next_row, seg_ref, HALO + ROWS, line, band_ref)
            elif r % 2 == 0:
                value = mine[r // 2 - skip]
            else:
                value = jnp.where(even, theirs[r // 2], theirs[(r // 2 + 1) % lists])
            rows = [value[j : j + 1].astype(bf16) for j in range(NCHUNK)]
        for j in range(NCHUNK):
            filt[j, ROWS + r : ROWS + r + 1, :] = rows[j]

    for w in range(W):
        first = w * (L // CHUNK)
        lhs = jnp.concatenate([filt[first + q] for q in range(COVER // CHUNK)], axis=1)
        lead = (W - 1 - w) * SHIFT
        raw = jnp.dot(lhs, dft_ref[lead : lead + COVER, :], preferred_element_type=f32)
        power = jnp.sum(raw * raw, axis=-1, keepdims=True) * (1.0 / L)
        spec[:, w * 2 * FP : (w + 1) * 2 * FP] = (raw * lax.rsqrt(power + 1e-06)).astype(bf16)

    row = lax.broadcasted_iota(jnp.int32, (count, count), 0)
    column = lax.broadcasted_iota(jnp.int32, (count, count), 1)
    ahead = row - index_ref[0]
    ahead = jnp.where(ahead < 0, ahead + count, ahead)
    order = jnp.where(ahead == column, 1.0, 0.0).astype(bf16)
    spec[ROWS:, :] = jnp.dot(order, spec[ROWS:, :], preferred_element_type=f32).astype(bf16)

    group = turned.shape[0] // CB
    steps = LAGS // group
    own_seg = seg_ref[HALO : HALO + CB, :]

    def multiply(step, slot):
        start = pl.multiple_of(step * group, group)
        cosines = lag_ref[0, pl.ds(start, group), :]
        sines = lag_ref[1, pl.ds(start, group), :]
        for w in range(W):
            re_at, im_at = w * 2 * FP, w * 2 * FP + FP
            re = spec[:CB, re_at : re_at + FP].astype(f32)
            im = spec[:CB, im_at : im_at + FP].astype(f32)
            for g in range(group):
                c, s = cosines[g : g + 1, :], sines[g : g + 1, :]
                turned[g * CB : (g + 1) * CB, re_at : re_at + FP] = (re * c + im * s).astype(bf16)
                turned[g * CB : (g + 1) * CB, im_at : im_at + FP] = (im * c - re * s).astype(bf16)
        totals[slot] = lax.dot_general(
            turned[...], spec[...], (((1,), (1,)), ((), ())), preferred_element_type=f32
        )

    def write(step, slot):
        start = pl.multiple_of(step * group, group)
        for pair in range(group // 2):
            low, high = 2 * pair * CB, (2 * pair + 1) * CB
            lanes = pl.ds(pl.multiple_of(start * CB + pair * 2 * CB, 2 * CB), 2 * CB)
            for k in range(BAND + 1):
                both = jnp.concatenate(
                    [totals[slot, at : at + CB, k * CB : (k + 1) * CB] for at in (low, high)], axis=1
                )
                keep = own_seg == pseg_ref[k : k + 1, :]
                out_ref[k, :, lanes] = jnp.where(keep, both, 0.0).astype(bf16)
        sources = jnp.concatenate(
            [totals[slot, g * CB : (g + 1) * CB, ROWS : ROWS + count] for g in range(group)], axis=1
        )
        src_ref[:, pl.ds(pl.multiple_of(start * count, group * count), group * count)] = sources.astype(bf16)

    multiply(0, 0)

    @pl.loop(1, steps)
    def _(step):
        write(step - 1, (step - 1) % 2)
        multiply(step, step % 2)

    write(steps - 1, (steps - 1) % 2)


VMEM = pl.BlockSpec(memory_space=pltpu.VMEM)
SMEM = pl.BlockSpec(memory_space=pltpu.SMEM)
HBM = pl.BlockSpec(memory_space=pltpu.HBM)


def call(kernel, shapes, scratch, specs, **kwargs):
    return pl.pallas_call(
        kernel, out_shape=shapes, in_specs=specs, out_specs=jax.tree.map(lambda _: VMEM, shapes), scratch_shapes=scratch, **kwargs
    )


def per_device(records, filter_taps, segment_ids):
    count = lax.axis_size("fibre")
    device = lax.axis_index("fibre")

    def ahead(value, distance):
        return lax.ppermute(value, "fibre", [(i, (i - distance) % count) for i in range(count)])

    def swap(value):
        return lax.ppermute(value, "fibre", [(i, i ^ 1) for i in range(count)])

    index = device.reshape(1)
    few = count <= 16
    stay = functools.partial(pltpu.with_memory_space_constraint, memory_space=pltpu.HBM)

    edge = call(
        edge_kernel,
        jax.ShapeDtypeStruct((2 * HALO, W * L), bf16),
        [pltpu.SemaphoreType.DMA((2,))],
        [HBM],
        compiler_params=pltpu.CompilerParams(vmem_limit_bytes=EDGE_LIMIT),
    )(stay(records))
    route = [(i, (i + 1) % count if i % 2 else (i - BAND - 1) % count) for i in range(count)]
    halo = lax.ppermute(edge, "fibre", route)
    sown = swap(records)
    four = ahead(records, 4)
    two = ahead(records, 2)

    source, band, segs, pseg = call(
        prep_kernel,
        (
            jax.ShapeDtypeStruct((SLOT, CHUNK), bf16),
            jax.ShapeDtypeStruct((SPAN * CHUNK, 2 * CHUNK), bf16),
            jax.ShapeDtypeStruct((ROWS + 2 * HALO, CHUNK), f32),
            jax.ShapeDtypeStruct((8, CHUNK), f32),
        ),
        [
            pltpu.VMEM(filter_taps.shape, bf16),
            pltpu.VMEM((1,) + segment_ids.shape, jnp.int32),
            pltpu.VMEM((SLOT, SPAN * CHUNK), f32),
            pltpu.SemaphoreType.DMA((2,)),
        ],
        [SMEM] + [VMEM] * 3 + [HBM] * 2,
        compiler_params=pltpu.CompilerParams(vmem_limit_bytes=PREP_LIMIT if few else None),
    )(index, edge, halo, sown, stay(filter_taps), stay(segment_ids.reshape(1, -1)))
    tables = (records, dft_table(), lag_tables())
    own, dft, lags = call(
        table_kernel,
        tuple(jax.ShapeDtypeStruct(table.shape, table.dtype) for table in tables),
        [pltpu.SemaphoreType.DMA((len(tables),))],
        [HBM] * len(tables),
        compiler_params=pltpu.CompilerParams(vmem_limit_bytes=TABLE_LIMIT),
    )(*map(stay, tables))

    lists = count // 2
    first = BAND // 2 + 1 if lists <= 8 else 1
    parts = [ahead(source, 2 * s) for s in range(first, min(8, lists))]
    have = 8
    if have < lists:
        known = jnp.concatenate([source] + parts, axis=0)
    while have < lists:
        more = []
        for s in range(1, 8):
            left = lists - s * have
            if left > 0:
                more.append(ahead(known[: SLOT * left], 2 * s * have))
        parts += more
        known = jnp.concatenate([known] + more, axis=0)
        have = known.shape[0] // SLOT
    swapped = [swap(part) for part in [source] + parts]
    sfour, stwo = swap(four), swap(two)

    group = 8
    stacked, source_out = call(
        functools.partial(main_kernel, len(parts), count),
        (
            jax.ShapeDtypeStruct((BAND + 1, CB, LAGS * CB), bf16),
            jax.ShapeDtypeStruct((CB, LAGS * count), bf16),
        ),
        [
            pltpu.VMEM((NCHUNK, ROWS + 2 * HALO, CHUNK), f32),
            pltpu.VMEM((2, NCHUNK * CB, SPAN * CHUNK), bf16),
            pltpu.VMEM((NCHUNK, ROWS + count, CHUNK), bf16),
            pltpu.VMEM((ROWS + count, KP), bf16),
            pltpu.VMEM((group * CB, KP), bf16),
            pltpu.VMEM((2, group * CB, ROWS + count), f32),
            pltpu.VMEM((SLOT, SPAN * CHUNK), f32),
        ],
        [SMEM] + [VMEM] * (13 + 2 * len(parts)),
        compiler_params=pltpu.CompilerParams(vmem_limit_bytes=VMEM_LIMIT if few else None),
    )(
        index, own, two, four, sown, stwo, sfour, halo, *parts, *swapped, segs, pseg, band, dft, lags,
    )
    return (jnp.swapaxes(stacked, 0, 1), source_out)


def solution(mesh):
    return jax.shard_map(
        per_device,
        mesh=mesh,
        in_specs=(P(("runs", "fibre"), None), P(), P("runs")),
        out_specs=(P(("runs", "fibre"), None, None), P(("runs", "fibre"), None)),
        check_vma=False,
    )
```

```python
import functools

import jax
import jax.numpy as jnp
import numpy as np
from jax import lax
from jax.experimental import pallas as pl
from jax.experimental.pallas import tpu as pltpu
from jax.sharding import PartitionSpec as P


CB = 64
W = 4
F = 200
L = 400
TAPS = 63
SPAN = 9
LAGS = 32
BAND = 4
HALF = (SPAN - 1) // 2
SLOT = 16
HALO = 8
CHUNK = 128
NCHUNK = -(-W * L // CHUNK)
FP = 256
KP = W * 2 * FP
ROWS = (BAND + 1) * CB
SHIFT = L % CHUNK
COVER = 4 * CHUNK

VMEM_LIMIT = 28 << 20
PREP_LIMIT = 12 << 20
EDGE_LIMIT = 1 << 20
TABLE_LIMIT = 2 << 20

f32 = jnp.float32
bf16 = jnp.bfloat16


def dft_table():
    t = np.arange(L)
    taper = 0.5 - 0.5 * np.cos((t + 0.5) * (2.0 * np.pi / L))
    phase = (t[:, None] * np.arange(F)[None, :] % L) * (2.0 * np.pi / L)
    lead = (W - 1) * SHIFT
    table = np.zeros((lead + COVER, 2 * FP))
    table[lead : lead + L, :F] = taper[:, None] * np.cos(phase)
    table[lead : lead + L, FP : FP + F] = -taper[:, None] * np.sin(phase)
    return jnp.asarray(table.astype(np.float32), bf16)


def lag_tables():
    m = np.arange(LAGS) - LAGS // 2
    phase = (m[:, None] * np.arange(F)[None, :] % L) * (2.0 * np.pi / L)
    scale = 1.0 / np.sqrt(2.0 * L)
    tables = np.zeros((2, LAGS, FP))
    tables[0, :, :F] = np.cos(phase) * scale
    tables[1, :, :F] = -np.sin(phase) * scale
    return jnp.asarray(tables.astype(np.float32), bf16).astype(f32)


def start_loads(pairs, sems):
    loads = [pltpu.make_async_copy(source, target, sems.at[i]) for i, (source, target) in enumerate(pairs)]
    for load in loads:
        load.start()
    return loads


def edge_kernel(own_hbm, edge_ref, sems):
    last = (own_hbm.at[pl.ds(CB - HALO, HALO)], edge_ref.at[pl.ds(0, HALO)])
    first = (own_hbm.at[pl.ds(0, HALO)], edge_ref.at[pl.ds(HALO, HALO)])
    for load in start_loads((last, first), sems):
        load.wait()


def chunk(rows, j):
    piece = rows[:, j * CHUNK : min((j + 1) * CHUNK, W * L)]
    if piece.shape[1] < CHUNK:
        piece = jnp.concatenate([piece, jnp.zeros((piece.shape[0], CHUNK - piece.shape[1]), piece.dtype)], axis=1)
    return piece


def filter_row(row_at, seg_ref, centre, line, band_ref):
    own = seg_ref[centre : centre + 1, :]
    line[...] = jnp.zeros_like(line)
    for e in range(SPAN):
        at = centre - HALF + e
        keep = seg_ref[at : at + 1, :] == own
        for j in range(NCHUNK):
            line[j : j + 1, e * CHUNK : (e + 1) * CHUNK] = jnp.where(keep, row_at(e, j), 0.0)
    share = jnp.dot(line[...].astype(bf16), band_ref[...], preferred_element_type=f32)
    before = jnp.concatenate([jnp.zeros((1, CHUNK), f32), share[:-1, CHUNK:]], axis=0)
    return share[:, :CHUNK] + before


def prep_kernel(
    index_ref, edge_ref, halo_ref, sown_ref, taps_hbm, ids_hbm, own_hbm, dft_hbm, lag_hbm,
    source_ref, band_ref, seg_ref, own_ref, dft_ref, lag_ref, taps_ref, ids_ref, line, sems,
):
    loads = start_loads(
        ((taps_hbm, taps_ref), (ids_hbm, ids_ref), (own_hbm, own_ref), (dft_hbm, dft_ref), (lag_hbm, lag_ref)), sems
    )
    device = index_ref[0]
    total = ids_ref.shape[1]
    loads[0].wait()
    wide = jnp.concatenate([taps_ref[...].astype(f32), jnp.zeros((SPAN, 2 * CHUNK - TAPS), f32)], axis=1)
    for e in range(SPAN):
        row = jnp.broadcast_to(wide[e : e + 1, :], (CHUNK, 2 * CHUNK))
        band_ref[e * CHUNK : (e + 1) * CHUNK, :] = pltpu.roll(row, 0, 1, stride=1, stride_axis=0).astype(bf16)

    loads[1].wait()
    ids = jnp.broadcast_to(ids_ref[...].astype(bf16), (CHUNK, total))
    channels = device * CB - HALO + lax.broadcasted_iota(jnp.int32, (ROWS + 2 * HALO, 1), 0)
    channels = jnp.where(channels < 0, channels + total, channels)
    channels = jnp.where(channels >= total, channels - total, channels)
    hit = lax.broadcasted_iota(jnp.int32, (ROWS + 2 * HALO, total), 1) == channels
    seg_ref[...] = lax.dot_general(
        jnp.where(hit, 1.0, 0.0).astype(bf16), ids, (((1,), (1,)), ((), ())), preferred_element_type=f32
    )

    even = device % 2 == 0
    behind = jnp.where(even, halo_ref[:HALO].astype(f32), sown_ref[CB - HALO :].astype(f32))
    first = edge_ref[HALO:].astype(f32)

    def row_at(e, j):
        rows, at = (behind, HALO - HALF + e) if e < HALF else (first, e - HALF)
        return chunk(rows, j)[at : at + 1]

    source_ref[...] = filter_row(row_at, seg_ref, HALO, line, band_ref).astype(bf16)
    for load in loads[2:]:
        load.wait()


def partner_kernel(count, index_ref, seg_ref, pseg_ref):
    for k in range(BAND + 1):
        block = seg_ref[HALO + k * CB : HALO + (k + 1) * CB, :]
        turned = jnp.transpose(jnp.concatenate([block, block], axis=0))
        pseg_ref[k : k + 1, :] = jnp.where(index_ref[0] + k < count, turned[:1], -1.0)
    pseg_ref[BAND + 1 :, :] = jnp.full((8 - BAND - 1, CHUNK), -1.0, f32)


def main_kernel(pieces, count, *refs):
    index_ref, own_ref, two_ref, four_ref, sown_ref, stwo_ref, sfour_ref, halo_ref = refs[:8]
    part_refs, refs = refs[8 : 8 + pieces], refs[8 + pieces :]
    seg_ref, pseg_ref, band_ref, dft_ref, lag_ref, out_ref, src_ref = refs[:7]
    rec, masked, filt, spec, turned, totals, line = refs[7:]
    even = index_ref[0] % 2 == 0

    def put(start, rows):
        for j in range(NCHUNK):
            rec[j, start : start + rows.shape[0], :] = chunk(rows, j)

    stwo, sfour = stwo_ref[...].astype(f32), sfour_ref[...].astype(f32)
    sown, halo = sown_ref[...].astype(f32), halo_ref[...].astype(f32)
    put(0, jnp.where(even, halo[:HALO], sown[CB - HALO :]))
    put(HALO, own_ref[...].astype(f32))
    put(HALO + CB, jnp.where(even, sown, stwo))
    put(HALO + 2 * CB, two_ref[...].astype(f32))
    put(HALO + 3 * CB, jnp.where(even, stwo, sfour))
    put(HALO + 4 * CB, four_ref[...].astype(f32))
    put(HALO + ROWS, jnp.where(even, sfour[:HALO], halo[HALO:]))

    def filtered(inputs, rows, start):
        share = jnp.dot(inputs[...], band_ref[...], preferred_element_type=f32)
        for j in range(NCHUNK):
            result = share[j * rows : (j + 1) * rows, :CHUNK]
            if j:
                result = result + share[(j - 1) * rows : j * rows, CHUNK:]
            filt[j, pl.ds(start, rows), :] = result.astype(bf16)

    for k in range(BAND + 1):
        base = k * CB
        held = masked.at[k % 2]
        centre = seg_ref[pl.ds(base + HALO, CB), :]
        for e in range(SPAN):
            first = base + (HALO - HALF + e)
            keep = seg_ref[pl.ds(first, CB), :] == centre
            for j in range(NCHUNK):
                rows = rec[j, pl.ds(first, CB), :]
                held[j * CB : (j + 1) * CB, e * CHUNK : (e + 1) * CHUNK] = jnp.where(keep, rows, 0.0).astype(bf16)
        filtered(held, CB, base)

    rows = []
    for ref in part_refs:
        value = ref[...].astype(f32)
        rows += [value[at : at + SLOT] for at in range(0, value.shape[0], SLOT)]
    mine, theirs = rows[::2], rows[1::2]
    lists = count // 2
    skip = lists - len(mine)
    mine, theirs = ([part[0]] + [None] * skip + part[1:] for part in (mine, theirs))

    def next_row(e, j):
        at = HALO + ROWS - HALF + e
        return rec[j, at : at + 1, :]

    for r in range(count):
        if r <= BAND:
            rows = [filt[j, r * CB : r * CB + 1, :] for j in range(NCHUNK)]
        else:
            if r == BAND + 1:
                value = filter_row(next_row, seg_ref, HALO + ROWS, line, band_ref)
            elif r % 2 == 0:
                value = mine[r // 2]
            else:
                value = jnp.where(even, theirs[r // 2], theirs[(r // 2 + 1) % lists])
            rows = [value[j : j + 1].astype(bf16) for j in range(NCHUNK)]
        for j in range(NCHUNK):
            filt[j, ROWS + r : ROWS + r + 1, :] = rows[j]

    for w in range(W):
        first = w * (L // CHUNK)
        lhs = jnp.concatenate([filt[first + q] for q in range(COVER // CHUNK)], axis=1)
        lead = (W - 1 - w) * SHIFT
        raw = jnp.dot(lhs, dft_ref[lead : lead + COVER, :], preferred_element_type=f32)
        power = jnp.sum(raw * raw, axis=-1, keepdims=True) * (1.0 / L)
        spec[:, w * 2 * FP : (w + 1) * 2 * FP] = (raw * lax.rsqrt(power + 1e-06)).astype(bf16)

    row = lax.broadcasted_iota(jnp.int32, (count, count), 0)
    column = lax.broadcasted_iota(jnp.int32, (count, count), 1)
    ahead = row - index_ref[0]
    ahead = jnp.where(ahead < 0, ahead + count, ahead)
    order = jnp.where(ahead == column, 1.0, 0.0).astype(bf16)
    spec[ROWS:, :] = jnp.dot(order, spec[ROWS:, :], preferred_element_type=f32).astype(bf16)

    group = turned.shape[0] // CB
    steps = LAGS // group
    own_seg = seg_ref[HALO : HALO + CB, :]

    def multiply(step, slot):
        start = pl.multiple_of(step * group, group)
        cosines = lag_ref[0, pl.ds(start, group), :]
        sines = lag_ref[1, pl.ds(start, group), :]
        for w in range(W):
            re_at, im_at = w * 2 * FP, w * 2 * FP + FP
            re = spec[:CB, re_at : re_at + FP].astype(f32)
            im = spec[:CB, im_at : im_at + FP].astype(f32)
            for g in range(group):
                c, s = cosines[g : g + 1, :], sines[g : g + 1, :]
                turned[g * CB : (g + 1) * CB, re_at : re_at + FP] = (re * c + im * s).astype(bf16)
                turned[g * CB : (g + 1) * CB, im_at : im_at + FP] = (im * c - re * s).astype(bf16)
        totals[slot] = lax.dot_general(
            turned[...], spec[...], (((1,), (1,)), ((), ())), preferred_element_type=f32
        )

    def write(step, slot):
        start = pl.multiple_of(step * group, group)
        for pair in range(group // 2):
            low, high = 2 * pair * CB, (2 * pair + 1) * CB
            lanes = pl.ds(pl.multiple_of(start * CB + pair * 2 * CB, 2 * CB), 2 * CB)
            for k in range(BAND + 1):
                both = jnp.concatenate(
                    [totals[slot, at : at + CB, k * CB : (k + 1) * CB] for at in (low, high)], axis=1
                )
                keep = own_seg == pseg_ref[k : k + 1, :]
                out_ref[k, :, lanes] = jnp.where(keep, both, 0.0).astype(bf16)
        sources = jnp.concatenate(
            [totals[slot, g * CB : (g + 1) * CB, ROWS : ROWS + count] for g in range(group)], axis=1
        )
        src_ref[:, pl.ds(pl.multiple_of(start * count, group * count), group * count)] = sources.astype(bf16)

    multiply(0, 0)

    @pl.loop(1, steps)
    def _(step):
        write(step - 1, (step - 1) % 2)
        multiply(step, step % 2)

    write(steps - 1, (steps - 1) % 2)


VMEM = pl.BlockSpec(memory_space=pltpu.VMEM)
SMEM = pl.BlockSpec(memory_space=pltpu.SMEM)
HBM = pl.BlockSpec(memory_space=pltpu.HBM)


def call(kernel, shapes, scratch, specs, **kwargs):
    return pl.pallas_call(
        kernel, out_shape=shapes, in_specs=specs, out_specs=jax.tree.map(lambda _: VMEM, shapes), scratch_shapes=scratch, **kwargs
    )


def per_device(records, filter_taps, segment_ids):
    count = lax.axis_size("fibre")
    device = lax.axis_index("fibre")

    def ahead(value, distance):
        return lax.ppermute(value, "fibre", [(i, (i - distance) % count) for i in range(count)])

    def swap(value):
        return lax.ppermute(value, "fibre", [(i, i ^ 1) for i in range(count)])

    index = device.reshape(1)
    few = count <= 16
    stay = functools.partial(pltpu.with_memory_space_constraint, memory_space=pltpu.HBM)

    edge = call(
        edge_kernel,
        jax.ShapeDtypeStruct((2 * HALO, W * L), bf16),
        [pltpu.SemaphoreType.DMA((2,))],
        [HBM],
        compiler_params=pltpu.CompilerParams(vmem_limit_bytes=EDGE_LIMIT),
    )(stay(records))
    route = [(i, (i + 1) % count if i % 2 else (i - BAND - 1) % count) for i in range(count)]
    halo = lax.ppermute(edge, "fibre", route)
    sown = swap(records)
    four = ahead(records, 4)
    two = ahead(records, 2)

    dft, lags = dft_table(), lag_tables()
    source, band, segs, own, dft, lags = call(
        prep_kernel,
        (
            jax.ShapeDtypeStruct((SLOT, CHUNK), bf16),
            jax.ShapeDtypeStruct((SPAN * CHUNK, 2 * CHUNK), bf16),
            jax.ShapeDtypeStruct((ROWS + 2 * HALO, CHUNK), f32),
            jax.ShapeDtypeStruct(records.shape, bf16),
            jax.ShapeDtypeStruct(dft.shape, bf16),
            jax.ShapeDtypeStruct(lags.shape, f32),
        ),
        [
            pltpu.VMEM(filter_taps.shape, bf16),
            pltpu.VMEM((1,) + segment_ids.shape, jnp.int32),
            pltpu.VMEM((SLOT, SPAN * CHUNK), f32),
            pltpu.SemaphoreType.DMA((5,)),
        ],
        [SMEM] + [VMEM] * 3 + [HBM] * 5,
        compiler_params=pltpu.CompilerParams(vmem_limit_bytes=PREP_LIMIT if few else None),
    )(
        index, edge, halo, sown, stay(filter_taps), stay(segment_ids.reshape(1, -1)), stay(records), stay(dft),
        stay(lags),
    )

    lists = count // 2
    pair = jnp.concatenate([source, swap(source)], axis=0)
    first = BAND // 2 + 1 if lists <= 8 else 1
    parts = [pair] + [ahead(pair, 2 * s) for s in range(first, min(8, lists))]
    have = 8
    while have < lists:
        known = jnp.concatenate(parts, axis=0)
        for s in range(1, 8):
            left = lists - s * have
            if left > 0:
                parts.append(ahead(known[: 2 * SLOT * left], 2 * s * have))
        have = min(8 * have, lists)
    pseg = call(
        functools.partial(partner_kernel, count), jax.ShapeDtypeStruct((8, CHUNK), f32), (), [SMEM, VMEM],
        compiler_params=pltpu.CompilerParams(vmem_limit_bytes=TABLE_LIMIT),
    )(index, segs)
    sfour, stwo = swap(four), swap(two)

    group = 8
    stacked, source_out = call(
        functools.partial(main_kernel, len(parts), count),
        (
            jax.ShapeDtypeStruct((BAND + 1, CB, LAGS * CB), bf16),
            jax.ShapeDtypeStruct((CB, LAGS * count), bf16),
        ),
        [
            pltpu.VMEM((NCHUNK, ROWS + 2 * HALO, CHUNK), f32),
            pltpu.VMEM((2, NCHUNK * CB, SPAN * CHUNK), bf16),
            pltpu.VMEM((NCHUNK, ROWS + count, CHUNK), bf16),
            pltpu.VMEM((ROWS + count, KP), bf16),
            pltpu.VMEM((group * CB, KP), bf16),
            pltpu.VMEM((2, group * CB, ROWS + count), f32),
            pltpu.VMEM((SLOT, SPAN * CHUNK), f32),
        ],
        [SMEM] + [VMEM] * (12 + len(parts)),
        compiler_params=pltpu.CompilerParams(vmem_limit_bytes=VMEM_LIMIT if few else None),
    )(
        index, own, two, four, sown, stwo, sfour, halo, *parts, segs, pseg, band, dft, lags,
    )
    return (jnp.swapaxes(stacked, 0, 1), source_out)


def solution(mesh):
    return jax.shard_map(
        per_device,
        mesh=mesh,
        in_specs=(P(("runs", "fibre"), None), P(), P("runs")),
        out_specs=(P(("runs", "fibre"), None, None), P(("runs", "fibre"), None)),
        check_vma=False,
    )
```

```python
import functools

import jax
import jax.numpy as jnp
import numpy as np
from jax import lax
from jax.experimental import pallas as pl
from jax.experimental.pallas import tpu as pltpu
from jax.sharding import PartitionSpec as P


CB = 64
W = 4
F = 200
L = 400
TAPS = 63
SPAN = 9
LAGS = 32
BAND = 4
HALF = (SPAN - 1) // 2
SLOT = 16
HALO = 8
CHUNK = 128
NCHUNK = -(-W * L // CHUNK)
KP = -(-W * L // CHUNK) * CHUNK
ROWS = (BAND + 1) * CB
SHIFT = L % CHUNK
COVER = 4 * CHUNK

VMEM_LIMIT = 28 << 20
PREP_LIMIT = 12 << 20
EDGE_LIMIT = 1 << 20
TABLE_LIMIT = 2 << 20

f32 = jnp.float32
bf16 = jnp.bfloat16


def dft_tables():
    t = np.arange(L)
    taper = 0.5 - 0.5 * np.cos((t + 0.5) * (2.0 * np.pi / L))
    phase = (t[:, None] * np.arange(F)[None, :] % L) * (2.0 * np.pi / L)
    table = np.concatenate([taper[:, None] * np.cos(phase), -taper[:, None] * np.sin(phase)], axis=1)
    tables = np.zeros((W, COVER, COVER))
    for w in range(W):
        tables[w, w * SHIFT : w * SHIFT + L, w * SHIFT : w * SHIFT + L] = table
    return jnp.asarray(tables.astype(np.float32), bf16)


def lag_tables():
    m = np.arange(LAGS) - LAGS // 2
    phase = (m[:, None] * np.arange(F)[None, :] % L) * (2.0 * np.pi / L)
    scale = 1.0 / np.sqrt(2.0 * L)
    straight, crossed = np.cos(phase) * scale, -np.sin(phase) * scale
    tables = np.zeros((2, LAGS, KP))
    tables[0, :, : W * L] = np.tile(np.concatenate([straight, straight], axis=1), (1, W))
    tables[1, :, : W * L] = np.tile(np.concatenate([crossed, -crossed], axis=1), (1, W))
    return jnp.asarray(tables.astype(np.float32), bf16).astype(f32)


def start_loads(pairs, sems):
    loads = [pltpu.make_async_copy(source, target, sems.at[i]) for i, (source, target) in enumerate(pairs)]
    for load in loads:
        load.start()
    return loads


def edge_kernel(own_hbm, edge_ref, sems):
    last = (own_hbm.at[pl.ds(CB - HALO, HALO)], edge_ref.at[pl.ds(0, HALO)])
    first = (own_hbm.at[pl.ds(0, HALO)], edge_ref.at[pl.ds(HALO, HALO)])
    for load in start_loads((last, first), sems):
        load.wait()


def chunk(rows, j):
    piece = rows[:, j * CHUNK : min((j + 1) * CHUNK, W * L)]
    if piece.shape[1] < CHUNK:
        piece = jnp.concatenate([piece, jnp.zeros((piece.shape[0], CHUNK - piece.shape[1]), piece.dtype)], axis=1)
    return piece


def filter_row(row_at, seg_ref, centre, line, band_ref):
    own = seg_ref[centre : centre + 1, :]
    line[...] = jnp.zeros_like(line)
    for e in range(SPAN):
        at = centre - HALF + e
        keep = seg_ref[at : at + 1, :] == own
        for j in range(NCHUNK):
            line[j : j + 1, e * CHUNK : (e + 1) * CHUNK] = jnp.where(keep, row_at(e, j), 0.0)
    share = jnp.dot(line[...].astype(bf16), band_ref[...], preferred_element_type=f32)
    before = jnp.concatenate([jnp.zeros((1, CHUNK), f32), share[:-1, CHUNK:]], axis=0)
    return share[:, :CHUNK] + before


def prep_kernel(
    index_ref, edge_ref, halo_ref, sown_ref, taps_hbm, ids_hbm, own_hbm, dft_hbm, lag_hbm,
    source_ref, band_ref, seg_ref, own_ref, dft_ref, lag_ref, taps_ref, ids_ref, line, sems,
):
    loads = start_loads(
        ((taps_hbm, taps_ref), (ids_hbm, ids_ref), (own_hbm, own_ref), (dft_hbm, dft_ref), (lag_hbm, lag_ref)), sems
    )
    device = index_ref[0]
    total = ids_ref.shape[1]
    loads[0].wait()
    wide = jnp.concatenate([taps_ref[...].astype(f32), jnp.zeros((SPAN, 2 * CHUNK - TAPS), f32)], axis=1)
    for e in range(SPAN):
        row = jnp.broadcast_to(wide[e : e + 1, :], (CHUNK, 2 * CHUNK))
        band_ref[e * CHUNK : (e + 1) * CHUNK, :] = pltpu.roll(row, 0, 1, stride=1, stride_axis=0).astype(bf16)

    loads[1].wait()
    ids = jnp.broadcast_to(ids_ref[...].astype(bf16), (CHUNK, total))
    channels = device * CB - HALO + lax.broadcasted_iota(jnp.int32, (ROWS + 2 * HALO, 1), 0)
    channels = jnp.where(channels < 0, channels + total, channels)
    channels = jnp.where(channels >= total, channels - total, channels)
    hit = lax.broadcasted_iota(jnp.int32, (ROWS + 2 * HALO, total), 1) == channels
    seg_ref[...] = lax.dot_general(
        jnp.where(hit, 1.0, 0.0).astype(bf16), ids, (((1,), (1,)), ((), ())), preferred_element_type=f32
    )

    even = device % 2 == 0
    behind = jnp.where(even, halo_ref[:HALO].astype(f32), sown_ref[CB - HALO :].astype(f32))
    first = edge_ref[HALO:].astype(f32)

    def row_at(e, j):
        rows, at = (behind, HALO - HALF + e) if e < HALF else (first, e - HALF)
        return chunk(rows, j)[at : at + 1]

    source_ref[...] = filter_row(row_at, seg_ref, HALO, line, band_ref).astype(bf16)
    for load in loads[2:]:
        load.wait()


def partner_kernel(count, index_ref, seg_ref, pseg_ref):
    for k in range(BAND + 1):
        block = seg_ref[HALO + k * CB : HALO + (k + 1) * CB, :]
        turned = jnp.transpose(jnp.concatenate([block, block], axis=0))
        pseg_ref[k : k + 1, :] = jnp.where(index_ref[0] + k < count, turned[:1], -1.0)
    pseg_ref[BAND + 1 :, :] = jnp.full((8 - BAND - 1, CHUNK), -1.0, f32)


def main_kernel(pieces, count, *refs):
    index_ref, own_ref, two_ref, four_ref, sown_ref, stwo_ref, sfour_ref, halo_ref = refs[:8]
    part_refs, refs = refs[8 : 8 + pieces], refs[8 + pieces :]
    seg_ref, pseg_ref, band_ref, dft_ref, lag_ref, out_ref, src_ref = refs[:7]
    rec, masked, filt, spec, turned, totals, line, swapped = refs[7:]
    even = index_ref[0] % 2 == 0

    def put(start, rows):
        for j in range(NCHUNK):
            rec[j, start : start + rows.shape[0], :] = chunk(rows, j)

    stwo, sfour = stwo_ref[...].astype(f32), sfour_ref[...].astype(f32)
    sown, halo = sown_ref[...].astype(f32), halo_ref[...].astype(f32)
    put(0, jnp.where(even, halo[:HALO], sown[CB - HALO :]))
    put(HALO, own_ref[...].astype(f32))
    put(HALO + CB, jnp.where(even, sown, stwo))
    put(HALO + 2 * CB, two_ref[...].astype(f32))
    put(HALO + 3 * CB, jnp.where(even, stwo, sfour))
    put(HALO + 4 * CB, four_ref[...].astype(f32))
    put(HALO + ROWS, jnp.where(even, sfour[:HALO], halo[HALO:]))

    def filtered(inputs, rows, start):
        share = jnp.dot(inputs[...], band_ref[...], preferred_element_type=f32)
        for j in range(NCHUNK):
            result = share[j * rows : (j + 1) * rows, :CHUNK]
            if j:
                result = result + share[(j - 1) * rows : j * rows, CHUNK:]
            filt[j, pl.ds(start, rows), :] = result.astype(bf16)

    for k in range(BAND + 1):
        base = k * CB
        held = masked.at[k % 2]
        centre = seg_ref[pl.ds(base + HALO, CB), :]
        for e in range(SPAN):
            first = base + (HALO - HALF + e)
            keep = jnp.where(seg_ref[pl.ds(first, CB), :] == centre, 1.0, 0.0)
            for j in range(NCHUNK):
                rows = rec[j, pl.ds(first, CB), :]
                held[j * CB : (j + 1) * CB, e * CHUNK : (e + 1) * CHUNK] = (rows * keep).astype(bf16)
        filtered(held, CB, base)

    rows = []
    for ref in part_refs:
        value = ref[...].astype(f32)
        rows += [value[at : at + SLOT] for at in range(0, value.shape[0], SLOT)]
    mine, theirs = rows[::2], rows[1::2]
    lists = count // 2
    skip = lists - len(mine)
    mine, theirs = ([part[0]] + [None] * skip + part[1:] for part in (mine, theirs))

    def next_row(e, j):
        at = HALO + ROWS - HALF + e
        return rec[j, at : at + 1, :]

    for r in range(count):
        if r <= BAND:
            rows = [filt[j, r * CB : r * CB + 1, :] for j in range(NCHUNK)]
        else:
            if r == BAND + 1:
                value = filter_row(next_row, seg_ref, HALO + ROWS, line, band_ref)
            elif r % 2 == 0:
                value = mine[r // 2]
            else:
                value = jnp.where(even, theirs[r // 2], theirs[(r // 2 + 1) % lists])
            rows = [value[j : j + 1].astype(bf16) for j in range(NCHUNK)]
        for j in range(NCHUNK):
            filt[j, ROWS + r : ROWS + r + 1, :] = rows[j]

    tiles = COVER // CHUNK - 1
    tail = None
    for w in range(W):
        lhs = jnp.concatenate([filt[w * tiles + q] for q in range(tiles + 1)], axis=1)
        raw = jnp.dot(lhs, dft_ref[w], preferred_element_type=f32)
        power = jnp.sum(raw * raw, axis=-1, keepdims=True) * (1.0 / L)
        whitened = raw * lax.rsqrt(power + 1e-06)
        head = whitened[:, :CHUNK] if tail is None else tail + whitened[:, :CHUNK]
        spec[:, w * tiles * CHUNK : (w * tiles + 1) * CHUNK] = head.astype(bf16)
        spec[:, (w * tiles + 1) * CHUNK : (w + 1) * tiles * CHUNK] = whitened[:, CHUNK : tiles * CHUNK].astype(bf16)
        tail = whitened[:, tiles * CHUNK :]
    spec[:, W * tiles * CHUNK :] = tail.astype(bf16)

    row = lax.broadcasted_iota(jnp.int32, (count, count), 0)
    column = lax.broadcasted_iota(jnp.int32, (count, count), 1)
    ahead = row - index_ref[0]
    ahead = jnp.where(ahead < 0, ahead + count, ahead)
    order = jnp.where(ahead == column, 1.0, 0.0).astype(bf16)
    spec[ROWS:, :] = jnp.dot(order, spec[ROWS:, :], preferred_element_type=f32).astype(bf16)

    own = spec[:CB, :].astype(f32)
    pieces = []
    for w in range(W):
        pieces += [own[:, w * L + F : (w + 1) * L], own[:, w * L : w * L + F]]
    swapped[...] = jnp.concatenate(pieces + [jnp.zeros((CB, KP - W * L), f32)], axis=1)

    group = turned.shape[0] // CB
    steps = LAGS // group
    own_seg = seg_ref[HALO : HALO + CB, :]

    def multiply(step, slot):
        start = pl.multiple_of(step * group, group)
        for at in range(0, KP, CHUNK):
            lanes = slice(at, at + CHUNK)
            straight, crossed = lag_ref[0, pl.ds(start, group), lanes], lag_ref[1, pl.ds(start, group), lanes]
            own, other = spec[:CB, lanes].astype(f32), swapped[:, lanes]
            for g in range(group):
                turned[g * CB : (g + 1) * CB, lanes] = (
                    own * straight[g : g + 1, :] + other * crossed[g : g + 1, :]
                ).astype(bf16)
        totals[slot] = lax.dot_general(
            turned[...], spec[...], (((1,), (1,)), ((), ())), preferred_element_type=f32
        )

    def write(step, slot):
        start = pl.multiple_of(step * group, group)
        for pair in range(group // 2):
            low, high = 2 * pair * CB, (2 * pair + 1) * CB
            lanes = pl.ds(pl.multiple_of(start * CB + pair * 2 * CB, 2 * CB), 2 * CB)
            for k in range(BAND + 1):
                both = jnp.concatenate(
                    [totals[slot, at : at + CB, k * CB : (k + 1) * CB] for at in (low, high)], axis=1
                )
                keep = own_seg == pseg_ref[k : k + 1, :]
                out_ref[k, :, lanes] = jnp.where(keep, both, 0.0).astype(bf16)
        sources = jnp.concatenate(
            [totals[slot, g * CB : (g + 1) * CB, ROWS : ROWS + count] for g in range(group)], axis=1
        )
        src_ref[:, pl.ds(pl.multiple_of(start * count, group * count), group * count)] = sources.astype(bf16)

    multiply(0, 0)

    @pl.loop(1, steps)
    def _(step):
        write(step - 1, (step - 1) % 2)
        multiply(step, step % 2)

    write(steps - 1, (steps - 1) % 2)


VMEM = pl.BlockSpec(memory_space=pltpu.VMEM)
SMEM = pl.BlockSpec(memory_space=pltpu.SMEM)
HBM = pl.BlockSpec(memory_space=pltpu.HBM)


def call(kernel, shapes, scratch, specs, **kwargs):
    return pl.pallas_call(
        kernel, out_shape=shapes, in_specs=specs, out_specs=jax.tree.map(lambda _: VMEM, shapes), scratch_shapes=scratch, **kwargs
    )


def per_device(records, filter_taps, segment_ids):
    count = lax.axis_size("fibre")
    device = lax.axis_index("fibre")

    def ahead(value, distance):
        return lax.ppermute(value, "fibre", [(i, (i - distance) % count) for i in range(count)])

    def swap(value):
        return lax.ppermute(value, "fibre", [(i, i ^ 1) for i in range(count)])

    index = device.reshape(1)
    few = count <= 16
    stay = functools.partial(pltpu.with_memory_space_constraint, memory_space=pltpu.HBM)

    edge = call(
        edge_kernel,
        jax.ShapeDtypeStruct((2 * HALO, W * L), bf16),
        [pltpu.SemaphoreType.DMA((2,))],
        [HBM],
        compiler_params=pltpu.CompilerParams(vmem_limit_bytes=EDGE_LIMIT),
    )(stay(records))
    route = [(i, (i + 1) % count if i % 2 else (i - BAND - 1) % count) for i in range(count)]
    halo = lax.ppermute(edge, "fibre", route)
    sown = swap(records)
    four = ahead(records, 4)
    two = ahead(records, 2)

    dft, lags = dft_tables(), lag_tables()
    source, band, segs, own, dft, lags = call(
        prep_kernel,
        (
            jax.ShapeDtypeStruct((SLOT, CHUNK), bf16),
            jax.ShapeDtypeStruct((SPAN * CHUNK, 2 * CHUNK), bf16),
            jax.ShapeDtypeStruct((ROWS + 2 * HALO, CHUNK), f32),
            jax.ShapeDtypeStruct(records.shape, bf16),
            jax.ShapeDtypeStruct(dft.shape, bf16),
            jax.ShapeDtypeStruct(lags.shape, f32),
        ),
        [
            pltpu.VMEM(filter_taps.shape, bf16),
            pltpu.VMEM((1,) + segment_ids.shape, jnp.int32),
            pltpu.VMEM((SLOT, SPAN * CHUNK), f32),
            pltpu.SemaphoreType.DMA((5,)),
        ],
        [SMEM] + [VMEM] * 3 + [HBM] * 5,
        compiler_params=pltpu.CompilerParams(vmem_limit_bytes=PREP_LIMIT if few else None),
    )(
        index, edge, halo, sown, stay(filter_taps), stay(segment_ids.reshape(1, -1)), stay(records), stay(dft),
        stay(lags),
    )

    lists = count // 2
    pair = jnp.concatenate([source, swap(source)], axis=0)
    first = BAND // 2 + 1 if lists <= 8 else 1
    parts = [pair] + [ahead(pair, 2 * s) for s in range(first, min(8, lists))]
    have = 8
    while have < lists:
        known = jnp.concatenate(parts, axis=0)
        for s in range(1, 8):
            left = lists - s * have
            if left > 0:
                parts.append(ahead(known[: 2 * SLOT * left], 2 * s * have))
        have = min(8 * have, lists)
    pseg = call(
        functools.partial(partner_kernel, count), jax.ShapeDtypeStruct((8, CHUNK), f32), (), [SMEM, VMEM],
        compiler_params=pltpu.CompilerParams(vmem_limit_bytes=TABLE_LIMIT),
    )(index, segs)
    sfour, stwo = swap(four), swap(two)

    group = 8
    stacked, source_out = call(
        functools.partial(main_kernel, len(parts), count),
        (
            jax.ShapeDtypeStruct((BAND + 1, CB, LAGS * CB), bf16),
            jax.ShapeDtypeStruct((CB, LAGS * count), bf16),
        ),
        [
            pltpu.VMEM((NCHUNK, ROWS + 2 * HALO, CHUNK), f32),
            pltpu.VMEM((2, NCHUNK * CB, SPAN * CHUNK), bf16),
            pltpu.VMEM((NCHUNK, ROWS + count, CHUNK), bf16),
            pltpu.VMEM((ROWS + count, KP), bf16),
            pltpu.VMEM((group * CB, KP), bf16),
            pltpu.VMEM((2, group * CB, ROWS + count), f32),
            pltpu.VMEM((SLOT, SPAN * CHUNK), f32),
            pltpu.VMEM((CB, KP), f32),
        ],
        [SMEM] + [VMEM] * (12 + len(parts)),
        compiler_params=pltpu.CompilerParams(vmem_limit_bytes=VMEM_LIMIT if few else None),
    )(
        index, own, two, four, sown, stwo, sfour, halo, *parts, segs, pseg, band, dft, lags,
    )
    return (jnp.swapaxes(stacked, 0, 1), source_out)


def solution(mesh):
    return jax.shard_map(
        per_device,
        mesh=mesh,
        in_specs=(P(("runs", "fibre"), None), P(), P("runs")),
        out_specs=(P(("runs", "fibre"), None, None), P(("runs", "fibre"), None)),
        check_vma=False,
    )
```

```python
import functools

import jax
import jax.numpy as jnp
import numpy as np
from jax import lax
from jax.experimental import pallas as pl
from jax.experimental.pallas import tpu as pltpu
from jax.sharding import PartitionSpec as P


CB = 64
W = 4
F = 200
L = 400
TAPS = 63
SPAN = 9
LAGS = 32
BAND = 4
HALF = (SPAN - 1) // 2
SLOT = 16
HALO = 8
CHUNK = 128
NCHUNK = -(-W * L // CHUNK)
KP = -(-W * L // CHUNK) * CHUNK
ROWS = (BAND + 1) * CB
NEAR = BAND // 2 + 1
GROUP = 8
SHIFT = L % CHUNK
COVER = 4 * CHUNK

MAIN_LIMIT = 20 << 20
PREP_LIMIT = 12 << 20
EDGE_LIMIT = 1 << 20
TABLE_LIMIT = 2 << 20

f32 = jnp.float32
bf16 = jnp.bfloat16


def dft_tables():
    t = np.arange(L)
    taper = 0.5 - 0.5 * np.cos((t + 0.5) * (2.0 * np.pi / L))
    phase = (t[:, None] * np.arange(F)[None, :] % L) * (2.0 * np.pi / L)
    table = np.concatenate([taper[:, None] * np.cos(phase), -taper[:, None] * np.sin(phase)], axis=1)
    tables = np.zeros((W, COVER, COVER))
    for w in range(W):
        tables[w, w * SHIFT : w * SHIFT + L, w * SHIFT : w * SHIFT + L] = table
    return jnp.asarray(tables.astype(np.float32), bf16)


def lag_tables():
    m = np.arange(LAGS) - LAGS // 2
    phase = (m[:, None] * np.arange(F)[None, :] % L) * (2.0 * np.pi / L)
    scale = 1.0 / np.sqrt(2.0 * L)
    straight, crossed = np.cos(phase) * scale, -np.sin(phase) * scale
    tables = np.zeros((2, LAGS, KP))
    tables[0, :, : W * L] = np.tile(np.concatenate([straight, straight], axis=1), (1, W))
    tables[1, :, : W * L] = np.tile(np.concatenate([crossed, -crossed], axis=1), (1, W))
    return jnp.asarray(tables.astype(np.float32), bf16).astype(f32)


def start_loads(pairs, sems):
    loads = [pltpu.make_async_copy(source, target, sems.at[i]) for i, (source, target) in enumerate(pairs)]
    for load in loads:
        load.start()
    return loads


def edge_kernel(own_hbm, edge_ref, sems):
    last = (own_hbm.at[pl.ds(CB - HALO, HALO)], edge_ref.at[pl.ds(0, HALO)])
    first = (own_hbm.at[pl.ds(0, HALO)], edge_ref.at[pl.ds(HALO, HALO)])
    for load in start_loads((last, first), sems):
        load.wait()


def chunk(rows, j):
    piece = rows[:, j * CHUNK : min((j + 1) * CHUNK, W * L)]
    if piece.shape[1] < CHUNK:
        piece = jnp.concatenate([piece, jnp.zeros((piece.shape[0], CHUNK - piece.shape[1]), piece.dtype)], axis=1)
    return piece


def filter_rows(row_at, seg_ref, centres, line, band_ref):
    line[...] = jnp.zeros_like(line)
    for i, centre in enumerate(centres):
        own = seg_ref[centre : centre + 1, :]
        for e in range(SPAN):
            at = centre - HALF + e
            keep = jnp.where(seg_ref[at : at + 1, :] == own, 1.0, 0.0)
            for j in range(NCHUNK):
                line[i * SLOT + j : i * SLOT + j + 1, e * CHUNK : (e + 1) * CHUNK] = row_at(i, e, j) * keep
    share = jnp.dot(line[...].astype(bf16), band_ref[...], preferred_element_type=f32)
    results = []
    for i in range(len(centres)):
        part = share[i * SLOT : (i + 1) * SLOT]
        before = jnp.concatenate([jnp.zeros((1, CHUNK), f32), part[:-1, CHUNK:]], axis=0)
        results.append(part[:, :CHUNK] + before)
    return results


def prep_kernel(
    index_ref, edge_ref, halo_ref, sown_ref, taps_hbm, ids_hbm, own_hbm, dft_hbm, lag_hbm,
    source_ref, band_ref, seg_ref, own_ref, dft_ref, lag_ref, taps_ref, ids_ref, line, sems,
):
    loads = start_loads(
        ((taps_hbm, taps_ref), (ids_hbm, ids_ref), (own_hbm, own_ref), (dft_hbm, dft_ref), (lag_hbm, lag_ref)), sems
    )
    device = index_ref[0]
    total = ids_ref.shape[1]
    loads[0].wait()
    wide = jnp.concatenate([taps_ref[...].astype(f32), jnp.zeros((SPAN, 2 * CHUNK - TAPS), f32)], axis=1)
    for e in range(SPAN):
        row = jnp.broadcast_to(wide[e : e + 1, :], (CHUNK, 2 * CHUNK))
        band_ref[e * CHUNK : (e + 1) * CHUNK, :] = pltpu.roll(row, 0, 1, stride=1, stride_axis=0).astype(bf16)

    loads[1].wait()
    ids = jnp.broadcast_to(ids_ref[...].astype(bf16), (CHUNK, total))
    channels = device * CB - HALO + lax.broadcasted_iota(jnp.int32, (ROWS + 2 * HALO, 1), 0)
    channels = jnp.where(channels < 0, channels + total, channels)
    channels = jnp.where(channels >= total, channels - total, channels)
    hit = lax.broadcasted_iota(jnp.int32, (ROWS + 2 * HALO, total), 1) == channels
    seg_ref[...] = lax.dot_general(
        jnp.where(hit, 1.0, 0.0).astype(bf16), ids, (((1,), (1,)), ((), ())), preferred_element_type=f32
    )

    even = device % 2 == 0
    behind = jnp.where(even, halo_ref[:HALO].astype(f32), sown_ref[CB - HALO :].astype(f32))
    first = edge_ref[HALO:].astype(f32)

    def row_at(_, e, j):
        rows, at = (behind, HALO - HALF + e) if e < HALF else (first, e - HALF)
        return chunk(rows, j)[at : at + 1]

    source_ref[...] = filter_rows(row_at, seg_ref, (HALO,), line, band_ref)[0].astype(bf16)
    for load in loads[2:]:
        load.wait()


def partner_kernel(count, index_ref, seg_ref, pseg_ref):
    for k in range(BAND + 1):
        block = seg_ref[HALO + k * CB : HALO + (k + 1) * CB, :]
        turned = jnp.transpose(jnp.concatenate([block, block], axis=0))
        pseg_ref[k : k + 1, :] = jnp.where(index_ref[0] + k < count, turned[:1], -1.0)
    pseg_ref[BAND + 1 :, :] = jnp.full((8 - BAND - 1, CHUNK), -1.0, f32)


def spectra_kernel(pieces, count, *refs):
    index_ref, own_ref, two_ref, four_ref, sown_ref, stwo_ref, sfour_ref, halo_ref = refs[:8]
    part_refs, refs = refs[8 : 8 + pieces], refs[8 + pieces :]
    seg_ref, band_ref, dft_ref, spec, give_ref, rec, masked, filt, line = refs
    even = index_ref[0] % 2 == 0

    def put(start, rows):
        for j in range(NCHUNK):
            rec[j, start : start + rows.shape[0], :] = chunk(rows, j)

    stwo, sfour = stwo_ref[...].astype(f32), sfour_ref[...].astype(f32)
    sown, halo = sown_ref[...].astype(f32), halo_ref[...].astype(f32)
    put(0, jnp.where(even, halo[:HALO], sown[CB - HALO :]))
    put(HALO, own_ref[...].astype(f32))
    put(HALO + CB, jnp.where(even, sown[:HALO], stwo[:HALO]))
    put(2 * CB, jnp.where(even, sown[CB - HALO :], stwo[CB - HALO :]))
    put(HALO + 2 * CB, two_ref[...].astype(f32))
    put(HALO + 3 * CB, jnp.where(even, stwo[:HALO], sfour[:HALO]))
    put(4 * CB, jnp.where(even, stwo[CB - HALO :], sfour[CB - HALO :]))
    put(HALO + 4 * CB, four_ref[...].astype(f32))
    put(HALO + ROWS, jnp.where(even, sfour[:HALO], halo[HALO:]))

    for i in range(NEAR):
        base = 2 * i * CB
        held = masked.at[i % 2]
        centre = seg_ref[base + HALO : base + HALO + CB, :]
        for e in range(SPAN):
            first = base + HALO - HALF + e
            keep = jnp.where(seg_ref[first : first + CB, :] == centre, 1.0, 0.0)
            for j in range(NCHUNK):
                held[j * CB : (j + 1) * CB, e * CHUNK : (e + 1) * CHUNK] = (
                    rec[j, first : first + CB, :] * keep
                ).astype(bf16)
        share = jnp.dot(held[...], band_ref[...], preferred_element_type=f32)
        for j in range(NCHUNK):
            result = share[j * CB : (j + 1) * CB, :CHUNK]
            if j:
                result = result + share[(j - 1) * CB : j * CB, CHUNK:]
            filt[j, i * CB : (i + 1) * CB, :] = result.astype(bf16)

    rows = []
    for ref in part_refs:
        value = ref[...].astype(f32)
        rows += [value[at : at + SLOT] for at in range(0, value.shape[0], SLOT)]
    mine, theirs = rows[::2], rows[1::2]
    lists = count // 2
    skip = lists - len(mine)
    mine, theirs = ([part[0]] + [None] * skip + part[1:] for part in (mine, theirs))
    between = [HALO + r * CB for r in range(1, BAND + 2, 2)]

    def row_at(i, e, j):
        at = between[i] - HALF + e
        return rec[j, at : at + 1, :]

    local = filter_rows(row_at, seg_ref, between, line, band_ref)
    for r in range(count):
        if r <= BAND and r % 2 == 0:
            rows = [filt[j, r // 2 * CB : r // 2 * CB + 1, :] for j in range(NCHUNK)]
        else:
            if r <= BAND + 1:
                value = local[r // 2]
            elif r % 2 == 0:
                value = mine[r // 2]
            else:
                value = jnp.where(even, theirs[r // 2], theirs[(r // 2 + 1) % lists])
            rows = [value[j : j + 1].astype(bf16) for j in range(NCHUNK)]
        for j in range(NCHUNK):
            filt[j, NEAR * CB + r : NEAR * CB + r + 1, :] = rows[j]

    @pl.when(index_ref[0] >= 0)
    def _():
        tiles = COVER // CHUNK - 1
        tail = None
        for w in range(W):
            lhs = jnp.concatenate([filt[w * tiles + q] for q in range(tiles + 1)], axis=1)
            raw = jnp.dot(lhs, dft_ref[w], preferred_element_type=f32)
            power = jnp.sum(raw * raw, axis=-1, keepdims=True) * (1.0 / L)
            whitened = raw * lax.rsqrt(power + 1e-06)
            head = whitened[:, :CHUNK] if tail is None else tail + whitened[:, :CHUNK]
            spec[:, w * tiles * CHUNK : (w * tiles + 1) * CHUNK] = head.astype(bf16)
            spec[:, (w * tiles + 1) * CHUNK : (w + 1) * tiles * CHUNK] = whitened[:, CHUNK : tiles * CHUNK].astype(bf16)
            tail = whitened[:, tiles * CHUNK :]
        spec[:, W * tiles * CHUNK :] = tail.astype(bf16)

    give_ref[...] = jnp.where(even, spec[CB : 3 * CB, :].astype(f32), spec[: 2 * CB, :].astype(f32)).astype(bf16)
    row = lax.broadcasted_iota(jnp.int32, (count, count), 0)
    column = lax.broadcasted_iota(jnp.int32, (count, count), 1)
    ahead = row - index_ref[0]
    ahead = jnp.where(ahead < 0, ahead + count, ahead)
    order = jnp.where(ahead == column, 1.0, 0.0).astype(bf16)
    spec[NEAR * CB :, :] = jnp.dot(order, spec[NEAR * CB :, :], preferred_element_type=f32).astype(bf16)


def turn_kernel(seg_ref, pseg_ref, spec, lag_ref, out_ref, src_ref, turned, totals, swapped):
    count = spec.shape[0] - NEAR * CB
    own = spec[:CB, :].astype(f32)
    pieces = []
    for w in range(W):
        pieces += [own[:, w * L + F : (w + 1) * L], own[:, w * L : w * L + F]]
    swapped[...] = jnp.concatenate(pieces + [jnp.zeros((CB, KP - W * L), f32)], axis=1)
    own_seg = seg_ref[HALO : HALO + CB, :]

    def multiply(step, slot):
        start = pl.multiple_of(step * GROUP, GROUP)
        first = pl.multiple_of(step * GROUP * CB, GROUP * CB)
        for at in range(0, KP, CHUNK):
            lanes = slice(at, at + CHUNK)
            straight, crossed = lag_ref[0, pl.ds(start, GROUP), lanes], lag_ref[1, pl.ds(start, GROUP), lanes]
            own, other = spec[:CB, lanes].astype(f32), swapped[:, lanes]
            for g in range(GROUP):
                turned[pl.ds(first + g * CB, CB), lanes] = (
                    own * straight[g : g + 1, :] + other * crossed[g : g + 1, :]
                ).astype(bf16)
        totals[slot] = lax.dot_general(
            turned[pl.ds(first, GROUP * CB), :], spec[...], (((1,), (1,)), ((), ())), preferred_element_type=f32
        )

    def write(step, slot):
        start = pl.multiple_of(step * GROUP, GROUP)
        write_pairs(totals.at[slot], step, own_seg, pseg_ref, out_ref, range(0, BAND + 1, 2))
        sources = jnp.concatenate(
            [totals[slot, g * CB : (g + 1) * CB, NEAR * CB :] for g in range(GROUP)], axis=1
        )
        src_ref[:, pl.ds(pl.multiple_of(start * count, GROUP * count), GROUP * count)] = sources.astype(bf16)

    multiply(0, 0)

    @pl.loop(1, LAGS // GROUP)
    def _(step):
        write(step - 1, (step - 1) % 2)
        multiply(step, step % 2)

    write(LAGS // GROUP - 1, (LAGS // GROUP - 1) % 2)


def write_pairs(total, step, own_seg, pseg_ref, out_ref, blocks):
    for pair in range(GROUP // 2):
        low, high = 2 * pair * CB, (2 * pair + 1) * CB
        lanes = pl.ds(pl.multiple_of(step * GROUP * CB + pair * 2 * CB, 2 * CB), 2 * CB)
        for i, k in enumerate(blocks):
            both = jnp.concatenate([total[at : at + CB, i * CB : (i + 1) * CB] for at in (low, high)], axis=1)
            keep = own_seg == pseg_ref[k : k + 1, :]
            out_ref[i, :, lanes] = jnp.where(keep, both, 0.0).astype(bf16)


def rest_kernel(seg_ref, pseg_ref, turned, take, even_ref, out_hbm, odd_ref, totals, even_sems, odd_sems):
    early = start_loads(
        tuple((even_ref.at[i], out_hbm.at[k]) for i, k in enumerate(range(0, BAND + 1, 2))), even_sems
    )
    own_seg = seg_ref[HALO : HALO + CB, :]
    steps = LAGS // GROUP

    def store(step, i):
        lanes = pl.ds(pl.multiple_of(step * GROUP * CB, GROUP * CB), GROUP * CB)
        return pltpu.make_async_copy(
            odd_ref.at[i, :, lanes], out_hbm.at[2 * i + 1, :, lanes], odd_sems.at[step, i]
        )

    def multiply(step, slot):
        rows = pl.ds(pl.multiple_of(step * GROUP * CB, GROUP * CB), GROUP * CB)
        totals[slot] = lax.dot_general(
            turned[rows, :], take[...], (((1,), (1,)), ((), ())), preferred_element_type=f32
        )

    def write(step, slot):
        write_pairs(totals.at[slot], step, own_seg, pseg_ref, odd_ref, range(1, BAND + 1, 2))
        for i in range(BAND // 2):
            store(step, i).start()

    multiply(0, 0)

    @pl.loop(1, steps)
    def _(step):
        write(step - 1, (step - 1) % 2)
        multiply(step, step % 2)

    write(steps - 1, (steps - 1) % 2)
    for step in range(steps):
        for i in range(BAND // 2):
            store(step, i).wait()
    for load in early:
        load.wait()


VMEM = pl.BlockSpec(memory_space=pltpu.VMEM)
SMEM = pl.BlockSpec(memory_space=pltpu.SMEM)
HBM = pl.BlockSpec(memory_space=pltpu.HBM)


def call(kernel, shapes, scratch, specs, **kwargs):
    return pl.pallas_call(
        kernel, out_shape=shapes, in_specs=specs, out_specs=jax.tree.map(lambda _: VMEM, shapes), scratch_shapes=scratch, **kwargs
    )


def per_device(records, filter_taps, segment_ids):
    count = lax.axis_size("fibre")
    device = lax.axis_index("fibre")

    def ahead(value, distance):
        return lax.ppermute(value, "fibre", [(i, (i - distance) % count) for i in range(count)])

    def swap(value):
        return lax.ppermute(value, "fibre", [(i, i ^ 1) for i in range(count)])

    index = device.reshape(1)
    few = count <= 16
    stay = functools.partial(pltpu.with_memory_space_constraint, memory_space=pltpu.HBM)

    edge = call(
        edge_kernel,
        jax.ShapeDtypeStruct((2 * HALO, W * L), bf16),
        [pltpu.SemaphoreType.DMA((2,))],
        [HBM],
        compiler_params=pltpu.CompilerParams(vmem_limit_bytes=EDGE_LIMIT),
    )(stay(records))
    route = [(i, (i + 1) % count if i % 2 else (i - BAND - 1) % count) for i in range(count)]
    halo = lax.ppermute(edge, "fibre", route)
    sown = swap(records)
    four = ahead(records, 4)
    two = ahead(records, 2)

    dft, lags = dft_tables(), lag_tables()
    source, band, segs, own, dft, lags = call(
        prep_kernel,
        (
            jax.ShapeDtypeStruct((SLOT, CHUNK), bf16),
            jax.ShapeDtypeStruct((SPAN * CHUNK, 2 * CHUNK), bf16),
            jax.ShapeDtypeStruct((ROWS + 2 * HALO, CHUNK), f32),
            jax.ShapeDtypeStruct(records.shape, bf16),
            jax.ShapeDtypeStruct(dft.shape, bf16),
            jax.ShapeDtypeStruct(lags.shape, f32),
        ),
        [
            pltpu.VMEM(filter_taps.shape, bf16),
            pltpu.VMEM((1,) + segment_ids.shape, jnp.int32),
            pltpu.VMEM((SLOT, SPAN * CHUNK), f32),
            pltpu.SemaphoreType.DMA((5,)),
        ],
        [SMEM] + [VMEM] * 3 + [HBM] * 5,
        compiler_params=pltpu.CompilerParams(vmem_limit_bytes=PREP_LIMIT if few else None),
    )(
        index, edge, halo, sown, stay(filter_taps), stay(segment_ids.reshape(1, -1)), stay(records), stay(dft),
        stay(lags),
    )

    lists = count // 2
    pair = jnp.concatenate([source, swap(source)], axis=0)
    first = BAND // 2 + 1 if lists <= 8 else 1
    parts = [pair] + [ahead(pair, 2 * s) for s in range(first, min(8, lists))]
    have = 8
    while have < lists:
        known = jnp.concatenate(parts, axis=0)
        for s in range(1, 8):
            left = lists - s * have
            if left > 0:
                parts.append(ahead(known[: 2 * SLOT * left], 2 * s * have))
        have = min(8 * have, lists)
    pseg = call(
        functools.partial(partner_kernel, count), jax.ShapeDtypeStruct((8, CHUNK), f32), (), [SMEM, VMEM],
        compiler_params=pltpu.CompilerParams(vmem_limit_bytes=TABLE_LIMIT),
    )(index, segs)
    sfour, stwo = swap(four), swap(two)

    limit = pltpu.CompilerParams(vmem_limit_bytes=MAIN_LIMIT if few else None)
    spec, give = call(
        functools.partial(spectra_kernel, len(parts), count),
        (
            jax.ShapeDtypeStruct((NEAR * CB + count, KP), bf16),
            jax.ShapeDtypeStruct((2 * CB, KP), bf16),
        ),
        [
            pltpu.VMEM((NCHUNK, ROWS + 2 * HALO, CHUNK), f32),
            pltpu.VMEM((2, NCHUNK * CB, SPAN * CHUNK), bf16),
            pltpu.VMEM((NCHUNK, NEAR * CB + count, CHUNK), bf16),
            pltpu.VMEM((NEAR * SLOT, SPAN * CHUNK), f32),
        ],
        [SMEM] + [VMEM] * (10 + len(parts)),
        compiler_params=limit,
    )(index, own, two, four, sown, stwo, sfour, halo, *parts, segs, band, dft)
    take = swap(give)
    even_blocks, source_out, turned = call(
        turn_kernel,
        (
            jax.ShapeDtypeStruct((NEAR, CB, LAGS * CB), bf16),
            jax.ShapeDtypeStruct((CB, LAGS * count), bf16),
            jax.ShapeDtypeStruct((LAGS * CB, KP), bf16),
        ),
        [
            pltpu.VMEM((2, GROUP * CB, NEAR * CB + count), f32),
            pltpu.VMEM((CB, KP), f32),
        ],
        [VMEM] * 4,
        compiler_params=limit,
    )(segs, pseg, spec, lags)
    stacked = pl.pallas_call(
        rest_kernel,
        out_shape=jax.ShapeDtypeStruct((BAND + 1, CB, LAGS * CB), bf16),
        in_specs=[VMEM] * 5,
        out_specs=HBM,
        scratch_shapes=[
            pltpu.VMEM((BAND // 2, CB, LAGS * CB), bf16),
            pltpu.VMEM((2, GROUP * CB, 2 * CB), f32),
            pltpu.SemaphoreType.DMA((NEAR,)),
            pltpu.SemaphoreType.DMA((LAGS // GROUP, BAND // 2)),
        ],
        compiler_params=limit,
    )(segs, pseg, turned, take, even_blocks)
    return (jnp.swapaxes(stacked, 0, 1), source_out)


def solution(mesh):
    return jax.shard_map(
        per_device,
        mesh=mesh,
        in_specs=(P(("runs", "fibre"), None), P(), P("runs")),
        out_specs=(P(("runs", "fibre"), None, None), P(("runs", "fibre"), None)),
        check_vma=False,
    )
```

```python
import functools

import jax
import jax.numpy as jnp
import numpy as np
from jax import lax
from jax.experimental import pallas as pl
from jax.experimental.pallas import tpu as pltpu
from jax.sharding import PartitionSpec as P


CB = 64
W = 4
F = 200
L = 400
TAPS = 63
SPAN = 9
LAGS = 32
BAND = 4
HALF = (SPAN - 1) // 2
SLOT = 16
HALO = 8
CHUNK = 128
NCHUNK = -(-W * L // CHUNK)
KP = -(-W * L // CHUNK) * CHUNK
ROWS = (BAND + 1) * CB
NEAR = BAND // 2 + 1
GROUP = 8
SHIFT = L % CHUNK
COVER = 4 * CHUNK

MAIN_LIMIT = 20 << 20
PREP_LIMIT = 12 << 20
EDGE_LIMIT = 1 << 20
TABLE_LIMIT = 2 << 20

f32 = jnp.float32
bf16 = jnp.bfloat16


def dft_tables():
    t = np.arange(L)
    taper = 0.5 - 0.5 * np.cos((t + 0.5) * (2.0 * np.pi / L))
    phase = (t[:, None] * np.arange(F)[None, :] % L) * (2.0 * np.pi / L)
    table = np.concatenate([taper[:, None] * np.cos(phase), -taper[:, None] * np.sin(phase)], axis=1)
    tables = np.zeros((W, COVER, COVER))
    for w in range(W):
        tables[w, w * SHIFT : w * SHIFT + L, w * SHIFT : w * SHIFT + L] = table
    return jnp.asarray(tables.astype(np.float32), bf16)


def lag_tables():
    m = np.arange(LAGS) - LAGS // 2
    phase = (m[:, None] * np.arange(F)[None, :] % L) * (2.0 * np.pi / L)
    scale = 1.0 / np.sqrt(2.0 * L)
    straight, crossed = np.cos(phase) * scale, -np.sin(phase) * scale
    tables = np.zeros((2, LAGS, KP))
    tables[0, :, : W * L] = np.tile(np.concatenate([straight, straight], axis=1), (1, W))
    tables[1, :, : W * L] = np.tile(np.concatenate([crossed, -crossed], axis=1), (1, W))
    return jnp.asarray(tables.astype(np.float32), bf16).astype(f32)


def start_loads(pairs, sems):
    loads = [pltpu.make_async_copy(source, target, sems.at[i]) for i, (source, target) in enumerate(pairs)]
    for load in loads:
        load.start()
    return loads


def edge_kernel(own_hbm, edge_ref, sems):
    last = (own_hbm.at[pl.ds(CB - HALO, HALO)], edge_ref.at[pl.ds(0, HALO)])
    first = (own_hbm.at[pl.ds(0, HALO)], edge_ref.at[pl.ds(HALO, HALO)])
    for load in start_loads((last, first), sems):
        load.wait()


def chunk(rows, j):
    piece = rows[:, j * CHUNK : min((j + 1) * CHUNK, W * L)]
    if piece.shape[1] < CHUNK:
        piece = jnp.concatenate([piece, jnp.zeros((piece.shape[0], CHUNK - piece.shape[1]), piece.dtype)], axis=1)
    return piece


def filter_rows(row_at, seg_ref, centres, line, band_ref):
    line[...] = jnp.zeros_like(line)
    for i, centre in enumerate(centres):
        own = seg_ref[centre : centre + 1, :]
        for e in range(SPAN):
            at = centre - HALF + e
            keep = jnp.where(seg_ref[at : at + 1, :] == own, 1.0, 0.0)
            for j in range(NCHUNK):
                line[i * SLOT + j : i * SLOT + j + 1, e * CHUNK : (e + 1) * CHUNK] = row_at(i, e, j) * keep
    share = jnp.dot(line[...].astype(bf16), band_ref[...], preferred_element_type=f32)
    results = []
    for i in range(len(centres)):
        part = share[i * SLOT : (i + 1) * SLOT]
        before = jnp.concatenate([jnp.zeros((1, CHUNK), f32), part[:-1, CHUNK:]], axis=0)
        results.append(part[:, :CHUNK] + before)
    return results


def prep_kernel(
    index_ref, edge_ref, halo_ref, sown_ref, taps_hbm, ids_hbm, own_hbm, dft_hbm, lag_hbm,
    source_ref, band_ref, seg_ref, own_ref, dft_ref, lag_ref, taps_ref, ids_ref, line, sems,
):
    loads = start_loads(
        ((taps_hbm, taps_ref), (ids_hbm, ids_ref), (own_hbm, own_ref), (dft_hbm, dft_ref), (lag_hbm, lag_ref)), sems
    )
    device = index_ref[0]
    total = ids_ref.shape[1]
    loads[0].wait()
    wide = jnp.concatenate([taps_ref[...].astype(f32), jnp.zeros((SPAN, 2 * CHUNK - TAPS), f32)], axis=1)
    for e in range(SPAN):
        row = jnp.broadcast_to(wide[e : e + 1, :], (CHUNK, 2 * CHUNK))
        band_ref[e * CHUNK : (e + 1) * CHUNK, :] = pltpu.roll(row, 0, 1, stride=1, stride_axis=0).astype(bf16)

    loads[1].wait()
    ids = jnp.broadcast_to(ids_ref[...].astype(bf16), (CHUNK, total))
    channels = device * CB - HALO + lax.broadcasted_iota(jnp.int32, (ROWS + 2 * HALO, 1), 0)
    channels = jnp.where(channels < 0, channels + total, channels)
    channels = jnp.where(channels >= total, channels - total, channels)
    hit = lax.broadcasted_iota(jnp.int32, (ROWS + 2 * HALO, total), 1) == channels
    seg_ref[...] = lax.dot_general(
        jnp.where(hit, 1.0, 0.0).astype(bf16), ids, (((1,), (1,)), ((), ())), preferred_element_type=f32
    )

    even = device % 2 == 0
    behind = jnp.where(even, halo_ref[:HALO].astype(f32), sown_ref[CB - HALO :].astype(f32))
    first = edge_ref[HALO:].astype(f32)

    def row_at(_, e, j):
        rows, at = (behind, HALO - HALF + e) if e < HALF else (first, e - HALF)
        return chunk(rows, j)[at : at + 1]

    source_ref[...] = filter_rows(row_at, seg_ref, (HALO,), line, band_ref)[0].astype(bf16)
    for load in loads[2:]:
        load.wait()


def partner_kernel(count, index_ref, seg_ref, pseg_ref):
    for k in range(BAND + 1):
        block = seg_ref[HALO + k * CB : HALO + (k + 1) * CB, :]
        turned = jnp.transpose(jnp.concatenate([block, block], axis=0))
        pseg_ref[k : k + 1, :] = jnp.where(index_ref[0] + k < count, turned[:1], -1.0)
    pseg_ref[BAND + 1 :, :] = jnp.full((8 - BAND - 1, CHUNK), -1.0, f32)


def spectra_kernel(pieces, count, *refs):
    index_ref, own_ref, two_ref, four_ref, sown_ref, stwo_ref, sfour_ref, halo_ref = refs[:8]
    part_refs, refs = refs[8 : 8 + pieces], refs[8 + pieces :]
    seg_ref, band_ref, dft_ref, spec, give_ref, rec, masked, filt, line = refs
    even = index_ref[0] % 2 == 0

    def put(start, rows):
        for j in range(NCHUNK):
            rec[j, start : start + rows.shape[0], :] = chunk(rows, j)

    stwo, sfour = stwo_ref[...].astype(f32), sfour_ref[...].astype(f32)
    sown, halo = sown_ref[...].astype(f32), halo_ref[...].astype(f32)
    put(0, jnp.where(even, halo[:HALO], sown[CB - HALO :]))
    put(HALO, own_ref[...].astype(f32))
    put(HALO + CB, jnp.where(even, sown[:HALO], stwo[:HALO]))
    put(2 * CB, jnp.where(even, sown[CB - HALO :], stwo[CB - HALO :]))
    put(HALO + 2 * CB, two_ref[...].astype(f32))
    put(HALO + 3 * CB, jnp.where(even, stwo[:HALO], sfour[:HALO]))
    put(4 * CB, jnp.where(even, stwo[CB - HALO :], sfour[CB - HALO :]))
    put(HALO + 4 * CB, four_ref[...].astype(f32))
    put(HALO + ROWS, jnp.where(even, sfour[:HALO], halo[HALO:]))

    for i in range(NEAR):
        base = 2 * i * CB
        held = masked.at[i % 2]
        centre = seg_ref[base + HALO : base + HALO + CB, :]
        for e in range(SPAN):
            first = base + HALO - HALF + e
            keep = jnp.where(seg_ref[first : first + CB, :] == centre, 1.0, 0.0)
            for j in range(NCHUNK):
                held[j * CB : (j + 1) * CB, e * CHUNK : (e + 1) * CHUNK] = (
                    rec[j, first : first + CB, :] * keep
                ).astype(bf16)
        share = jnp.dot(held[...], band_ref[...], preferred_element_type=f32)
        for j in range(NCHUNK):
            result = share[j * CB : (j + 1) * CB, :CHUNK]
            if j:
                result = result + share[(j - 1) * CB : j * CB, CHUNK:]
            filt[j, i * CB : (i + 1) * CB, :] = result.astype(bf16)

    rows = []
    for ref in part_refs:
        value = ref[...].astype(f32)
        rows += [value[at : at + SLOT] for at in range(0, value.shape[0], SLOT)]
    mine, theirs = rows[::2], rows[1::2]
    lists = count // 2
    skip = lists - len(mine)
    mine, theirs = ([part[0]] + [None] * skip + part[1:] for part in (mine, theirs))
    between = [HALO + r * CB for r in range(1, BAND + 2, 2)]

    def row_at(i, e, j):
        at = between[i] - HALF + e
        return rec[j, at : at + 1, :]

    local = filter_rows(row_at, seg_ref, between, line, band_ref)
    for r in range(count):
        if r <= BAND and r % 2 == 0:
            rows = [filt[j, r // 2 * CB : r // 2 * CB + 1, :] for j in range(NCHUNK)]
        else:
            if r <= BAND + 1:
                value = local[r // 2]
            elif r % 2 == 0:
                value = mine[r // 2]
            else:
                value = jnp.where(even, theirs[r // 2], theirs[(r // 2 + 1) % lists])
            rows = [value[j : j + 1].astype(bf16) for j in range(NCHUNK)]
        for j in range(NCHUNK):
            filt[j, NEAR * CB + r : NEAR * CB + r + 1, :] = rows[j]

    @pl.when(index_ref[0] >= 0)
    def _():
        tiles = COVER // CHUNK - 1
        tail = None
        for w in range(W):
            lhs = jnp.concatenate([filt[w * tiles + q] for q in range(tiles + 1)], axis=1)
            raw = jnp.dot(lhs, dft_ref[w], preferred_element_type=f32)
            power = jnp.sum(raw * raw, axis=-1, keepdims=True) * (1.0 / L)
            whitened = raw * lax.rsqrt(power + 1e-06)
            head = whitened[:, :CHUNK] if tail is None else tail + whitened[:, :CHUNK]
            spec[:, w * tiles * CHUNK : (w * tiles + 1) * CHUNK] = head.astype(bf16)
            spec[:, (w * tiles + 1) * CHUNK : (w + 1) * tiles * CHUNK] = whitened[:, CHUNK : tiles * CHUNK].astype(bf16)
            tail = whitened[:, tiles * CHUNK :]
        spec[:, W * tiles * CHUNK :] = tail.astype(bf16)

    give_ref[...] = jnp.where(even, spec[CB : 3 * CB, :].astype(f32), spec[: 2 * CB, :].astype(f32)).astype(bf16)
    row = lax.broadcasted_iota(jnp.int32, (count, count), 0)
    column = lax.broadcasted_iota(jnp.int32, (count, count), 1)
    ahead = row - index_ref[0]
    ahead = jnp.where(ahead < 0, ahead + count, ahead)
    order = jnp.where(ahead == column, 1.0, 0.0).astype(bf16)
    spec[NEAR * CB :, :] = jnp.dot(order, spec[NEAR * CB :, :], preferred_element_type=f32).astype(bf16)


def turn_kernel(seg_ref, pseg_ref, spec, lag_ref, out_ref, src_ref, turned, totals, swapped):
    count = spec.shape[0] - NEAR * CB
    own = spec[:CB, :].astype(f32)
    pieces = []
    for w in range(W):
        pieces += [own[:, w * L + F : (w + 1) * L], own[:, w * L : w * L + F]]
    swapped[...] = jnp.concatenate(pieces + [jnp.zeros((CB, KP - W * L), f32)], axis=1)
    own_seg = seg_ref[HALO : HALO + CB, :]

    def multiply(step, slot):
        start, first = step * GROUP, step * GROUP * CB
        for at in range(0, KP, CHUNK):
            lanes = slice(at, at + CHUNK)
            straight, crossed = lag_ref[0, start : start + GROUP, lanes], lag_ref[1, start : start + GROUP, lanes]
            own, other = spec[:CB, lanes].astype(f32), swapped[:, lanes]
            for g in range(GROUP):
                turned[first + g * CB : first + (g + 1) * CB, lanes] = (
                    own * straight[g : g + 1, :] + other * crossed[g : g + 1, :]
                ).astype(bf16)
        totals[slot] = lax.dot_general(
            turned[first : first + GROUP * CB, :], spec[...], (((1,), (1,)), ((), ())), preferred_element_type=f32
        )

    def write(step, slot):
        start = step * GROUP
        write_pairs(totals.at[slot], step, own_seg, pseg_ref, out_ref, range(0, BAND + 1, 2))
        sources = jnp.concatenate(
            [totals[slot, g * CB : (g + 1) * CB, NEAR * CB :] for g in range(GROUP)], axis=1
        )
        src_ref[:, start * count : (start + GROUP) * count] = sources.astype(bf16)

    for step in range(LAGS // GROUP):
        multiply(step, step % 2)
        if step:
            write(step - 1, (step - 1) % 2)
    write(LAGS // GROUP - 1, (LAGS // GROUP - 1) % 2)


def write_pairs(total, step, own_seg, pseg_ref, out_ref, blocks):
    for pair in range(GROUP // 2):
        low, high = 2 * pair * CB, (2 * pair + 1) * CB
        at = step * GROUP * CB + pair * 2 * CB
        lanes = slice(at, at + 2 * CB)
        for i, k in enumerate(blocks):
            both = jnp.concatenate([total[row : row + CB, i * CB : (i + 1) * CB] for row in (low, high)], axis=1)
            keep = own_seg == pseg_ref[k : k + 1, :]
            out_ref[i, :, lanes] = jnp.where(keep, both, 0.0).astype(bf16)


def rest_kernel(seg_ref, pseg_ref, turned, take, even_ref, out_hbm, odd_ref, totals, even_sems, odd_sems):
    early = start_loads(
        tuple((even_ref.at[i], out_hbm.at[k]) for i, k in enumerate(range(0, BAND + 1, 2))), even_sems
    )
    own_seg = seg_ref[HALO : HALO + CB, :]
    steps = LAGS // GROUP

    def store(step, i):
        lanes = pl.ds(step * GROUP * CB, GROUP * CB)
        return pltpu.make_async_copy(
            odd_ref.at[i, :, lanes], out_hbm.at[2 * i + 1, :, lanes], odd_sems.at[step, i]
        )

    def multiply(step, slot):
        first = step * GROUP * CB
        totals[slot] = lax.dot_general(
            turned[first : first + GROUP * CB, :], take[...], (((1,), (1,)), ((), ())), preferred_element_type=f32
        )

    def write(step, slot):
        write_pairs(totals.at[slot], step, own_seg, pseg_ref, odd_ref, range(1, BAND + 1, 2))
        for i in range(BAND // 2):
            store(step, i).start()

    for step in range(steps):
        multiply(step, step % 2)
        if step:
            write(step - 1, (step - 1) % 2)
    write(steps - 1, (steps - 1) % 2)
    for step in range(steps):
        for i in range(BAND // 2):
            store(step, i).wait()
    for load in early:
        load.wait()


VMEM = pl.BlockSpec(memory_space=pltpu.VMEM)
SMEM = pl.BlockSpec(memory_space=pltpu.SMEM)
HBM = pl.BlockSpec(memory_space=pltpu.HBM)


def call(kernel, shapes, scratch, specs, **kwargs):
    return pl.pallas_call(
        kernel, out_shape=shapes, in_specs=specs, out_specs=jax.tree.map(lambda _: VMEM, shapes), scratch_shapes=scratch, **kwargs
    )


def per_device(records, filter_taps, segment_ids):
    count = lax.axis_size("fibre")
    device = lax.axis_index("fibre")

    def ahead(value, distance):
        return lax.ppermute(value, "fibre", [(i, (i - distance) % count) for i in range(count)])

    def swap(value):
        return lax.ppermute(value, "fibre", [(i, i ^ 1) for i in range(count)])

    index = device.reshape(1)
    few = count <= 16
    stay = functools.partial(pltpu.with_memory_space_constraint, memory_space=pltpu.HBM)

    edge = call(
        edge_kernel,
        jax.ShapeDtypeStruct((2 * HALO, W * L), bf16),
        [pltpu.SemaphoreType.DMA((2,))],
        [HBM],
        compiler_params=pltpu.CompilerParams(vmem_limit_bytes=EDGE_LIMIT),
    )(stay(records))
    route = [(i, (i + 1) % count if i % 2 else (i - BAND - 1) % count) for i in range(count)]
    halo = lax.ppermute(edge, "fibre", route)
    sown = swap(records)
    four = ahead(records, 4)
    two = ahead(records, 2)

    dft, lags = dft_tables(), lag_tables()
    source, band, segs, own, dft, lags = call(
        prep_kernel,
        (
            jax.ShapeDtypeStruct((SLOT, CHUNK), bf16),
            jax.ShapeDtypeStruct((SPAN * CHUNK, 2 * CHUNK), bf16),
            jax.ShapeDtypeStruct((ROWS + 2 * HALO, CHUNK), f32),
            jax.ShapeDtypeStruct(records.shape, bf16),
            jax.ShapeDtypeStruct(dft.shape, bf16),
            jax.ShapeDtypeStruct(lags.shape, f32),
        ),
        [
            pltpu.VMEM(filter_taps.shape, bf16),
            pltpu.VMEM((1,) + segment_ids.shape, jnp.int32),
            pltpu.VMEM((SLOT, SPAN * CHUNK), f32),
            pltpu.SemaphoreType.DMA((5,)),
        ],
        [SMEM] + [VMEM] * 3 + [HBM] * 5,
        compiler_params=pltpu.CompilerParams(vmem_limit_bytes=PREP_LIMIT if few else None),
    )(
        index, edge, halo, sown, stay(filter_taps), stay(segment_ids.reshape(1, -1)), stay(records), stay(dft),
        stay(lags),
    )

    lists = count // 2
    pair = jnp.concatenate([source, swap(source)], axis=0)
    first = BAND // 2 + 1 if lists <= 8 else 1
    parts = [pair] + [ahead(pair, 2 * s) for s in range(first, min(8, lists))]
    have = 8
    while have < lists:
        known = jnp.concatenate(parts, axis=0)
        for s in range(1, 8):
            left = lists - s * have
            if left > 0:
                parts.append(ahead(known[: 2 * SLOT * left], 2 * s * have))
        have = min(8 * have, lists)
    pseg = call(
        functools.partial(partner_kernel, count), jax.ShapeDtypeStruct((8, CHUNK), f32), (), [SMEM, VMEM],
        compiler_params=pltpu.CompilerParams(vmem_limit_bytes=TABLE_LIMIT),
    )(index, segs)
    sfour, stwo = swap(four), swap(two)

    limit = pltpu.CompilerParams(vmem_limit_bytes=MAIN_LIMIT if few else None)
    spec, give = call(
        functools.partial(spectra_kernel, len(parts), count),
        (
            jax.ShapeDtypeStruct((NEAR * CB + count, KP), bf16),
            jax.ShapeDtypeStruct((2 * CB, KP), bf16),
        ),
        [
            pltpu.VMEM((NCHUNK, ROWS + 2 * HALO, CHUNK), f32),
            pltpu.VMEM((2, NCHUNK * CB, SPAN * CHUNK), bf16),
            pltpu.VMEM((NCHUNK, NEAR * CB + count, CHUNK), bf16),
            pltpu.VMEM((NEAR * SLOT, SPAN * CHUNK), f32),
        ],
        [SMEM] + [VMEM] * (10 + len(parts)),
        compiler_params=limit,
    )(index, own, two, four, sown, stwo, sfour, halo, *parts, segs, band, dft)
    take = swap(give)
    even_blocks, source_out, turned = call(
        turn_kernel,
        (
            jax.ShapeDtypeStruct((NEAR, CB, LAGS * CB), bf16),
            jax.ShapeDtypeStruct((CB, LAGS * count), bf16),
            jax.ShapeDtypeStruct((LAGS * CB, KP), bf16),
        ),
        [
            pltpu.VMEM((2, GROUP * CB, NEAR * CB + count), f32),
            pltpu.VMEM((CB, KP), f32),
        ],
        [VMEM] * 4,
        compiler_params=limit,
    )(segs, pseg, spec, lags)
    stacked = pl.pallas_call(
        rest_kernel,
        out_shape=jax.ShapeDtypeStruct((BAND + 1, CB, LAGS * CB), bf16),
        in_specs=[VMEM] * 5,
        out_specs=HBM,
        scratch_shapes=[
            pltpu.VMEM((BAND // 2, CB, LAGS * CB), bf16),
            pltpu.VMEM((2, GROUP * CB, 2 * CB), f32),
            pltpu.SemaphoreType.DMA((NEAR,)),
            pltpu.SemaphoreType.DMA((LAGS // GROUP, BAND // 2)),
        ],
        compiler_params=limit,
    )(segs, pseg, turned, take, even_blocks)
    return (jnp.swapaxes(stacked, 0, 1), source_out)


def solution(mesh):
    return jax.shard_map(
        per_device,
        mesh=mesh,
        in_specs=(P(("runs", "fibre"), None), P(), P("runs")),
        out_specs=(P(("runs", "fibre"), None, None), P(("runs", "fibre"), None)),
        check_vma=False,
    )
```

```python
import functools

import jax
import jax.numpy as jnp
import numpy as np
from jax import lax
from jax.experimental import pallas as pl
from jax.experimental.pallas import tpu as pltpu
from jax.sharding import PartitionSpec as P


CB = 64
W = 4
F = 200
L = 400
TAPS = 63
SPAN = 9
LAGS = 32
BAND = 4
HALF = (SPAN - 1) // 2
SLOT = 16
HALO = 8
CHUNK = 128
NCHUNK = -(-W * L // CHUNK)
KP = -(-W * L // CHUNK) * CHUNK
ROWS = (BAND + 1) * CB
NEAR = BAND // 2 + 1
GROUP = 8
SHIFT = L % CHUNK
COVER = 4 * CHUNK

MAIN_LIMIT = 20 << 20
PREP_LIMIT = 12 << 20
EDGE_LIMIT = 1 << 20
TABLE_LIMIT = 2 << 20

f32 = jnp.float32
bf16 = jnp.bfloat16


def dft_tables():
    t = np.arange(L)
    taper = 0.5 - 0.5 * np.cos((t + 0.5) * (2.0 * np.pi / L))
    phase = (t[:, None] * np.arange(F)[None, :] % L) * (2.0 * np.pi / L)
    table = np.concatenate([taper[:, None] * np.cos(phase), -taper[:, None] * np.sin(phase)], axis=1)
    tables = np.zeros((W, COVER, COVER))
    for w in range(W):
        tables[w, w * SHIFT : w * SHIFT + L, w * SHIFT : w * SHIFT + L] = table
    return jnp.asarray(tables.astype(np.float32), bf16)


def lag_tables():
    m = np.arange(LAGS) - LAGS // 2
    phase = (m[:, None] * np.arange(F)[None, :] % L) * (2.0 * np.pi / L)
    scale = 1.0 / np.sqrt(2.0 * L)
    straight, crossed = np.cos(phase) * scale, -np.sin(phase) * scale
    tables = np.zeros((2, LAGS, KP))
    tables[0, :, : W * L] = np.tile(np.concatenate([straight, straight], axis=1), (1, W))
    tables[1, :, : W * L] = np.tile(np.concatenate([crossed, -crossed], axis=1), (1, W))
    return jnp.asarray(tables.astype(np.float32), bf16).astype(f32)


def start_loads(pairs, sems):
    loads = [pltpu.make_async_copy(source, target, sems.at[i]) for i, (source, target) in enumerate(pairs)]
    for load in loads:
        load.start()
    return loads


def edge_kernel(own_hbm, edge_ref, sems):
    last = (own_hbm.at[pl.ds(CB - HALO, HALO)], edge_ref.at[pl.ds(0, HALO)])
    first = (own_hbm.at[pl.ds(0, HALO)], edge_ref.at[pl.ds(HALO, HALO)])
    for load in start_loads((last, first), sems):
        load.wait()


def chunk(rows, j):
    piece = rows[:, j * CHUNK : min((j + 1) * CHUNK, W * L)]
    if piece.shape[1] < CHUNK:
        piece = jnp.concatenate([piece, jnp.zeros((piece.shape[0], CHUNK - piece.shape[1]), piece.dtype)], axis=1)
    return piece


def filter_rows(row_at, seg_ref, centres, line, band_ref):
    line[...] = jnp.zeros_like(line)
    for i, centre in enumerate(centres):
        own = seg_ref[centre : centre + 1, :]
        for e in range(SPAN):
            at = centre - HALF + e
            keep = jnp.where(seg_ref[at : at + 1, :] == own, 1.0, 0.0)
            for j in range(NCHUNK):
                line[i * SLOT + j : i * SLOT + j + 1, e * CHUNK : (e + 1) * CHUNK] = row_at(i, e, j) * keep
    share = jnp.dot(line[...].astype(bf16), band_ref[...], preferred_element_type=f32)
    results = []
    for i in range(len(centres)):
        part = share[i * SLOT : (i + 1) * SLOT]
        before = jnp.concatenate([jnp.zeros((1, CHUNK), f32), part[:-1, CHUNK:]], axis=0)
        results.append(part[:, :CHUNK] + before)
    return results


def prep_kernel(
    index_ref, edge_ref, halo_ref, sown_ref, taps_hbm, ids_hbm, own_hbm, dft_hbm, lag_hbm,
    source_ref, band_ref, seg_ref, own_ref, dft_ref, lag_ref, taps_ref, ids_ref, line, sems,
):
    loads = start_loads(
        ((taps_hbm, taps_ref), (ids_hbm, ids_ref), (own_hbm, own_ref), (dft_hbm, dft_ref), (lag_hbm, lag_ref)), sems
    )
    device = index_ref[0]
    total = ids_ref.shape[1]
    loads[0].wait()
    wide = jnp.concatenate([taps_ref[...].astype(f32), jnp.zeros((SPAN, 2 * CHUNK - TAPS), f32)], axis=1)
    for e in range(SPAN):
        row = jnp.broadcast_to(wide[e : e + 1, :], (CHUNK, 2 * CHUNK))
        band_ref[e * CHUNK : (e + 1) * CHUNK, :] = pltpu.roll(row, 0, 1, stride=1, stride_axis=0).astype(bf16)

    loads[1].wait()
    ids = jnp.broadcast_to(ids_ref[...].astype(bf16), (CHUNK, total))
    channels = device * CB - HALO + lax.broadcasted_iota(jnp.int32, (ROWS + 2 * HALO, 1), 0)
    channels = jnp.where(channels < 0, channels + total, channels)
    channels = jnp.where(channels >= total, channels - total, channels)
    hit = lax.broadcasted_iota(jnp.int32, (ROWS + 2 * HALO, total), 1) == channels
    seg_ref[...] = lax.dot_general(
        jnp.where(hit, 1.0, 0.0).astype(bf16), ids, (((1,), (1,)), ((), ())), preferred_element_type=f32
    )

    even = device % 2 == 0
    behind = jnp.where(even, halo_ref[:HALO].astype(f32), sown_ref[CB - HALO :].astype(f32))
    first = edge_ref[HALO:].astype(f32)

    def row_at(_, e, j):
        rows, at = (behind, HALO - HALF + e) if e < HALF else (first, e - HALF)
        return chunk(rows, j)[at : at + 1]

    source_ref[...] = filter_rows(row_at, seg_ref, (HALO,), line, band_ref)[0].astype(bf16)
    for load in loads[2:]:
        load.wait()


def partner_kernel(count, index_ref, seg_ref, pseg_ref):
    for k in range(BAND + 1):
        block = seg_ref[HALO + k * CB : HALO + (k + 1) * CB, :]
        turned = jnp.transpose(jnp.concatenate([block, block], axis=0))
        pseg_ref[k : k + 1, :] = jnp.where(index_ref[0] + k < count, turned[:1], -1.0)
    pseg_ref[BAND + 1 :, :] = jnp.full((8 - BAND - 1, CHUNK), -1.0, f32)


def whiten(filt, dft_ref, spec):
    tiles = COVER // CHUNK - 1
    tail = None
    for w in range(W):
        lhs = jnp.concatenate([filt[w * tiles + q] for q in range(tiles + 1)], axis=1)
        raw = jnp.dot(lhs, dft_ref[w], preferred_element_type=f32)
        power = jnp.sum(raw * raw, axis=-1, keepdims=True) * (1.0 / L)
        whitened = raw * lax.rsqrt(power + 1e-06)
        head = whitened[:, :CHUNK] if tail is None else tail + whitened[:, :CHUNK]
        spec[:, w * tiles * CHUNK : (w * tiles + 1) * CHUNK] = head.astype(bf16)
        spec[:, (w * tiles + 1) * CHUNK : (w + 1) * tiles * CHUNK] = whitened[:, CHUNK : tiles * CHUNK].astype(bf16)
        tail = whitened[:, tiles * CHUNK :]
    spec[:, W * tiles * CHUNK :] = tail.astype(bf16)


def spectra_kernel(*refs):
    index_ref, own_ref, two_ref, four_ref, sown_ref, stwo_ref, sfour_ref, halo_ref = refs[:8]
    seg_ref, band_ref, dft_ref, spec, give_ref, near_ref, rec, masked, filt, line = refs[8:]
    even = index_ref[0] % 2 == 0

    def put(start, rows):
        for j in range(NCHUNK):
            rec[j, start : start + rows.shape[0], :] = chunk(rows, j)

    stwo, sfour = stwo_ref[...].astype(f32), sfour_ref[...].astype(f32)
    sown, halo = sown_ref[...].astype(f32), halo_ref[...].astype(f32)
    put(0, jnp.where(even, halo[:HALO], sown[CB - HALO :]))
    put(HALO, own_ref[...].astype(f32))
    put(HALO + CB, jnp.where(even, sown[:HALO], stwo[:HALO]))
    put(2 * CB, jnp.where(even, sown[CB - HALO :], stwo[CB - HALO :]))
    put(HALO + 2 * CB, two_ref[...].astype(f32))
    put(HALO + 3 * CB, jnp.where(even, stwo[:HALO], sfour[:HALO]))
    put(4 * CB, jnp.where(even, stwo[CB - HALO :], sfour[CB - HALO :]))
    put(HALO + 4 * CB, four_ref[...].astype(f32))
    put(HALO + ROWS, jnp.where(even, sfour[:HALO], halo[HALO:]))

    for i in range(NEAR):
        base = 2 * i * CB
        held = masked.at[i % 2]
        centre = seg_ref[base + HALO : base + HALO + CB, :]
        for e in range(SPAN):
            first = base + HALO - HALF + e
            keep = jnp.where(seg_ref[first : first + CB, :] == centre, 1.0, 0.0)
            for j in range(NCHUNK):
                held[j * CB : (j + 1) * CB, e * CHUNK : (e + 1) * CHUNK] = (
                    rec[j, first : first + CB, :] * keep
                ).astype(bf16)
        share = jnp.dot(held[...], band_ref[...], preferred_element_type=f32)
        for j in range(NCHUNK):
            result = share[j * CB : (j + 1) * CB, :CHUNK]
            if j:
                result = result + share[(j - 1) * CB : j * CB, CHUNK:]
            filt[j, i * CB : (i + 1) * CB, :] = result.astype(bf16)

    between = [HALO + r * CB for r in range(1, BAND + 2, 2)]

    def row_at(i, e, j):
        at = between[i] - HALF + e
        return rec[j, at : at + 1, :]

    local = filter_rows(row_at, seg_ref, between, line, band_ref)
    near_ref[...] = jnp.zeros_like(near_ref)
    for r in range(BAND + 2):
        for j in range(NCHUNK):
            if r % 2 == 0:
                near_ref[j, r : r + 1, :] = filt[j, r // 2 * CB : r // 2 * CB + 1, :]
            else:
                near_ref[j, r : r + 1, :] = local[r // 2][j : j + 1].astype(bf16)

    @pl.when(index_ref[0] >= 0)
    def _():
        whiten(filt, dft_ref, spec)

    give_ref[...] = jnp.where(even, spec[CB:, :].astype(f32), spec[: 2 * CB, :].astype(f32)).astype(bf16)


def turn_kernel(count, *refs):
    index_ref, seg_ref, pseg_ref, spec, lag_ref, dft_ref, near_ref = refs[:7]
    part_refs, refs = refs[7:-7], refs[-7:]
    out_ref, src_ref, turned, totals, swapped, filt, ahead_spec = refs
    even = index_ref[0] % 2 == 0

    rows = []
    for ref in part_refs:
        value = ref[...].astype(f32)
        rows += [value[at : at + SLOT] for at in range(0, value.shape[0], SLOT)]
    mine, theirs = rows[::2], rows[1::2]
    lists = count // 2
    skip = lists - len(mine)
    mine, theirs = ([part[0]] + [None] * skip + part[1:] for part in (mine, theirs))
    filt[:, :SLOT, :] = near_ref[...]
    for r in range(BAND + 2, count):
        value = mine[r // 2] if r % 2 == 0 else jnp.where(even, theirs[r // 2], theirs[(r // 2 + 1) % lists])
        for j in range(NCHUNK):
            filt[j, r : r + 1, :] = value[j : j + 1].astype(bf16)
    whiten(filt, dft_ref, ahead_spec)
    row = lax.broadcasted_iota(jnp.int32, (count, count), 0)
    column = lax.broadcasted_iota(jnp.int32, (count, count), 1)
    ahead = row - index_ref[0]
    ahead = jnp.where(ahead < 0, ahead + count, ahead)
    order = jnp.where(ahead == column, 1.0, 0.0).astype(bf16)
    src_ref[...] = jnp.dot(order, ahead_spec[...], preferred_element_type=f32).astype(bf16)

    own = spec[:CB, :].astype(f32)
    pieces = []
    for w in range(W):
        pieces += [own[:, w * L + F : (w + 1) * L], own[:, w * L : w * L + F]]
    swapped[...] = jnp.concatenate(pieces + [jnp.zeros((CB, KP - W * L), f32)], axis=1)
    own_seg = seg_ref[HALO : HALO + CB, :]

    def multiply(step, slot):
        start, first = step * GROUP, step * GROUP * CB
        for at in range(0, KP, CHUNK):
            lanes = slice(at, at + CHUNK)
            straight, crossed = lag_ref[0, start : start + GROUP, lanes], lag_ref[1, start : start + GROUP, lanes]
            own, other = spec[:CB, lanes].astype(f32), swapped[:, lanes]
            for g in range(GROUP):
                turned[first + g * CB : first + (g + 1) * CB, lanes] = (
                    own * straight[g : g + 1, :] + other * crossed[g : g + 1, :]
                ).astype(bf16)
        totals[slot] = lax.dot_general(
            turned[first : first + GROUP * CB, :], spec[...], (((1,), (1,)), ((), ())), preferred_element_type=f32
        )

    def write(step, slot):
        write_pairs(totals.at[slot], step, own_seg, pseg_ref, out_ref, range(0, BAND + 1, 2))

    for step in range(LAGS // GROUP):
        multiply(step, step % 2)
        if step:
            write(step - 1, (step - 1) % 2)
    write(LAGS // GROUP - 1, (LAGS // GROUP - 1) % 2)


def write_pairs(total, step, own_seg, pseg_ref, out_ref, blocks):
    for pair in range(GROUP // 2):
        low, high = 2 * pair * CB, (2 * pair + 1) * CB
        at = step * GROUP * CB + pair * 2 * CB
        lanes = slice(at, at + 2 * CB)
        for i, k in enumerate(blocks):
            both = jnp.concatenate([total[row : row + CB, i * CB : (i + 1) * CB] for row in (low, high)], axis=1)
            keep = own_seg == pseg_ref[k : k + 1, :]
            out_ref[i, :, lanes] = jnp.where(keep, both, 0.0).astype(bf16)


def rest_kernel(
    seg_ref, pseg_ref, turned, take, sources, even_ref, out_hbm, src_ref, odd_ref, totals, others, even_sems, odd_sems
):
    count = sources.shape[0]
    others[: 2 * CB, :] = take[...]
    others[2 * CB :, :] = sources[...]
    early = start_loads(
        tuple((even_ref.at[i], out_hbm.at[k]) for i, k in enumerate(range(0, BAND + 1, 2))), even_sems
    )
    own_seg = seg_ref[HALO : HALO + CB, :]
    steps = LAGS // GROUP

    def store(step, i):
        lanes = pl.ds(step * GROUP * CB, GROUP * CB)
        return pltpu.make_async_copy(
            odd_ref.at[i, :, lanes], out_hbm.at[2 * i + 1, :, lanes], odd_sems.at[step, i]
        )

    def multiply(step, slot):
        first = step * GROUP * CB
        totals[slot] = lax.dot_general(
            turned[first : first + GROUP * CB, :], others[...], (((1,), (1,)), ((), ())), preferred_element_type=f32
        )

    def write(step, slot):
        write_pairs(totals.at[slot], step, own_seg, pseg_ref, odd_ref, range(1, BAND + 1, 2))
        products = jnp.concatenate(
            [totals[slot, g * CB : (g + 1) * CB, 2 * CB :] for g in range(GROUP)], axis=1
        )
        src_ref[:, step * GROUP * count : (step + 1) * GROUP * count] = products.astype(bf16)
        for i in range(BAND // 2):
            store(step, i).start()

    for step in range(steps):
        multiply(step, step % 2)
        if step:
            write(step - 1, (step - 1) % 2)
    write(steps - 1, (steps - 1) % 2)
    for step in range(steps):
        for i in range(BAND // 2):
            store(step, i).wait()
    for load in early:
        load.wait()


VMEM = pl.BlockSpec(memory_space=pltpu.VMEM)
SMEM = pl.BlockSpec(memory_space=pltpu.SMEM)
HBM = pl.BlockSpec(memory_space=pltpu.HBM)


def call(kernel, shapes, scratch, specs, **kwargs):
    return pl.pallas_call(
        kernel, out_shape=shapes, in_specs=specs, out_specs=jax.tree.map(lambda _: VMEM, shapes), scratch_shapes=scratch, **kwargs
    )


def per_device(records, filter_taps, segment_ids):
    count = lax.axis_size("fibre")
    device = lax.axis_index("fibre")

    def ahead(value, distance):
        return lax.ppermute(value, "fibre", [(i, (i - distance) % count) for i in range(count)])

    def swap(value):
        return lax.ppermute(value, "fibre", [(i, i ^ 1) for i in range(count)])

    index = device.reshape(1)
    few = count <= 16
    stay = functools.partial(pltpu.with_memory_space_constraint, memory_space=pltpu.HBM)

    edge = call(
        edge_kernel,
        jax.ShapeDtypeStruct((2 * HALO, W * L), bf16),
        [pltpu.SemaphoreType.DMA((2,))],
        [HBM],
        compiler_params=pltpu.CompilerParams(vmem_limit_bytes=EDGE_LIMIT),
    )(stay(records))
    route = [(i, (i + 1) % count if i % 2 else (i - BAND - 1) % count) for i in range(count)]
    halo = lax.ppermute(edge, "fibre", route)
    sown = swap(records)
    four = ahead(records, 4)
    two = ahead(records, 2)

    dft, lags = dft_tables(), lag_tables()
    source, band, segs, own, dft, lags = call(
        prep_kernel,
        (
            jax.ShapeDtypeStruct((SLOT, CHUNK), bf16),
            jax.ShapeDtypeStruct((SPAN * CHUNK, 2 * CHUNK), bf16),
            jax.ShapeDtypeStruct((ROWS + 2 * HALO, CHUNK), f32),
            jax.ShapeDtypeStruct(records.shape, bf16),
            jax.ShapeDtypeStruct(dft.shape, bf16),
            jax.ShapeDtypeStruct(lags.shape, f32),
        ),
        [
            pltpu.VMEM(filter_taps.shape, bf16),
            pltpu.VMEM((1,) + segment_ids.shape, jnp.int32),
            pltpu.VMEM((SLOT, SPAN * CHUNK), f32),
            pltpu.SemaphoreType.DMA((5,)),
        ],
        [SMEM] + [VMEM] * 3 + [HBM] * 5,
        compiler_params=pltpu.CompilerParams(vmem_limit_bytes=PREP_LIMIT if few else None),
    )(
        index, edge, halo, sown, stay(filter_taps), stay(segment_ids.reshape(1, -1)), stay(records), stay(dft),
        stay(lags),
    )

    lists = count // 2
    pair = jnp.concatenate([source, swap(source)], axis=0)
    first = BAND // 2 + 1 if lists <= 8 else 1
    parts = [pair] + [ahead(pair, 2 * s) for s in range(first, min(8, lists))]
    have = 8
    while have < lists:
        known = jnp.concatenate(parts, axis=0)
        for s in range(1, 8):
            left = lists - s * have
            if left > 0:
                parts.append(ahead(known[: 2 * SLOT * left], 2 * s * have))
        have = min(8 * have, lists)
    pseg = call(
        functools.partial(partner_kernel, count), jax.ShapeDtypeStruct((8, CHUNK), f32), (), [SMEM, VMEM],
        compiler_params=pltpu.CompilerParams(vmem_limit_bytes=TABLE_LIMIT),
    )(index, segs)
    sfour, stwo = swap(four), swap(two)

    limit = pltpu.CompilerParams(vmem_limit_bytes=MAIN_LIMIT if few else None)
    spec, give, near = call(
        spectra_kernel,
        (
            jax.ShapeDtypeStruct((NEAR * CB, KP), bf16),
            jax.ShapeDtypeStruct((2 * CB, KP), bf16),
            jax.ShapeDtypeStruct((NCHUNK, SLOT, CHUNK), bf16),
        ),
        [
            pltpu.VMEM((NCHUNK, ROWS + 2 * HALO, CHUNK), f32),
            pltpu.VMEM((2, NCHUNK * CB, SPAN * CHUNK), bf16),
            pltpu.VMEM((NCHUNK, NEAR * CB, CHUNK), bf16),
            pltpu.VMEM((NEAR * SLOT, SPAN * CHUNK), f32),
        ],
        [SMEM] + [VMEM] * 10,
        compiler_params=limit,
    )(index, own, two, four, sown, stwo, sfour, halo, segs, band, dft)
    take = swap(give)
    even_blocks, sources, turned = call(
        functools.partial(turn_kernel, count),
        (
            jax.ShapeDtypeStruct((NEAR, CB, LAGS * CB), bf16),
            jax.ShapeDtypeStruct((count, KP), bf16),
            jax.ShapeDtypeStruct((LAGS * CB, KP), bf16),
        ),
        [
            pltpu.VMEM((2, GROUP * CB, NEAR * CB), f32),
            pltpu.VMEM((CB, KP), f32),
            pltpu.VMEM((NCHUNK, count, CHUNK), bf16),
            pltpu.VMEM((count, KP), bf16),
        ],
        [SMEM] + [VMEM] * (6 + len(parts)),
        compiler_params=limit,
    )(index, segs, pseg, spec, lags, dft, near, *parts)
    stacked, source_out = pl.pallas_call(
        rest_kernel,
        out_shape=(
            jax.ShapeDtypeStruct((BAND + 1, CB, LAGS * CB), bf16),
            jax.ShapeDtypeStruct((CB, LAGS * count), bf16),
        ),
        in_specs=[VMEM] * 6,
        out_specs=(HBM, VMEM),
        scratch_shapes=[
            pltpu.VMEM((BAND // 2, CB, LAGS * CB), bf16),
            pltpu.VMEM((2, GROUP * CB, 2 * CB + count), f32),
            pltpu.VMEM((2 * CB + count, KP), bf16),
            pltpu.SemaphoreType.DMA((NEAR,)),
            pltpu.SemaphoreType.DMA((LAGS // GROUP, BAND // 2)),
        ],
        compiler_params=limit,
    )(segs, pseg, turned, take, sources, even_blocks)
    return (jnp.swapaxes(stacked, 0, 1), source_out)


def solution(mesh):
    return jax.shard_map(
        per_device,
        mesh=mesh,
        in_specs=(P(("runs", "fibre"), None), P(), P("runs")),
        out_specs=(P(("runs", "fibre"), None, None), P(("runs", "fibre"), None)),
        check_vma=False,
    )
```

```python
import functools

import jax
import jax.numpy as jnp
import numpy as np
from jax import lax
from jax.experimental import pallas as pl
from jax.experimental.pallas import tpu as pltpu
from jax.sharding import PartitionSpec as P


CB = 64
W = 4
F = 200
L = 400
TAPS = 63
SPAN = 9
LAGS = 32
BAND = 4
HALF = (SPAN - 1) // 2
SLOT = 16
HALO = 8
CHUNK = 128
NCHUNK = -(-W * L // CHUNK)
KP = -(-W * L // CHUNK) * CHUNK
ROWS = (BAND + 1) * CB
NEAR = BAND // 2 + 1
GROUP = 8
SHIFT = L % CHUNK
COVER = 4 * CHUNK

MAIN_LIMIT = 20 << 20
PREP_LIMIT = 12 << 20
EDGE_LIMIT = 1 << 20
TABLE_LIMIT = 2 << 20

f32 = jnp.float32
bf16 = jnp.bfloat16


def dft_tables():
    t = np.arange(L)
    taper = 0.5 - 0.5 * np.cos((t + 0.5) * (2.0 * np.pi / L))
    phase = (t[:, None] * np.arange(F)[None, :] % L) * (2.0 * np.pi / L)
    table = np.concatenate([taper[:, None] * np.cos(phase), -taper[:, None] * np.sin(phase)], axis=1)
    tables = np.zeros((W, COVER, COVER))
    for w in range(W):
        tables[w, w * SHIFT : w * SHIFT + L, w * SHIFT : w * SHIFT + L] = table
    return jnp.asarray(tables.astype(np.float32), bf16)


def lag_tables():
    m = np.arange(LAGS) - LAGS // 2
    phase = (m[:, None] * np.arange(F)[None, :] % L) * (2.0 * np.pi / L)
    scale = 1.0 / np.sqrt(2.0 * L)
    straight, crossed = np.cos(phase) * scale, -np.sin(phase) * scale
    tables = np.zeros((2, LAGS, KP))
    tables[0, :, : W * L] = np.tile(np.concatenate([straight, straight], axis=1), (1, W))
    tables[1, :, : W * L] = np.tile(np.concatenate([crossed, -crossed], axis=1), (1, W))
    return jnp.asarray(tables.astype(np.float32), bf16).astype(f32)


def start_loads(pairs, sems):
    loads = [pltpu.make_async_copy(source, target, sems.at[i]) for i, (source, target) in enumerate(pairs)]
    for load in loads:
        load.start()
    return loads


def edge_kernel(own_hbm, edge_ref, sems):
    last = (own_hbm.at[pl.ds(CB - HALO, HALO)], edge_ref.at[pl.ds(0, HALO)])
    first = (own_hbm.at[pl.ds(0, HALO)], edge_ref.at[pl.ds(HALO, HALO)])
    for load in start_loads((last, first), sems):
        load.wait()


def chunk(rows, j):
    piece = rows[:, j * CHUNK : min((j + 1) * CHUNK, W * L)]
    if piece.shape[1] < CHUNK:
        piece = jnp.concatenate([piece, jnp.zeros((piece.shape[0], CHUNK - piece.shape[1]), piece.dtype)], axis=1)
    return piece


def filter_rows(row_at, seg_ref, centres, line, band_ref):
    line[...] = jnp.zeros_like(line)
    for i, centre in enumerate(centres):
        own = seg_ref[centre : centre + 1, :]
        for e in range(SPAN):
            at = centre - HALF + e
            keep = jnp.where(seg_ref[at : at + 1, :] == own, 1.0, 0.0)
            for j in range(NCHUNK):
                line[i * SLOT + j : i * SLOT + j + 1, e * CHUNK : (e + 1) * CHUNK] = row_at(i, e, j) * keep
    share = jnp.dot(line[...].astype(bf16), band_ref[...], preferred_element_type=f32)
    results = []
    for i in range(len(centres)):
        part = share[i * SLOT : (i + 1) * SLOT]
        before = jnp.concatenate([jnp.zeros((1, CHUNK), f32), part[:-1, CHUNK:]], axis=0)
        results.append(part[:, :CHUNK] + before)
    return results


def prep_kernel(
    index_ref, edge_ref, halo_ref, sown_ref, taps_hbm, ids_hbm, own_hbm, dft_hbm, lag_hbm,
    source_ref, band_ref, seg_ref, own_ref, dft_ref, lag_ref, taps_ref, ids_ref, line, sems,
):
    loads = start_loads(
        ((taps_hbm, taps_ref), (ids_hbm, ids_ref), (own_hbm, own_ref), (dft_hbm, dft_ref), (lag_hbm, lag_ref)), sems
    )
    device = index_ref[0]
    total = ids_ref.shape[1]
    loads[0].wait()
    wide = jnp.concatenate([taps_ref[...].astype(f32), jnp.zeros((SPAN, 2 * CHUNK - TAPS), f32)], axis=1)
    for e in range(SPAN):
        row = jnp.broadcast_to(wide[e : e + 1, :], (CHUNK, 2 * CHUNK))
        band_ref[e * CHUNK : (e + 1) * CHUNK, :] = pltpu.roll(row, 0, 1, stride=1, stride_axis=0).astype(bf16)

    loads[1].wait()
    ids = jnp.broadcast_to(ids_ref[...].astype(bf16), (CHUNK, total))
    channels = device * CB - HALO + lax.broadcasted_iota(jnp.int32, (ROWS + 2 * HALO, 1), 0)
    channels = jnp.where(channels < 0, channels + total, channels)
    channels = jnp.where(channels >= total, channels - total, channels)
    hit = lax.broadcasted_iota(jnp.int32, (ROWS + 2 * HALO, total), 1) == channels
    seg_ref[...] = lax.dot_general(
        jnp.where(hit, 1.0, 0.0).astype(bf16), ids, (((1,), (1,)), ((), ())), preferred_element_type=f32
    )

    even = device % 2 == 0
    behind = jnp.where(even, halo_ref[:HALO].astype(f32), sown_ref[CB - HALO :].astype(f32))
    first = edge_ref[HALO:].astype(f32)

    def row_at(_, e, j):
        rows, at = (behind, HALO - HALF + e) if e < HALF else (first, e - HALF)
        return chunk(rows, j)[at : at + 1]

    source_ref[...] = filter_rows(row_at, seg_ref, (HALO,), line, band_ref)[0].astype(bf16)
    for load in loads[2:]:
        load.wait()


def partner_kernel(count, index_ref, seg_ref, pseg_ref):
    for k in range(BAND + 1):
        block = seg_ref[HALO + k * CB : HALO + (k + 1) * CB, :]
        turned = jnp.transpose(jnp.concatenate([block, block], axis=0))
        pseg_ref[k : k + 1, :] = jnp.where(index_ref[0] + k < count, turned[:1], -1.0)
    pseg_ref[BAND + 1 :, :] = jnp.full((8 - BAND - 1, CHUNK), -1.0, f32)


def whiten(filt, dft_ref, spec):
    tiles = COVER // CHUNK - 1
    tail = None
    for w in range(W):
        lhs = jnp.concatenate([filt[w * tiles + q] for q in range(tiles + 1)], axis=1)
        raw = jnp.dot(lhs, dft_ref[w], preferred_element_type=f32)
        power = jnp.sum(raw * raw, axis=-1, keepdims=True) * (1.0 / L)
        whitened = raw * lax.rsqrt(power + 1e-06)
        head = whitened[:, :CHUNK] if tail is None else tail + whitened[:, :CHUNK]
        spec[:, w * tiles * CHUNK : (w * tiles + 1) * CHUNK] = head.astype(bf16)
        spec[:, (w * tiles + 1) * CHUNK : (w + 1) * tiles * CHUNK] = whitened[:, CHUNK : tiles * CHUNK].astype(bf16)
        tail = whitened[:, tiles * CHUNK :]
    spec[:, W * tiles * CHUNK :] = tail.astype(bf16)


def spectra_kernel(*refs):
    index_ref, own_ref, two_ref, four_ref, sown_ref, stwo_ref, sfour_ref, halo_ref = refs[:8]
    seg_ref, band_ref, dft_ref, spec, give_ref, rec, masked, filt = refs[8:]
    even = index_ref[0] % 2 == 0

    def put(start, rows):
        for j in range(NCHUNK):
            rec[j, start : start + rows.shape[0], :] = chunk(rows, j)

    stwo, sfour = stwo_ref[...].astype(f32), sfour_ref[...].astype(f32)
    sown, halo = sown_ref[...].astype(f32), halo_ref[...].astype(f32)
    put(0, jnp.where(even, halo[:HALO], sown[CB - HALO :]))
    put(HALO, own_ref[...].astype(f32))
    put(HALO + CB, jnp.where(even, sown[:HALO], stwo[:HALO]))
    put(2 * CB, jnp.where(even, sown[CB - HALO :], stwo[CB - HALO :]))
    put(HALO + 2 * CB, two_ref[...].astype(f32))
    put(HALO + 3 * CB, jnp.where(even, stwo[:HALO], sfour[:HALO]))
    put(4 * CB, jnp.where(even, stwo[CB - HALO :], sfour[CB - HALO :]))
    put(HALO + 4 * CB, four_ref[...].astype(f32))
    put(HALO + ROWS, jnp.where(even, sfour[:HALO], halo[HALO:]))

    for i in range(NEAR):
        base = 2 * i * CB
        held = masked.at[i % 2]
        centre = seg_ref[base + HALO : base + HALO + CB, :]
        for e in range(SPAN):
            first = base + HALO - HALF + e
            keep = jnp.where(seg_ref[first : first + CB, :] == centre, 1.0, 0.0)
            for j in range(NCHUNK):
                held[j * CB : (j + 1) * CB, e * CHUNK : (e + 1) * CHUNK] = (
                    rec[j, first : first + CB, :] * keep
                ).astype(bf16)
        share = jnp.dot(held[...], band_ref[...], preferred_element_type=f32)
        for j in range(NCHUNK):
            result = share[j * CB : (j + 1) * CB, :CHUNK]
            if j:
                result = result + share[(j - 1) * CB : j * CB, CHUNK:]
            filt[j, i * CB : (i + 1) * CB, :] = result.astype(bf16)

    @pl.when(index_ref[0] >= 0)
    def _():
        whiten(filt, dft_ref, spec)

    give_ref[...] = jnp.where(even, spec[CB:, :].astype(f32), spec[: 2 * CB, :].astype(f32)).astype(bf16)


def turn_kernel(
    doubled, index_ref, seg_ref, pseg_ref, spec, lag_ref, dft_ref, low_ref, high_ref,
    out_ref, src_ref, turned, totals, swapped, filt, found,
):
    count = filt.shape[1]
    for q in range(count):
        ref, at = (low_ref, q * SLOT) if 2 * q < count else (high_ref, q * SLOT - low_ref.shape[0])
        rows = ref[at : at + SLOT, :].astype(f32)
        for j in range(NCHUNK):
            filt[j, q : q + 1, :] = rows[j : j + 1].astype(bf16)
    whiten(filt, dft_ref, found)
    row = lax.broadcasted_iota(jnp.int32, (count, count), 0)
    column = lax.broadcasted_iota(jnp.int32, (count, count), 1)
    if doubled:
        row = jnp.bitwise_xor(row, index_ref[0])
    order = jnp.where(row == column, 1.0, 0.0).astype(bf16)
    src_ref[...] = jnp.dot(order, found[...], preferred_element_type=f32).astype(bf16)

    own = spec[:CB, :].astype(f32)
    pieces = []
    for w in range(W):
        pieces += [own[:, w * L + F : (w + 1) * L], own[:, w * L : w * L + F]]
    swapped[...] = jnp.concatenate(pieces + [jnp.zeros((CB, KP - W * L), f32)], axis=1)
    own_seg = seg_ref[HALO : HALO + CB, :]

    def multiply(step, slot):
        start, first = step * GROUP, step * GROUP * CB
        for at in range(0, KP, CHUNK):
            lanes = slice(at, at + CHUNK)
            straight, crossed = lag_ref[0, start : start + GROUP, lanes], lag_ref[1, start : start + GROUP, lanes]
            own, other = spec[:CB, lanes].astype(f32), swapped[:, lanes]
            for g in range(GROUP):
                turned[first + g * CB : first + (g + 1) * CB, lanes] = (
                    own * straight[g : g + 1, :] + other * crossed[g : g + 1, :]
                ).astype(bf16)
        totals[slot] = lax.dot_general(
            turned[first : first + GROUP * CB, :], spec[...], (((1,), (1,)), ((), ())), preferred_element_type=f32
        )

    def write(step, slot):
        write_pairs(totals.at[slot], step, own_seg, pseg_ref, out_ref, range(0, BAND + 1, 2))

    for step in range(LAGS // GROUP):
        multiply(step, step % 2)
        if step:
            write(step - 1, (step - 1) % 2)
    write(LAGS // GROUP - 1, (LAGS // GROUP - 1) % 2)


def write_pairs(total, step, own_seg, pseg_ref, out_ref, blocks):
    for pair in range(GROUP // 2):
        low, high = 2 * pair * CB, (2 * pair + 1) * CB
        at = step * GROUP * CB + pair * 2 * CB
        lanes = slice(at, at + 2 * CB)
        for i, k in enumerate(blocks):
            both = jnp.concatenate([total[row : row + CB, i * CB : (i + 1) * CB] for row in (low, high)], axis=1)
            keep = own_seg == pseg_ref[k : k + 1, :]
            out_ref[i, :, lanes] = jnp.where(keep, both, 0.0).astype(bf16)


def rest_kernel(
    seg_ref, pseg_ref, turned, take, sources, even_ref, out_hbm, src_hbm,
    odd_ref, src_ref, totals, others, even_sems, odd_sems, src_sems,
):
    count = sources.shape[0]
    others[: 2 * CB, :] = take[...]
    others[2 * CB :, :] = sources[...]
    early = start_loads(
        tuple((even_ref.at[i], out_hbm.at[k]) for i, k in enumerate(range(0, BAND + 1, 2))), even_sems
    )
    own_seg = seg_ref[HALO : HALO + CB, :]
    steps = LAGS // GROUP

    def store(step, i):
        lanes = pl.ds(step * GROUP * CB, GROUP * CB)
        return pltpu.make_async_copy(
            odd_ref.at[i, :, lanes], out_hbm.at[2 * i + 1, :, lanes], odd_sems.at[step, i]
        )

    def store_sources(step):
        lanes = pl.ds(step * GROUP * count, GROUP * count)
        return pltpu.make_async_copy(src_ref.at[:, lanes], src_hbm.at[:, lanes], src_sems.at[step])

    def multiply(step, slot):
        first = step * GROUP * CB
        totals[slot] = lax.dot_general(
            turned[first : first + GROUP * CB, :], others[...], (((1,), (1,)), ((), ())), preferred_element_type=f32
        )

    def write(step, slot):
        write_pairs(totals.at[slot], step, own_seg, pseg_ref, odd_ref, range(1, BAND + 1, 2))
        products = jnp.concatenate(
            [totals[slot, g * CB : (g + 1) * CB, 2 * CB :] for g in range(GROUP)], axis=1
        )
        src_ref[:, step * GROUP * count : (step + 1) * GROUP * count] = products.astype(bf16)
        for i in range(BAND // 2):
            store(step, i).start()
        store_sources(step).start()

    for step in range(steps):
        multiply(step, step % 2)
        if step:
            write(step - 1, (step - 1) % 2)
    write(steps - 1, (steps - 1) % 2)
    for step in range(steps):
        for i in range(BAND // 2):
            store(step, i).wait()
        store_sources(step).wait()
    for load in early:
        load.wait()


VMEM = pl.BlockSpec(memory_space=pltpu.VMEM)
SMEM = pl.BlockSpec(memory_space=pltpu.SMEM)
HBM = pl.BlockSpec(memory_space=pltpu.HBM)


def call(kernel, shapes, scratch, specs, **kwargs):
    return pl.pallas_call(
        kernel, out_shape=shapes, in_specs=specs, out_specs=jax.tree.map(lambda _: VMEM, shapes), scratch_shapes=scratch, **kwargs
    )


def per_device(records, filter_taps, segment_ids):
    count = lax.axis_size("fibre")
    device = lax.axis_index("fibre")

    def ahead(value, distance):
        return lax.ppermute(value, "fibre", [(i, (i - distance) % count) for i in range(count)])

    def swap(value):
        return lax.ppermute(value, "fibre", [(i, i ^ 1) for i in range(count)])

    index = device.reshape(1)
    few = count <= 16
    stay = functools.partial(pltpu.with_memory_space_constraint, memory_space=pltpu.HBM)

    edge = call(
        edge_kernel,
        jax.ShapeDtypeStruct((2 * HALO, W * L), bf16),
        [pltpu.SemaphoreType.DMA((2,))],
        [HBM],
        compiler_params=pltpu.CompilerParams(vmem_limit_bytes=EDGE_LIMIT),
    )(stay(records))
    route = [(i, (i + 1) % count if i % 2 else (i - BAND - 1) % count) for i in range(count)]
    halo = lax.ppermute(edge, "fibre", route)
    sown = swap(records)
    four = ahead(records, 4)
    two = ahead(records, 2)

    dft, lags = dft_tables(), lag_tables()
    source, band, segs, own, dft, lags = call(
        prep_kernel,
        (
            jax.ShapeDtypeStruct((SLOT, CHUNK), bf16),
            jax.ShapeDtypeStruct((SPAN * CHUNK, 2 * CHUNK), bf16),
            jax.ShapeDtypeStruct((ROWS + 2 * HALO, CHUNK), f32),
            jax.ShapeDtypeStruct(records.shape, bf16),
            jax.ShapeDtypeStruct(dft.shape, bf16),
            jax.ShapeDtypeStruct(lags.shape, f32),
        ),
        [
            pltpu.VMEM(filter_taps.shape, bf16),
            pltpu.VMEM((1,) + segment_ids.shape, jnp.int32),
            pltpu.VMEM((SLOT, SPAN * CHUNK), f32),
            pltpu.SemaphoreType.DMA((5,)),
        ],
        [SMEM] + [VMEM] * 3 + [HBM] * 5,
        compiler_params=pltpu.CompilerParams(vmem_limit_bytes=PREP_LIMIT if few else None),
    )(
        index, edge, halo, sown, stay(filter_taps), stay(segment_ids.reshape(1, -1)), stay(records), stay(dft),
        stay(lags),
    )

    doubled = count & (count - 1) == 0
    if doubled:
        rows, bit = source, 1
        while bit < count:
            other = lax.ppermute(rows, "fibre", [(i, i ^ bit) for i in range(count)])
            halves = (rows, other)
            if 2 * bit < count:
                rows = jnp.concatenate(halves, axis=0)
            bit *= 2
    else:
        halves = jnp.split(lax.all_gather(source, "fibre", axis=0, tiled=True), 2, axis=0)
    pseg = call(
        functools.partial(partner_kernel, count), jax.ShapeDtypeStruct((8, CHUNK), f32), (), [SMEM, VMEM],
        compiler_params=pltpu.CompilerParams(vmem_limit_bytes=TABLE_LIMIT),
    )(index, segs)
    sfour, stwo = swap(four), swap(two)

    limit = pltpu.CompilerParams(vmem_limit_bytes=MAIN_LIMIT if few else None)
    spec, give = call(
        spectra_kernel,
        (
            jax.ShapeDtypeStruct((NEAR * CB, KP), bf16),
            jax.ShapeDtypeStruct((2 * CB, KP), bf16),
        ),
        [
            pltpu.VMEM((NCHUNK, ROWS + 2 * HALO, CHUNK), f32),
            pltpu.VMEM((2, NCHUNK * CB, SPAN * CHUNK), bf16),
            pltpu.VMEM((NCHUNK, NEAR * CB, CHUNK), bf16),
        ],
        [SMEM] + [VMEM] * 10,
        compiler_params=limit,
    )(index, own, two, four, sown, stwo, sfour, halo, segs, band, dft)
    take = swap(give)
    even_blocks, sources, turned = call(
        functools.partial(turn_kernel, doubled),
        (
            jax.ShapeDtypeStruct((NEAR, CB, LAGS * CB), bf16),
            jax.ShapeDtypeStruct((count, KP), bf16),
            jax.ShapeDtypeStruct((LAGS * CB, KP), bf16),
        ),
        [
            pltpu.VMEM((2, GROUP * CB, NEAR * CB), f32),
            pltpu.VMEM((CB, KP), f32),
            pltpu.VMEM((NCHUNK, count, CHUNK), bf16),
            pltpu.VMEM((count, KP), bf16),
        ],
        [SMEM] + [VMEM] * 7,
        compiler_params=limit,
    )(index, segs, pseg, spec, lags, dft, *halves)
    stacked, source_out = pl.pallas_call(
        rest_kernel,
        out_shape=(
            jax.ShapeDtypeStruct((BAND + 1, CB, LAGS * CB), bf16),
            jax.ShapeDtypeStruct((CB, LAGS * count), bf16),
        ),
        in_specs=[VMEM] * 6,
        out_specs=(HBM, HBM),
        scratch_shapes=[
            pltpu.VMEM((BAND // 2, CB, LAGS * CB), bf16),
            pltpu.VMEM((CB, LAGS * count), bf16),
            pltpu.VMEM((2, GROUP * CB, 2 * CB + count), f32),
            pltpu.VMEM((2 * CB + count, KP), bf16),
            pltpu.SemaphoreType.DMA((NEAR,)),
            pltpu.SemaphoreType.DMA((LAGS // GROUP, BAND // 2)),
            pltpu.SemaphoreType.DMA((LAGS // GROUP,)),
        ],
        compiler_params=limit,
    )(segs, pseg, turned, take, sources, even_blocks)
    return (jnp.swapaxes(stacked, 0, 1), source_out)


def solution(mesh):
    return jax.shard_map(
        per_device,
        mesh=mesh,
        in_specs=(P(("runs", "fibre"), None), P(), P("runs")),
        out_specs=(P(("runs", "fibre"), None, None), P(("runs", "fibre"), None)),
        check_vma=False,
    )
```

```python
import functools

import jax
import jax.numpy as jnp
import numpy as np
from jax import lax
from jax.experimental import pallas as pl
from jax.experimental.pallas import tpu as pltpu
from jax.sharding import PartitionSpec as P


CB = 64
W = 4
F = 200
L = 400
TAPS = 63
SPAN = 9
LAGS = 32
BAND = 4
HALF = (SPAN - 1) // 2
SLOT = 16
HALO = 8
CHUNK = 128
NCHUNK = -(-W * L // CHUNK)
KP = -(-W * L // CHUNK) * CHUNK
ROWS = (BAND + 1) * CB
NEAR = BAND // 2 + 1
GROUP = 8
SHIFT = L % CHUNK
COVER = 4 * CHUNK

MAIN_LIMIT = 20 << 20
PREP_LIMIT = 12 << 20
EDGE_LIMIT = 1 << 20
TABLE_LIMIT = 2 << 20

f32 = jnp.float32
bf16 = jnp.bfloat16


def dft_tables():
    t = np.arange(L)
    taper = 0.5 - 0.5 * np.cos((t + 0.5) * (2.0 * np.pi / L))
    phase = (t[:, None] * np.arange(F)[None, :] % L) * (2.0 * np.pi / L)
    table = np.concatenate([taper[:, None] * np.cos(phase), -taper[:, None] * np.sin(phase)], axis=1)
    tables = np.zeros((W, COVER, COVER))
    for w in range(W):
        tables[w, w * SHIFT : w * SHIFT + L, w * SHIFT : w * SHIFT + L] = table
    return jnp.asarray(tables.astype(np.float32), bf16)


def lag_tables():
    m = np.arange(LAGS) - LAGS // 2
    phase = (m[:, None] * np.arange(F)[None, :] % L) * (2.0 * np.pi / L)
    scale = 1.0 / np.sqrt(2.0 * L)
    straight, crossed = np.cos(phase) * scale, -np.sin(phase) * scale
    tables = np.zeros((2, LAGS, KP))
    tables[0, :, : W * L] = np.tile(np.concatenate([straight, straight], axis=1), (1, W))
    tables[1, :, : W * L] = np.tile(np.concatenate([crossed, -crossed], axis=1), (1, W))
    return jnp.asarray(tables.astype(np.float32), bf16).astype(f32)


def start_loads(pairs, sems):
    loads = [pltpu.make_async_copy(source, target, sems.at[i]) for i, (source, target) in enumerate(pairs)]
    for load in loads:
        load.start()
    return loads


def edge_kernel(own_hbm, edge_ref, sems):
    last = (own_hbm.at[pl.ds(CB - HALO, HALO)], edge_ref.at[pl.ds(0, HALO)])
    first = (own_hbm.at[pl.ds(0, HALO)], edge_ref.at[pl.ds(HALO, HALO)])
    for load in start_loads((last, first), sems):
        load.wait()


def chunk(rows, j):
    piece = rows[:, j * CHUNK : min((j + 1) * CHUNK, W * L)]
    if piece.shape[1] < CHUNK:
        piece = jnp.concatenate([piece, jnp.zeros((piece.shape[0], CHUNK - piece.shape[1]), piece.dtype)], axis=1)
    return piece


def filter_rows(row_at, seg_ref, centres, line, band_ref):
    line[...] = jnp.zeros_like(line)
    for i, centre in enumerate(centres):
        own = seg_ref[centre : centre + 1, :]
        for e in range(SPAN):
            at = centre - HALF + e
            keep = jnp.where(seg_ref[at : at + 1, :] == own, 1.0, 0.0)
            for j in range(NCHUNK):
                line[i * SLOT + j : i * SLOT + j + 1, e * CHUNK : (e + 1) * CHUNK] = row_at(i, e, j) * keep
    share = jnp.dot(line[...].astype(bf16), band_ref[...], preferred_element_type=f32)
    results = []
    for i in range(len(centres)):
        part = share[i * SLOT : (i + 1) * SLOT]
        before = jnp.concatenate([jnp.zeros((1, CHUNK), f32), part[:-1, CHUNK:]], axis=0)
        results.append(part[:, :CHUNK] + before)
    return results


def prep_kernel(
    index_ref, edge_ref, halo_ref, sown_ref, taps_hbm, ids_hbm, own_hbm, dft_hbm, lag_hbm,
    source_ref, band_ref, seg_ref, own_ref, dft_ref, lag_ref, taps_ref, ids_ref, line, sems,
):
    loads = start_loads(
        ((taps_hbm, taps_ref), (ids_hbm, ids_ref), (own_hbm, own_ref), (dft_hbm, dft_ref), (lag_hbm, lag_ref)), sems
    )
    device = index_ref[0]
    total = ids_ref.shape[1]
    loads[0].wait()
    wide = jnp.concatenate([taps_ref[...].astype(f32), jnp.zeros((SPAN, 2 * CHUNK - TAPS), f32)], axis=1)
    for e in range(SPAN):
        row = jnp.broadcast_to(wide[e : e + 1, :], (CHUNK, 2 * CHUNK))
        band_ref[e * CHUNK : (e + 1) * CHUNK, :] = pltpu.roll(row, 0, 1, stride=1, stride_axis=0).astype(bf16)

    loads[1].wait()
    ids = jnp.broadcast_to(ids_ref[...].astype(bf16), (CHUNK, total))
    channels = device * CB - HALO + lax.broadcasted_iota(jnp.int32, (ROWS + 2 * HALO, 1), 0)
    channels = jnp.where(channels < 0, channels + total, channels)
    channels = jnp.where(channels >= total, channels - total, channels)
    hit = lax.broadcasted_iota(jnp.int32, (ROWS + 2 * HALO, total), 1) == channels
    seg_ref[...] = lax.dot_general(
        jnp.where(hit, 1.0, 0.0).astype(bf16), ids, (((1,), (1,)), ((), ())), preferred_element_type=f32
    )

    even = device % 2 == 0
    behind = jnp.where(even, halo_ref[:HALO].astype(f32), sown_ref[CB - HALO :].astype(f32))
    first = edge_ref[HALO:].astype(f32)

    def row_at(_, e, j):
        rows, at = (behind, HALO - HALF + e) if e < HALF else (first, e - HALF)
        return chunk(rows, j)[at : at + 1]

    source_ref[...] = filter_rows(row_at, seg_ref, (HALO,), line, band_ref)[0].astype(bf16)
    for load in loads[2:]:
        load.wait()


def partner_kernel(count, index_ref, seg_ref, pseg_ref):
    for k in range(BAND + 1):
        block = seg_ref[HALO + k * CB : HALO + (k + 1) * CB, :]
        turned = jnp.transpose(jnp.concatenate([block, block], axis=0))
        pseg_ref[k : k + 1, :] = jnp.where(index_ref[0] + k < count, turned[:1], -1.0)
    pseg_ref[BAND + 1 :, :] = jnp.full((8 - BAND - 1, CHUNK), -1.0, f32)


def whiten(filt, dft_ref, spec):
    tiles = COVER // CHUNK - 1
    tail = None
    for w in range(W):
        lhs = jnp.concatenate([filt[w * tiles + q] for q in range(tiles + 1)], axis=1)
        raw = jnp.dot(lhs, dft_ref[w], preferred_element_type=f32)
        power = jnp.sum(raw * raw, axis=-1, keepdims=True) * (1.0 / L)
        whitened = raw * lax.rsqrt(power + 1e-06)
        head = whitened[:, :CHUNK] if tail is None else tail + whitened[:, :CHUNK]
        spec[:, w * tiles * CHUNK : (w * tiles + 1) * CHUNK] = head.astype(bf16)
        spec[:, (w * tiles + 1) * CHUNK : (w + 1) * tiles * CHUNK] = whitened[:, CHUNK : tiles * CHUNK].astype(bf16)
        tail = whitened[:, tiles * CHUNK :]
    spec[:, W * tiles * CHUNK :] = tail.astype(bf16)


def spectra_kernel(*refs):
    index_ref, own_ref, two_ref, four_ref, sown_ref, stwo_ref, sfour_ref, halo_ref = refs[:8]
    seg_ref, band_ref, dft_ref, spec, give_ref, rec, masked, filt = refs[8:]
    even = index_ref[0] % 2 == 0

    def put(start, rows):
        for j in range(NCHUNK):
            rec[j, start : start + rows.shape[0], :] = chunk(rows, j)

    stwo, sfour = stwo_ref[...].astype(f32), sfour_ref[...].astype(f32)
    sown, halo = sown_ref[...].astype(f32), halo_ref[...].astype(f32)
    put(0, jnp.where(even, halo[:HALO], sown[CB - HALO :]))
    put(HALO, own_ref[...].astype(f32))
    put(HALO + CB, jnp.where(even, sown[:HALO], stwo[:HALO]))
    put(2 * CB, jnp.where(even, sown[CB - HALO :], stwo[CB - HALO :]))
    put(HALO + 2 * CB, two_ref[...].astype(f32))
    put(HALO + 3 * CB, jnp.where(even, stwo[:HALO], sfour[:HALO]))
    put(4 * CB, jnp.where(even, stwo[CB - HALO :], sfour[CB - HALO :]))
    put(HALO + 4 * CB, four_ref[...].astype(f32))
    put(HALO + ROWS, jnp.where(even, sfour[:HALO], halo[HALO:]))

    for i in range(NEAR):
        base = 2 * i * CB
        held = masked.at[i % 2]
        centre = seg_ref[base + HALO : base + HALO + CB, :]
        for e in range(SPAN):
            first = base + HALO - HALF + e
            keep = jnp.where(seg_ref[first : first + CB, :] == centre, 1.0, 0.0)
            for j in range(NCHUNK):
                held[j * CB : (j + 1) * CB, e * CHUNK : (e + 1) * CHUNK] = (
                    rec[j, first : first + CB, :] * keep
                ).astype(bf16)
        share = jnp.dot(held[...], band_ref[...], preferred_element_type=f32)
        for j in range(NCHUNK):
            result = share[j * CB : (j + 1) * CB, :CHUNK]
            if j:
                result = result + share[(j - 1) * CB : j * CB, CHUNK:]
            filt[j, i * CB : (i + 1) * CB, :] = result.astype(bf16)

    @pl.when(index_ref[0] >= 0)
    def _():
        whiten(filt, dft_ref, spec)

    give_ref[...] = jnp.where(even, spec[CB:, :].astype(f32), spec[: 2 * CB, :].astype(f32)).astype(bf16)


def turn_kernel(seg_ref, pseg_ref, spec, lag_ref, out_ref, turned, totals, swapped):
    own = spec[:CB, :].astype(f32)
    pieces = []
    for w in range(W):
        pieces += [own[:, w * L + F : (w + 1) * L], own[:, w * L : w * L + F]]
    swapped[...] = jnp.concatenate(pieces + [jnp.zeros((CB, KP - W * L), f32)], axis=1)
    own_seg = seg_ref[HALO : HALO + CB, :]

    def multiply(step, slot):
        start, first = step * GROUP, step * GROUP * CB
        for at in range(0, KP, CHUNK):
            lanes = slice(at, at + CHUNK)
            straight, crossed = lag_ref[0, start : start + GROUP, lanes], lag_ref[1, start : start + GROUP, lanes]
            own, other = spec[:CB, lanes].astype(f32), swapped[:, lanes]
            for g in range(GROUP):
                turned[first + g * CB : first + (g + 1) * CB, lanes] = (
                    own * straight[g : g + 1, :] + other * crossed[g : g + 1, :]
                ).astype(bf16)
        totals[slot] = lax.dot_general(
            turned[first : first + GROUP * CB, :], spec[...], (((1,), (1,)), ((), ())), preferred_element_type=f32
        )

    def write(step, slot):
        write_pairs(totals.at[slot], step, own_seg, pseg_ref, out_ref, range(0, BAND + 1, 2))

    for step in range(LAGS // GROUP):
        multiply(step, step % 2)
        if step:
            write(step - 1, (step - 1) % 2)
    write(LAGS // GROUP - 1, (LAGS // GROUP - 1) % 2)


def write_pairs(total, step, own_seg, pseg_ref, out_ref, blocks):
    for pair in range(GROUP // 2):
        low, high = 2 * pair * CB, (2 * pair + 1) * CB
        at = step * GROUP * CB + pair * 2 * CB
        lanes = slice(at, at + 2 * CB)
        for i, k in enumerate(blocks):
            both = jnp.concatenate([total[row : row + CB, i * CB : (i + 1) * CB] for row in (low, high)], axis=1)
            keep = own_seg == pseg_ref[k : k + 1, :]
            out_ref[i, :, lanes] = jnp.where(keep, both, 0.0).astype(bf16)


def rest_kernel(
    doubled, index_ref, seg_ref, pseg_ref, turned, take, dft_ref, low_ref, high_ref, even_ref, out_hbm, src_hbm,
    odd_ref, src_ref, totals, others, filt, found, even_sems, odd_sems, src_sems,
):
    early = start_loads(
        tuple((even_ref.at[i], out_hbm.at[k]) for i, k in enumerate(range(0, BAND + 1, 2))), even_sems
    )
    count = filt.shape[1]
    for q in range(count):
        ref, at = (low_ref, q * SLOT) if 2 * q < count else (high_ref, q * SLOT - low_ref.shape[0])
        rows = ref[at : at + SLOT, :].astype(f32)
        for j in range(NCHUNK):
            filt[j, q : q + 1, :] = rows[j : j + 1].astype(bf16)
    whiten(filt, dft_ref, found)
    row = lax.broadcasted_iota(jnp.int32, (count, count), 0)
    column = lax.broadcasted_iota(jnp.int32, (count, count), 1)
    if doubled:
        row = jnp.bitwise_xor(row, index_ref[0])
    order = jnp.where(row == column, 1.0, 0.0).astype(bf16)
    others[2 * CB :, :] = jnp.dot(order, found[...], preferred_element_type=f32).astype(bf16)
    others[: 2 * CB, :] = take[...]
    own_seg = seg_ref[HALO : HALO + CB, :]
    steps = LAGS // GROUP

    def store(step, i):
        lanes = pl.ds(step * GROUP * CB, GROUP * CB)
        return pltpu.make_async_copy(
            odd_ref.at[i, :, lanes], out_hbm.at[2 * i + 1, :, lanes], odd_sems.at[step, i]
        )

    def store_sources(step):
        lanes = pl.ds(step * GROUP * count, GROUP * count)
        return pltpu.make_async_copy(src_ref.at[:, lanes], src_hbm.at[:, lanes], src_sems.at[step])

    def multiply(step, slot):
        first = step * GROUP * CB
        totals[slot] = lax.dot_general(
            turned[first : first + GROUP * CB, :], others[...], (((1,), (1,)), ((), ())), preferred_element_type=f32
        )

    def write(step, slot):
        write_pairs(totals.at[slot], step, own_seg, pseg_ref, odd_ref, range(1, BAND + 1, 2))
        products = jnp.concatenate(
            [totals[slot, g * CB : (g + 1) * CB, 2 * CB :] for g in range(GROUP)], axis=1
        )
        src_ref[:, step * GROUP * count : (step + 1) * GROUP * count] = products.astype(bf16)
        for i in range(BAND // 2):
            store(step, i).start()
        store_sources(step).start()

    for step in range(steps):
        multiply(step, step % 2)
        if step:
            write(step - 1, (step - 1) % 2)
    write(steps - 1, (steps - 1) % 2)
    for step in range(steps):
        for i in range(BAND // 2):
            store(step, i).wait()
        store_sources(step).wait()
    for load in early:
        load.wait()


VMEM = pl.BlockSpec(memory_space=pltpu.VMEM)
SMEM = pl.BlockSpec(memory_space=pltpu.SMEM)
HBM = pl.BlockSpec(memory_space=pltpu.HBM)


def call(kernel, shapes, scratch, specs, **kwargs):
    return pl.pallas_call(
        kernel, out_shape=shapes, in_specs=specs, out_specs=jax.tree.map(lambda _: VMEM, shapes), scratch_shapes=scratch, **kwargs
    )


def per_device(records, filter_taps, segment_ids):
    count = lax.axis_size("fibre")
    device = lax.axis_index("fibre")

    def ahead(value, distance):
        return lax.ppermute(value, "fibre", [(i, (i - distance) % count) for i in range(count)])

    def swap(value):
        return lax.ppermute(value, "fibre", [(i, i ^ 1) for i in range(count)])

    index = device.reshape(1)
    few = count <= 16
    stay = functools.partial(pltpu.with_memory_space_constraint, memory_space=pltpu.HBM)

    edge = call(
        edge_kernel,
        jax.ShapeDtypeStruct((2 * HALO, W * L), bf16),
        [pltpu.SemaphoreType.DMA((2,))],
        [HBM],
        compiler_params=pltpu.CompilerParams(vmem_limit_bytes=EDGE_LIMIT),
    )(stay(records))
    route = [(i, (i + 1) % count if i % 2 else (i - BAND - 1) % count) for i in range(count)]
    halo = lax.ppermute(edge, "fibre", route)
    sown = swap(records)
    four = ahead(records, 4)
    two = ahead(records, 2)

    dft, lags = dft_tables(), lag_tables()
    source, band, segs, own, dft, lags = call(
        prep_kernel,
        (
            jax.ShapeDtypeStruct((SLOT, CHUNK), bf16),
            jax.ShapeDtypeStruct((SPAN * CHUNK, 2 * CHUNK), bf16),
            jax.ShapeDtypeStruct((ROWS + 2 * HALO, CHUNK), f32),
            jax.ShapeDtypeStruct(records.shape, bf16),
            jax.ShapeDtypeStruct(dft.shape, bf16),
            jax.ShapeDtypeStruct(lags.shape, f32),
        ),
        [
            pltpu.VMEM(filter_taps.shape, bf16),
            pltpu.VMEM((1,) + segment_ids.shape, jnp.int32),
            pltpu.VMEM((SLOT, SPAN * CHUNK), f32),
            pltpu.SemaphoreType.DMA((5,)),
        ],
        [SMEM] + [VMEM] * 3 + [HBM] * 5,
        compiler_params=pltpu.CompilerParams(vmem_limit_bytes=PREP_LIMIT if few else None),
    )(
        index, edge, halo, sown, stay(filter_taps), stay(segment_ids.reshape(1, -1)), stay(records), stay(dft),
        stay(lags),
    )

    doubled = count & (count - 1) == 0
    if doubled:
        rows, bit = source, 1
        while bit < count:
            other = lax.ppermute(rows, "fibre", [(i, i ^ bit) for i in range(count)])
            halves = (rows, other)
            if 2 * bit < count:
                rows = jnp.concatenate(halves, axis=0)
            bit *= 2
    else:
        halves = jnp.split(lax.all_gather(source, "fibre", axis=0, tiled=True), 2, axis=0)
    pseg = call(
        functools.partial(partner_kernel, count), jax.ShapeDtypeStruct((8, CHUNK), f32), (), [SMEM, VMEM],
        compiler_params=pltpu.CompilerParams(vmem_limit_bytes=TABLE_LIMIT),
    )(index, segs)
    sfour, stwo = swap(four), swap(two)

    limit = pltpu.CompilerParams(vmem_limit_bytes=MAIN_LIMIT if few else None)
    spec, give = call(
        spectra_kernel,
        (
            jax.ShapeDtypeStruct((NEAR * CB, KP), bf16),
            jax.ShapeDtypeStruct((2 * CB, KP), bf16),
        ),
        [
            pltpu.VMEM((NCHUNK, ROWS + 2 * HALO, CHUNK), f32),
            pltpu.VMEM((2, NCHUNK * CB, SPAN * CHUNK), bf16),
            pltpu.VMEM((NCHUNK, NEAR * CB, CHUNK), bf16),
        ],
        [SMEM] + [VMEM] * 10,
        compiler_params=limit,
    )(index, own, two, four, sown, stwo, sfour, halo, segs, band, dft)
    take = swap(give)
    even_blocks, turned = call(
        turn_kernel,
        (
            jax.ShapeDtypeStruct((NEAR, CB, LAGS * CB), bf16),
            jax.ShapeDtypeStruct((LAGS * CB, KP), bf16),
        ),
        [
            pltpu.VMEM((2, GROUP * CB, NEAR * CB), f32),
            pltpu.VMEM((CB, KP), f32),
        ],
        [VMEM] * 4,
        compiler_params=limit,
    )(segs, pseg, spec, lags)
    stacked, source_out = pl.pallas_call(
        functools.partial(rest_kernel, doubled),
        out_shape=(
            jax.ShapeDtypeStruct((BAND + 1, CB, LAGS * CB), bf16),
            jax.ShapeDtypeStruct((CB, LAGS * count), bf16),
        ),
        in_specs=[SMEM] + [VMEM] * 8,
        out_specs=(HBM, HBM),
        scratch_shapes=[
            pltpu.VMEM((BAND // 2, CB, LAGS * CB), bf16),
            pltpu.VMEM((CB, LAGS * count), bf16),
            pltpu.VMEM((2, GROUP * CB, 2 * CB + count), f32),
            pltpu.VMEM((2 * CB + count, KP), bf16),
            pltpu.VMEM((NCHUNK, count, CHUNK), bf16),
            pltpu.VMEM((count, KP), bf16),
            pltpu.SemaphoreType.DMA((NEAR,)),
            pltpu.SemaphoreType.DMA((LAGS // GROUP, BAND // 2)),
            pltpu.SemaphoreType.DMA((LAGS // GROUP,)),
        ],
        compiler_params=limit,
    )(index, segs, pseg, turned, take, dft, *halves, even_blocks)
    return (jnp.swapaxes(stacked, 0, 1), source_out)


def solution(mesh):
    return jax.shard_map(
        per_device,
        mesh=mesh,
        in_specs=(P(("runs", "fibre"), None), P(), P("runs")),
        out_specs=(P(("runs", "fibre"), None, None), P(("runs", "fibre"), None)),
        check_vma=False,
    )
```

```python
import functools

import jax
import jax.numpy as jnp
import numpy as np
from jax import lax
from jax.experimental import pallas as pl
from jax.experimental.pallas import tpu as pltpu
from jax.sharding import PartitionSpec as P


CB = 64
W = 4
F = 200
L = 400
TAPS = 63
SPAN = 9
LAGS = 32
BAND = 4
HALF = (SPAN - 1) // 2
SLOT = 16
HALO = 8
CHUNK = 128
NCHUNK = -(-W * L // CHUNK)
KP = -(-W * L // CHUNK) * CHUNK
ROWS = (BAND + 1) * CB
NEAR = BAND // 2 + 1
GROUP = 8
SHIFT = L % CHUNK
COVER = 4 * CHUNK

MAIN_LIMIT = 20 << 20
PREP_LIMIT = 12 << 20
EDGE_LIMIT = 1 << 20
TABLE_LIMIT = 2 << 20

f32 = jnp.float32
bf16 = jnp.bfloat16


def dft_tables():
    t = np.arange(L)
    taper = 0.5 - 0.5 * np.cos((t + 0.5) * (2.0 * np.pi / L))
    phase = (t[:, None] * np.arange(F)[None, :] % L) * (2.0 * np.pi / L)
    table = np.concatenate([taper[:, None] * np.cos(phase), -taper[:, None] * np.sin(phase)], axis=1)
    tables = np.zeros((W, COVER, COVER))
    for w in range(W):
        tables[w, w * SHIFT : w * SHIFT + L, w * SHIFT : w * SHIFT + L] = table
    return jnp.asarray(tables.astype(np.float32), bf16)


def lag_tables():
    m = np.arange(LAGS) - LAGS // 2
    phase = (m[:, None] * np.arange(F)[None, :] % L) * (2.0 * np.pi / L)
    scale = 1.0 / np.sqrt(2.0 * L)
    straight, crossed = np.cos(phase) * scale, -np.sin(phase) * scale
    tables = np.zeros((2, LAGS, KP))
    tables[0, :, : W * L] = np.tile(np.concatenate([straight, straight], axis=1), (1, W))
    tables[1, :, : W * L] = np.tile(np.concatenate([crossed, -crossed], axis=1), (1, W))
    return jnp.asarray(tables.astype(np.float32), bf16).astype(f32)


def start_loads(pairs, sems):
    loads = [pltpu.make_async_copy(source, target, sems.at[i]) for i, (source, target) in enumerate(pairs)]
    for load in loads:
        load.start()
    return loads


def edge_kernel(own_hbm, edge_ref, sems):
    last = (own_hbm.at[pl.ds(CB - HALO, HALO)], edge_ref.at[pl.ds(0, HALO)])
    first = (own_hbm.at[pl.ds(0, HALO)], edge_ref.at[pl.ds(HALO, HALO)])
    for load in start_loads((last, first), sems):
        load.wait()


def chunk(rows, j):
    piece = rows[:, j * CHUNK : min((j + 1) * CHUNK, W * L)]
    if piece.shape[1] < CHUNK:
        piece = jnp.concatenate([piece, jnp.zeros((piece.shape[0], CHUNK - piece.shape[1]), piece.dtype)], axis=1)
    return piece


def filter_rows(row_at, seg_ref, centres, line, band_ref):
    line[...] = jnp.zeros_like(line)
    for i, centre in enumerate(centres):
        own = seg_ref[centre : centre + 1, :]
        for e in range(SPAN):
            at = centre - HALF + e
            keep = jnp.where(seg_ref[at : at + 1, :] == own, 1.0, 0.0)
            for j in range(NCHUNK):
                line[i * SLOT + j : i * SLOT + j + 1, e * CHUNK : (e + 1) * CHUNK] = row_at(i, e, j) * keep
    share = jnp.dot(line[...].astype(bf16), band_ref[...], preferred_element_type=f32)
    results = []
    for i in range(len(centres)):
        part = share[i * SLOT : (i + 1) * SLOT]
        before = jnp.concatenate([jnp.zeros((1, CHUNK), f32), part[:-1, CHUNK:]], axis=0)
        results.append(part[:, :CHUNK] + before)
    return results


def prep_kernel(
    index_ref, edge_ref, halo_ref, sown_ref, taps_hbm, ids_hbm, own_hbm,
    source_ref, band_ref, seg_ref, own_ref, taps_ref, ids_ref, line, sems,
):
    loads = start_loads(((taps_hbm, taps_ref), (ids_hbm, ids_ref), (own_hbm, own_ref)), sems)
    device = index_ref[0]
    total = ids_ref.shape[1]
    loads[0].wait()
    wide = jnp.concatenate([taps_ref[...].astype(f32), jnp.zeros((SPAN, 2 * CHUNK - TAPS), f32)], axis=1)
    for e in range(SPAN):
        row = jnp.broadcast_to(wide[e : e + 1, :], (CHUNK, 2 * CHUNK))
        band_ref[e * CHUNK : (e + 1) * CHUNK, :] = pltpu.roll(row, 0, 1, stride=1, stride_axis=0).astype(bf16)

    loads[1].wait()
    ids = jnp.broadcast_to(ids_ref[...].astype(bf16), (CHUNK, total))
    channels = device * CB - HALO + lax.broadcasted_iota(jnp.int32, (ROWS + 2 * HALO, 1), 0)
    channels = jnp.where(channels < 0, channels + total, channels)
    channels = jnp.where(channels >= total, channels - total, channels)
    hit = lax.broadcasted_iota(jnp.int32, (ROWS + 2 * HALO, total), 1) == channels
    seg_ref[...] = lax.dot_general(
        jnp.where(hit, 1.0, 0.0).astype(bf16), ids, (((1,), (1,)), ((), ())), preferred_element_type=f32
    )

    even = device % 2 == 0
    behind = jnp.where(even, halo_ref[:HALO].astype(f32), sown_ref[CB - HALO :].astype(f32))
    first = edge_ref[HALO:].astype(f32)

    def row_at(_, e, j):
        rows, at = (behind, HALO - HALF + e) if e < HALF else (first, e - HALF)
        return chunk(rows, j)[at : at + 1]

    source_ref[...] = filter_rows(row_at, seg_ref, (HALO,), line, band_ref)[0].astype(bf16)
    for load in loads[2:]:
        load.wait()


def partner_kernel(count, index_ref, seg_ref, pseg_ref):
    for k in range(BAND + 1):
        block = seg_ref[HALO + k * CB : HALO + (k + 1) * CB, :]
        turned = jnp.transpose(jnp.concatenate([block, block], axis=0))
        pseg_ref[k : k + 1, :] = jnp.where(index_ref[0] + k < count, turned[:1], -1.0)
    pseg_ref[BAND + 1 :, :] = jnp.full((8 - BAND - 1, CHUNK), -1.0, f32)


def whiten(filt, dft_ref, spec):
    tiles = COVER // CHUNK - 1
    tail = None
    for w in range(W):
        lhs = jnp.concatenate([filt[w * tiles + q] for q in range(tiles + 1)], axis=1)
        raw = jnp.dot(lhs, dft_ref[w], preferred_element_type=f32)
        power = jnp.sum(raw * raw, axis=-1, keepdims=True) * (1.0 / L)
        whitened = raw * lax.rsqrt(power + 1e-06)
        head = whitened[:, :CHUNK] if tail is None else tail + whitened[:, :CHUNK]
        spec[:, w * tiles * CHUNK : (w * tiles + 1) * CHUNK] = head.astype(bf16)
        spec[:, (w * tiles + 1) * CHUNK : (w + 1) * tiles * CHUNK] = whitened[:, CHUNK : tiles * CHUNK].astype(bf16)
        tail = whitened[:, tiles * CHUNK :]
    spec[:, W * tiles * CHUNK :] = tail.astype(bf16)


def spectra_kernel(*refs):
    index_ref, own_ref, two_ref, four_ref, sown_ref, stwo_ref, sfour_ref, halo_ref = refs[:8]
    seg_ref, band_ref, dft_hbm, lag_hbm, spec, give_ref, dft_ref, lag_ref, rec, masked, filt, sems = refs[8:]
    loads = start_loads(((dft_hbm, dft_ref), (lag_hbm, lag_ref)), sems)
    even = index_ref[0] % 2 == 0

    def put(start, rows):
        for j in range(NCHUNK):
            rec[j, start : start + rows.shape[0], :] = chunk(rows, j)

    stwo, sfour = stwo_ref[...].astype(f32), sfour_ref[...].astype(f32)
    sown, halo = sown_ref[...].astype(f32), halo_ref[...].astype(f32)
    put(0, jnp.where(even, halo[:HALO], sown[CB - HALO :]))
    put(HALO, own_ref[...].astype(f32))
    put(HALO + CB, jnp.where(even, sown[:HALO], stwo[:HALO]))
    put(2 * CB, jnp.where(even, sown[CB - HALO :], stwo[CB - HALO :]))
    put(HALO + 2 * CB, two_ref[...].astype(f32))
    put(HALO + 3 * CB, jnp.where(even, stwo[:HALO], sfour[:HALO]))
    put(4 * CB, jnp.where(even, stwo[CB - HALO :], sfour[CB - HALO :]))
    put(HALO + 4 * CB, four_ref[...].astype(f32))
    put(HALO + ROWS, jnp.where(even, sfour[:HALO], halo[HALO:]))

    for i in range(NEAR):
        base = 2 * i * CB
        held = masked.at[i % 2]
        centre = seg_ref[base + HALO : base + HALO + CB, :]
        for e in range(SPAN):
            first = base + HALO - HALF + e
            keep = jnp.where(seg_ref[first : first + CB, :] == centre, 1.0, 0.0)
            for j in range(NCHUNK):
                held[j * CB : (j + 1) * CB, e * CHUNK : (e + 1) * CHUNK] = (
                    rec[j, first : first + CB, :] * keep
                ).astype(bf16)
        share = jnp.dot(held[...], band_ref[...], preferred_element_type=f32)
        for j in range(NCHUNK):
            result = share[j * CB : (j + 1) * CB, :CHUNK]
            if j:
                result = result + share[(j - 1) * CB : j * CB, CHUNK:]
            filt[j, i * CB : (i + 1) * CB, :] = result.astype(bf16)

    for load in loads:
        load.wait()

    @pl.when(index_ref[0] >= 0)
    def _():
        whiten(filt, dft_ref, spec)

    give_ref[...] = jnp.where(even, spec[CB:, :].astype(f32), spec[: 2 * CB, :].astype(f32)).astype(bf16)


def turn_kernel(seg_ref, pseg_ref, spec, lag_ref, out_ref, turned, totals, swapped):
    own = spec[:CB, :].astype(f32)
    pieces = []
    for w in range(W):
        pieces += [own[:, w * L + F : (w + 1) * L], own[:, w * L : w * L + F]]
    swapped[...] = jnp.concatenate(pieces + [jnp.zeros((CB, KP - W * L), f32)], axis=1)
    own_seg = seg_ref[HALO : HALO + CB, :]

    def multiply(step, slot):
        start, first = step * GROUP, step * GROUP * CB
        for at in range(0, KP, CHUNK):
            lanes = slice(at, at + CHUNK)
            straight, crossed = lag_ref[0, start : start + GROUP, lanes], lag_ref[1, start : start + GROUP, lanes]
            own, other = spec[:CB, lanes].astype(f32), swapped[:, lanes]
            for g in range(GROUP):
                turned[first + g * CB : first + (g + 1) * CB, lanes] = (
                    own * straight[g : g + 1, :] + other * crossed[g : g + 1, :]
                ).astype(bf16)
        totals[slot] = lax.dot_general(
            turned[first : first + GROUP * CB, :], spec[...], (((1,), (1,)), ((), ())), preferred_element_type=f32
        )

    def write(step, slot):
        write_pairs(totals.at[slot], step, own_seg, pseg_ref, out_ref, range(0, BAND + 1, 2))

    for step in range(LAGS // GROUP):
        multiply(step, step % 2)
        if step:
            write(step - 1, (step - 1) % 2)
    write(LAGS // GROUP - 1, (LAGS // GROUP - 1) % 2)


def write_pairs(total, step, own_seg, pseg_ref, out_ref, blocks):
    for pair in range(GROUP // 2):
        low, high = 2 * pair * CB, (2 * pair + 1) * CB
        at = step * GROUP * CB + pair * 2 * CB
        lanes = slice(at, at + 2 * CB)
        for i, k in enumerate(blocks):
            both = jnp.concatenate([total[row : row + CB, i * CB : (i + 1) * CB] for row in (low, high)], axis=1)
            keep = own_seg == pseg_ref[k : k + 1, :]
            out_ref[i, :, lanes] = jnp.where(keep, both, 0.0).astype(bf16)


def rest_kernel(
    doubled, index_ref, seg_ref, pseg_ref, turned, take, dft_ref, low_ref, high_ref, even_ref, out_hbm, src_hbm,
    odd_ref, src_ref, totals, others, filt, found, even_sems, odd_sems, src_sems,
):
    early = start_loads(
        tuple((even_ref.at[i], out_hbm.at[k]) for i, k in enumerate(range(0, BAND + 1, 2))), even_sems
    )
    count = filt.shape[1]
    for q in range(count):
        ref, at = (low_ref, q * SLOT) if 2 * q < count else (high_ref, q * SLOT - low_ref.shape[0])
        rows = ref[at : at + SLOT, :].astype(f32)
        for j in range(NCHUNK):
            filt[j, q : q + 1, :] = rows[j : j + 1].astype(bf16)
    whiten(filt, dft_ref, found)
    row = lax.broadcasted_iota(jnp.int32, (count, count), 0)
    column = lax.broadcasted_iota(jnp.int32, (count, count), 1)
    if doubled:
        row = jnp.bitwise_xor(row, index_ref[0])
    order = jnp.where(row == column, 1.0, 0.0).astype(bf16)
    others[2 * CB :, :] = jnp.dot(order, found[...], preferred_element_type=f32).astype(bf16)
    others[: 2 * CB, :] = take[...]
    own_seg = seg_ref[HALO : HALO + CB, :]
    steps = LAGS // GROUP

    def store(step, i):
        lanes = pl.ds(step * GROUP * CB, GROUP * CB)
        return pltpu.make_async_copy(
            odd_ref.at[i, :, lanes], out_hbm.at[2 * i + 1, :, lanes], odd_sems.at[step, i]
        )

    def store_sources(step):
        lanes = pl.ds(step * GROUP * count, GROUP * count)
        return pltpu.make_async_copy(src_ref.at[:, lanes], src_hbm.at[:, lanes], src_sems.at[step])

    def multiply(step, slot):
        first = step * GROUP * CB
        totals[slot] = lax.dot_general(
            turned[first : first + GROUP * CB, :], others[...], (((1,), (1,)), ((), ())), preferred_element_type=f32
        )

    def write(step, slot):
        write_pairs(totals.at[slot], step, own_seg, pseg_ref, odd_ref, range(1, BAND + 1, 2))
        products = jnp.concatenate(
            [totals[slot, g * CB : (g + 1) * CB, 2 * CB :] for g in range(GROUP)], axis=1
        )
        src_ref[:, step * GROUP * count : (step + 1) * GROUP * count] = products.astype(bf16)
        for i in range(BAND // 2):
            store(step, i).start()
        store_sources(step).start()

    for step in range(steps):
        multiply(step, step % 2)
        if step:
            write(step - 1, (step - 1) % 2)
    write(steps - 1, (steps - 1) % 2)
    for step in range(steps):
        for i in range(BAND // 2):
            store(step, i).wait()
        store_sources(step).wait()
    for load in early:
        load.wait()


VMEM = pl.BlockSpec(memory_space=pltpu.VMEM)
SMEM = pl.BlockSpec(memory_space=pltpu.SMEM)
HBM = pl.BlockSpec(memory_space=pltpu.HBM)


def call(kernel, shapes, scratch, specs, **kwargs):
    return pl.pallas_call(
        kernel, out_shape=shapes, in_specs=specs, out_specs=jax.tree.map(lambda _: VMEM, shapes), scratch_shapes=scratch, **kwargs
    )


def per_device(records, filter_taps, segment_ids):
    count = lax.axis_size("fibre")
    device = lax.axis_index("fibre")

    def ahead(value, distance):
        return lax.ppermute(value, "fibre", [(i, (i - distance) % count) for i in range(count)])

    def swap(value):
        return lax.ppermute(value, "fibre", [(i, i ^ 1) for i in range(count)])

    index = device.reshape(1)
    few = count <= 16
    stay = functools.partial(pltpu.with_memory_space_constraint, memory_space=pltpu.HBM)

    edge = call(
        edge_kernel,
        jax.ShapeDtypeStruct((2 * HALO, W * L), bf16),
        [pltpu.SemaphoreType.DMA((2,))],
        [HBM],
        compiler_params=pltpu.CompilerParams(vmem_limit_bytes=EDGE_LIMIT),
    )(stay(records))
    route = [(i, (i + 1) % count if i % 2 else (i - BAND - 1) % count) for i in range(count)]
    halo = lax.ppermute(edge, "fibre", route)
    sown = swap(records)
    four = ahead(records, 4)
    two = ahead(records, 2)

    dft, lags = dft_tables(), lag_tables()
    source, band, segs, own = call(
        prep_kernel,
        (
            jax.ShapeDtypeStruct((SLOT, CHUNK), bf16),
            jax.ShapeDtypeStruct((SPAN * CHUNK, 2 * CHUNK), bf16),
            jax.ShapeDtypeStruct((ROWS + 2 * HALO, CHUNK), f32),
            jax.ShapeDtypeStruct(records.shape, bf16),
        ),
        [
            pltpu.VMEM(filter_taps.shape, bf16),
            pltpu.VMEM((1,) + segment_ids.shape, jnp.int32),
            pltpu.VMEM((SLOT, SPAN * CHUNK), f32),
            pltpu.SemaphoreType.DMA((3,)),
        ],
        [SMEM] + [VMEM] * 3 + [HBM] * 3,
        compiler_params=pltpu.CompilerParams(vmem_limit_bytes=PREP_LIMIT if few else None),
    )(
        index, edge, halo, sown, stay(filter_taps), stay(segment_ids.reshape(1, -1)), stay(records),
    )

    doubled = count & (count - 1) == 0
    if doubled:
        rows, bit = source, 1
        while bit < count:
            other = lax.ppermute(rows, "fibre", [(i, i ^ bit) for i in range(count)])
            halves = (rows, other)
            if 2 * bit < count:
                rows = jnp.concatenate(halves, axis=0)
            bit *= 2
    else:
        halves = jnp.split(lax.all_gather(source, "fibre", axis=0, tiled=True), 2, axis=0)
    pseg = call(
        functools.partial(partner_kernel, count), jax.ShapeDtypeStruct((8, CHUNK), f32), (), [SMEM, VMEM],
        compiler_params=pltpu.CompilerParams(vmem_limit_bytes=TABLE_LIMIT),
    )(index, segs)
    sfour, stwo = swap(four), swap(two)

    limit = pltpu.CompilerParams(vmem_limit_bytes=MAIN_LIMIT if few else None)
    spec, give, dft, lags = call(
        spectra_kernel,
        (
            jax.ShapeDtypeStruct((NEAR * CB, KP), bf16),
            jax.ShapeDtypeStruct((2 * CB, KP), bf16),
            jax.ShapeDtypeStruct(dft.shape, dft.dtype),
            jax.ShapeDtypeStruct(lags.shape, lags.dtype),
        ),
        [
            pltpu.VMEM((NCHUNK, ROWS + 2 * HALO, CHUNK), f32),
            pltpu.VMEM((2, NCHUNK * CB, SPAN * CHUNK), bf16),
            pltpu.VMEM((NCHUNK, NEAR * CB, CHUNK), bf16),
            pltpu.SemaphoreType.DMA((2,)),
        ],
        [SMEM] + [VMEM] * 9 + [HBM] * 2,
        compiler_params=limit,
    )(index, own, two, four, sown, stwo, sfour, halo, segs, band, stay(dft), stay(lags))
    take = swap(give)
    even_blocks, turned = call(
        turn_kernel,
        (
            jax.ShapeDtypeStruct((NEAR, CB, LAGS * CB), bf16),
            jax.ShapeDtypeStruct((LAGS * CB, KP), bf16),
        ),
        [
            pltpu.VMEM((2, GROUP * CB, NEAR * CB), f32),
            pltpu.VMEM((CB, KP), f32),
        ],
        [VMEM] * 4,
        compiler_params=limit,
    )(segs, pseg, spec, lags)
    stacked, source_out = pl.pallas_call(
        functools.partial(rest_kernel, doubled),
        out_shape=(
            jax.ShapeDtypeStruct((BAND + 1, CB, LAGS * CB), bf16),
            jax.ShapeDtypeStruct((CB, LAGS * count), bf16),
        ),
        in_specs=[SMEM] + [VMEM] * 8,
        out_specs=(HBM, HBM),
        scratch_shapes=[
            pltpu.VMEM((BAND // 2, CB, LAGS * CB), bf16),
            pltpu.VMEM((CB, LAGS * count), bf16),
            pltpu.VMEM((2, GROUP * CB, 2 * CB + count), f32),
            pltpu.VMEM((2 * CB + count, KP), bf16),
            pltpu.VMEM((NCHUNK, count, CHUNK), bf16),
            pltpu.VMEM((count, KP), bf16),
            pltpu.SemaphoreType.DMA((NEAR,)),
            pltpu.SemaphoreType.DMA((LAGS // GROUP, BAND // 2)),
            pltpu.SemaphoreType.DMA((LAGS // GROUP,)),
        ],
        compiler_params=limit,
    )(index, segs, pseg, turned, take, dft, *halves, even_blocks)
    return (jnp.swapaxes(stacked, 0, 1), source_out)


def solution(mesh):
    return jax.shard_map(
        per_device,
        mesh=mesh,
        in_specs=(P(("runs", "fibre"), None), P(), P("runs")),
        out_specs=(P(("runs", "fibre"), None, None), P(("runs", "fibre"), None)),
        check_vma=False,
    )
```
